512 devices in a mesh: seq: 8 (over y_lo, x), fsdp: 64 (over z, y_hi, core).
Axes of the slice: x: 4, y: 8 (y_hi: 4, y_lo: 2; y = y_hi * 2 + y_lo), z: 8, core: 2. Of those that a mesh axis runs over, the one named last changes fastest.
Arguments:
- hidden: bfloat16 [2048, 8192], P('seq', 'fsdp'), may hold values from -28 to 28
- q_weight: bfloat16 [8192, 8192], P('fsdp'), may hold values from -0.0625 to 0.0625
- kv_weight: bfloat16 [2048, 8192], P(None, 'fsdp'), may hold values from -0.0625 to 0.0625
- d_attended: bfloat16 [2048, 8192], P('seq', 'fsdp'), may hold values from -6 to 6
- doc_lengths: int32 [4], replicated, may hold values from 1 to 1536, as said below
- prompt_pos: int32 [128], replicated, may hold values from 0 to 2047, as said below
Outputs:
- attended: bfloat16 [2048, 8192], P('seq', 'fsdp')
- prompt_grad: float32 [128, 8192], P('seq', 'fsdp')
The draws below stay inside these ranges and needn't reach their ends.
Inputs may be any that keep to these rules, and one draw needn't show every extreme that they name: `doc_lengths`: 4 document lengths in pack order that sum to 2048; exactly one is 1536, at a position that varies from draw to draw, and the others are at least 1. `prompt_pos`: for every block i of 256 rows, entries i * 16 to (i + 1) * 16 - 1 are distinct rows of that block in rising order; row 0 and row 2047 are always among them.
All inputs are finite; a program needn't handle non-finite values.
Results may differ from the reference program's by a relative error of at most 0.017.
The reference program's roundings to bfloat16 on the way count: a program that leaves them out, or rounds other values in their place, can miss the bound.
Values may be sent and summed in bfloat16 or wider, within the bound.
A program may use at most 64 MiB of HBM per device.

```python
import math
import jax
import jax.numpy as jnp
from jax import lax

D = 8192
HEAD_DIM = 128
GROUP = 8
T_DEV = 256
P_DEV = 16
NDOC = 4
HEADS = 64
KV_HEADS = 8
SEQ = 2048
PROMPTS = 128
LONGEST = 1536


def draw_hidden(key, part):
    normal_part = jnp.clip(jax.random.normal(jax.random.fold_in(key, 11), (SEQ, D), jnp.float32), -6.0, 6.0)
    return normal_part.astype(jnp.bfloat16)


def draw_doc_lengths(key, part):
    remainder = SEQ - LONGEST
    cut_points = jnp.sort(jax.random.permutation(jax.random.fold_in(key, 31), remainder - 1)[:2]).astype(jnp.int32) + 1
    others = jnp.stack([cut_points[0], cut_points[1] - cut_points[0], remainder - cut_points[1]]).astype(jnp.int32)
    longest_at = jax.random.randint(jax.random.fold_in(key, 32), (), 0, NDOC, dtype=jnp.int32)
    indices = jnp.arange(NDOC, dtype=jnp.int32)
    other_index = jnp.clip(indices - (indices > longest_at).astype(jnp.int32), 0, 2)
    picked = jnp.take(others, other_index)
    return jnp.where(indices == longest_at, LONGEST, picked).astype(jnp.int32)


def draw_prompt_pos(key, part):
    block_total = SEQ // T_DEV
    block_keys = jax.random.split(jax.random.fold_in(key, 21), block_total)

    def choose(block_key):
        return jnp.sort(jax.random.permutation(block_key, T_DEV)[:P_DEV])
    picked = jax.vmap(choose)(block_keys).astype(jnp.int32)
    picked = picked.at[0, 0].set(0)
    picked = picked.at[block_total - 1, P_DEV - 1].set(T_DEV - 1)
    offsets = (jnp.arange(block_total, dtype=jnp.int32) * T_DEV)[:, None]
    return (picked + offsets).reshape(-1)


def block_levels(own_key, dims, cuts, least, high):
    loudness = 1.0
    for axis_at, blocks in cuts:
        steps = jax.random.uniform(jax.random.fold_in(jax.random.fold_in(own_key, 6), axis_at), (blocks,), jnp.float32, least / len(cuts), high / len(cuts))
        loudness = loudness * jnp.repeat(jnp.exp(steps), dims[axis_at] // blocks).reshape((-1,) + (1,) * (len(dims) - 1 - axis_at))
    return loudness


def noise(key, shape, scale, reach, pieces=(), kind=jnp.bfloat16):
    level = block_levels(key, shape, pieces, -0.22, 0.18) if pieces else 1.0
    values = jax.random.normal(key, shape, jnp.float32) * scale * level
    return jnp.minimum(jnp.maximum(values, -reach), reach).astype(kind)


def setup_inputs(seed: int = 0) -> dict:
    streams_of = jax.random.split(jax.random.key(seed), 7)
    hidden = draw_hidden(jax.random.fold_in(streams_of[6], 71), 0)
    q_weight = noise(streams_of[1], (HEADS * HEAD_DIM, D), D ** -0.5, 0.0625, ((0, 64),))
    kv_weight = noise(streams_of[2], (2 * KV_HEADS * HEAD_DIM, D), D ** -0.5, 0.0625, ((1, 64),))
    d_attended = noise(streams_of[3], (SEQ, HEADS * HEAD_DIM), 1.0, 6.0, ((0, 8), (1, 64)))
    doc_lengths = draw_doc_lengths(jax.random.fold_in(streams_of[6], 71), 0)
    prompt_pos = draw_prompt_pos(jax.random.fold_in(streams_of[6], 71), 0)
    return {"hidden": hidden, "q_weight": q_weight, "kv_weight": kv_weight, "d_attended": d_attended, "doc_lengths": doc_lengths, "prompt_pos": prompt_pos}


rope_theta = 1000000.0

def locate(tokens, doc_lengths):
    doc_ends = jnp.cumsum(doc_lengths).astype(jnp.int32)
    segment = lax.optimization_barrier(jnp.sum((tokens[:, None] >= doc_ends[None, :]).astype(jnp.int32), axis=1)).astype(jnp.int32)
    doc_starts = doc_ends - doc_lengths
    picked = segment[:, None] == jnp.arange(doc_lengths.shape[0], dtype=jnp.int32)[None, :]
    opening = lax.optimization_barrier(jnp.sum(jnp.where(picked, doc_starts[None, :], 0), axis=1)).astype(jnp.int32)
    return (segment, tokens - opening)

def rotate(vectors, positions, factor):
    halfway = vectors.shape[-1] // 2
    steps_up = jnp.arange(halfway, dtype=jnp.float32)
    frequency = jnp.exp(steps_up * (-2.0 * math.log(rope_theta) / vectors.shape[-1]))
    angles = positions.astype(jnp.float32)[:, None] * frequency[None, :]
    cosine = jnp.cos(angles)
    sine_part = jnp.sin(angles)
    leading = vectors[..., :halfway]
    trailing = vectors[..., halfway:]
    return jnp.concatenate([leading * cosine - factor * trailing * sine_part, trailing * cosine + factor * leading * sine_part], axis=-1)

def reference(hidden, q_weight, kv_weight, d_attended, doc_lengths, prompt_pos):
    score_scale = 1.0 / math.sqrt(HEAD_DIM)
    all_tokens = jnp.arange(SEQ, dtype=jnp.int32)
    segment_all, place_all = locate(all_tokens, doc_lengths)
    q_pre = jnp.dot(hidden, q_weight.T, preferred_element_type=jnp.float32)
    query_all = rotate(q_pre.reshape(SEQ, HEADS, HEAD_DIM).transpose(1, 0, 2), place_all, 1.0).astype(jnp.bfloat16)
    kv_rounded = jnp.dot(hidden, kv_weight.T, preferred_element_type=jnp.float32).astype(jnp.bfloat16)
    kv_heads = kv_rounded.reshape(SEQ, KV_HEADS, 2, HEAD_DIM).transpose(2, 1, 0, 3)
    key_all = rotate(kv_heads[0].astype(jnp.float32), place_all, 1.0).astype(jnp.bfloat16)
    value_all = kv_heads[1]
    upstream_all = d_attended.reshape(SEQ, HEADS, HEAD_DIM).transpose(1, 0, 2)
    allowed = (segment_all[:, None] == segment_all[None, :]) & (all_tokens[None, :] <= all_tokens[:, None])
    prompt_place = jnp.take(place_all, prompt_pos)

    def one_head(inputs):
        head_query, upstream, head_index = inputs
        kv_index = head_index // GROUP
        head_keys = lax.dynamic_index_in_dim(key_all, kv_index, 0, keepdims=False)
        values = lax.dynamic_index_in_dim(value_all, kv_index, 0, keepdims=False)
        raw_scores = jnp.dot(head_query, head_keys.T, preferred_element_type=jnp.float32) * score_scale
        scores = jnp.where(allowed, raw_scores, -jnp.inf)
        exponent_terms = jnp.exp(scores - lax.optimization_barrier(jnp.max(scores, axis=1, keepdims=True)))
        attention_probs = (exponent_terms / lax.optimization_barrier(jnp.sum(exponent_terms, axis=1, keepdims=True))).astype(jnp.bfloat16)
        attended = jnp.dot(attention_probs, values, preferred_element_type=jnp.float32).astype(jnp.bfloat16)
        rowdot = lax.optimization_barrier(jnp.sum(upstream.astype(jnp.float32) * attended.astype(jnp.float32), axis=1))
        row_dprobs = jnp.dot(jnp.take(upstream, prompt_pos, axis=0), values.T, preferred_element_type=jnp.float32)
        row_probs = jnp.take(attention_probs, prompt_pos, axis=0).astype(jnp.float32)
        row_dscores = (row_probs * (row_dprobs - jnp.take(rowdot, prompt_pos)[:, None])).astype(jnp.bfloat16)
        col_probs = jnp.take(attention_probs, prompt_pos, axis=1)
        col_dprobs = jnp.dot(upstream, jnp.take(values, prompt_pos, axis=0).T, preferred_element_type=jnp.float32)
        col_dscores = (col_probs.astype(jnp.float32) * (col_dprobs - rowdot[:, None])).astype(jnp.bfloat16)
        query_grad = jnp.dot(row_dscores, head_keys, preferred_element_type=jnp.float32) * score_scale
        query_grad = rotate(query_grad, prompt_place, -1.0).astype(jnp.bfloat16)
        key_grad = jnp.dot(col_dscores.T, head_query, preferred_element_type=jnp.float32) * score_scale
        key_grad = rotate(key_grad, prompt_place, -1.0)
        value_grad = jnp.dot(col_probs.T, upstream, preferred_element_type=jnp.float32)
        return (attended, query_grad, key_grad, value_grad)
    head_ids = jnp.arange(HEADS, dtype=jnp.int32)
    attended, query_grad, key_grad, value_grad = lax.map(one_head, (query_all, upstream_all, head_ids))
    attended_out = attended.transpose(1, 0, 2).reshape(SEQ, HEADS * HEAD_DIM)
    dq_rows = query_grad.transpose(1, 0, 2).reshape(PROMPTS, HEADS * HEAD_DIM)
    key_total = lax.optimization_barrier(jnp.sum(key_grad.reshape(KV_HEADS, GROUP, PROMPTS, HEAD_DIM), axis=1))
    value_total = lax.optimization_barrier(jnp.sum(value_grad.reshape(KV_HEADS, GROUP, PROMPTS, HEAD_DIM), axis=1))
    dkv_rows = jnp.stack([key_total, value_total], axis=1).transpose(2, 0, 1, 3)
    dkv_rows = dkv_rows.reshape(PROMPTS, 2 * KV_HEADS * HEAD_DIM).astype(jnp.bfloat16)
    prompt_grad = jnp.dot(dq_rows, q_weight, preferred_element_type=jnp.float32) + jnp.dot(dkv_rows, kv_weight, preferred_element_type=jnp.float32)
    return (attended_out, prompt_grad)
```

```python
import functools
import math

import jax
import jax.numpy as jnp
from jax import lax
from jax.experimental import pallas as pl
from jax.experimental.pallas import tpu as pltpu
from jax.sharding import PartitionSpec as P

ROPE_THETA = 1000000.0
MESH = pl.DeviceIdType.MESH
F32 = jnp.float32
BF16 = jnp.bfloat16
VMEM = pltpu.VMEM
DMA = pltpu.SemaphoreType.DMA

X, YL, YH, Z, C = 4, 2, 4, 8, 2
ROWS, HD, FB = 256, 128, 128


def nt(a, b):
    return lax.dot_general(a, b, (((1,), (1,)), ((), ())), preferred_element_type=F32)


class Place:
    def __init__(self):
        self.s = lax.axis_index("seq")
        self.f = lax.axis_index("fsdp")
        self.x = self.s % X
        self.yl = self.s // X
        self.z = self.f // (YH * C)
        self.yh = (self.f // C) % YH
        self.c = self.f % C
        self.o = 1 - self.c

    def fid(self, z, yh, c):
        return (z * YH + yh) * C + c


class Wires:
    def __init__(self):
        self.open = []

    def make(self, src, dst, ss, rs, seq, fs):
        return pltpu.make_async_remote_copy(
            src_ref=src, dst_ref=dst, send_sem=ss, recv_sem=rs,
            device_id={"seq": seq, "fsdp": fs}, device_id_type=MESH)

    def send(self, *args):
        copy = self.make(*args)
        copy.start()
        self.open.append(copy)

    def finish(self):
        for copy in self.open:
            copy.wait_send()


def nn(a, b):
    return lax.dot_general(a, b, (((1,), (0,)), ((), ())), preferred_element_type=F32)


def tn(a, b):
    return lax.dot_general(a, b, (((0,), (0,)), ((), ())), preferred_element_type=F32)


def lanes(k, n=128):
    return pl.ds(pl.multiple_of(k * n, n), n)


STEP = -2.0 * math.log(ROPE_THETA) / HD
SCALE = 1.0 / math.sqrt(HD)
SEQ, NP, PL = 2048, 128, 16


def openings(tokens, doc):
    end = jnp.int32(0)
    start = jnp.zeros_like(tokens)
    for i in range(4):
        end = end + doc[i]
        start = start + jnp.where(tokens >= end, doc[i], 0)
    return start


def whole(hid, qw, kvw, kvflat, dat, doc, prow, att_out, pg_out,
          H, W2, KW, PS, PR, SS, SR, KB, QP, QR, KVT, COS, SIN, QB, PB, CM, KVL,
          QG, GP, GR, G1, GX, G2, GY, DK, DKV, QF, QY, QS, QZ,
          s_h, r_h, r_h2, s_hz, s_w, r_w, l_w, s_k, r_k, l_k, s_p, r_p, s_s, r_s,
          s_b, r_b, s_x, r_x, s_c, r_c, s_q, r_q, l_v,
          s_g, r_g, s_d1, r_d1, s_d2, r_d2, s_d3, r_d3, s_d4, r_d4, s_e2, r_e2, s_e3, r_e3):
    d = Place()
    s, f, x, yl, z, yh, c, o = d.s, d.f, d.x, d.yl, d.z, d.yh, d.c, d.o
    mate = d.fid(z, yh, o)
    zup, zdn = (z + 1) % Z, (z + Z - 1) % Z
    w = Wires()

    bar = pltpu.get_barrier_semaphore()
    peers = [(s, mate)]
    ypeers = []
    for e in range(1, YH * YL):
        y = (yh * YL + yl + e) % (YH * YL)
        ypeers.append((y // YL, y % YL))
        peers.append(((y % YL) * X + x, d.fid(z, y // YL, c)))
    xpeers = [(x + e) % X for e in range(1, X)]
    for xx in xpeers:
        peers.append((yl * X + xx, f))
    zpeers = [(z + e) % Z for e in range(1, Z)]
    for zz in zpeers:
        peers.append((s, d.fid(zz, yh, c)))
        peers.append((s, d.fid(zz, yh, o)))
    for ps, pf in peers:
        pl.semaphore_signal(bar, inc=1, device_id={"seq": ps, "fsdp": pf}, device_id_type=MESH)
    pl.semaphore_wait(bar, len(peers))

    def hblock(zz, yy):
        return H.at[:, lanes(zz * YH + yy)]

    def wslice(yy):
        return kvw.at[:, yy // 2, :, yy % 2]

    def recv(ref, sem):
        w.make(ref, ref, s_q, sem, s, mate).wait_recv()

    for e in range(1, YH):
        yy = (yh + e) % YH
        w.send(hid, hblock(z, yh), s_h.at[e - 1], r_h.at[z * YH + yh], s, d.fid(z, yy, c))
    for i, zz in enumerate((zup, zdn)):
        w.send(hid, hblock(z, yh), s_hz.at[i, 0, 0], r_h.at[z * YH + yh], s, d.fid(zz, yh, c))
    for e in range(1, YH):
        yy = (yh + e) % YH
        w.send(wslice(yy), KW.at[:, :, :, lanes(yh)], s_k.at[e - 1], r_k.at[yh], s, d.fid(z, yy, c))
    kown = pltpu.make_async_copy(wslice(yh), KW.at[:, :, :, lanes(yh)], l_k)
    kown.start()

    def wload(k, _):
        pltpu.make_async_copy(qw.at[:, pl.ds(pl.multiple_of(k * 256 + c * 128, 128), 128)],
                              W2.at[pl.ds(c * 128, 128), lanes(k)], l_w).start()
        w.make(qw.at[:, pl.ds(pl.multiple_of(k * 256 + o * 128, 128), 128)],
               W2.at[pl.ds(c * 128, 128), lanes(k)], s_w, r_w, s, mate).start()
        return 0
    lax.fori_loop(0, Z * YH, wload, 0)
    kvload = pltpu.make_async_copy(kvflat, KVL, l_v)
    kvload.start()
    H[:, lanes(z * YH + yh)] = hid[...]

    tok = s * ROWS + lax.broadcasted_iota(jnp.int32, (1, ROWS), 1)
    place = (tok - openings(tok, doc)).astype(F32)
    freq = jnp.exp(lax.broadcasted_iota(jnp.int32, (HD // 2, 1), 0).astype(F32) * STEP)
    angle = freq * place
    COS[...] = jnp.cos(angle)
    SIN[...] = jnp.sin(angle)
    prompts = prow[...]
    for i in range(8):
        at = i * 256 + lax.broadcasted_iota(jnp.int32, (256, NP), 0)
        CM[pl.ds(i * 256, 256), :] = jnp.where(at == prompts, 1.0, 0.0).astype(BF16)
    near = lax.broadcasted_iota(jnp.int32, (PL, NP), 1) == (
        s * PL + lax.broadcasted_iota(jnp.int32, (PL, NP), 0))
    own_p = jnp.sum(jnp.where(near, prompts.astype(F32), 0.0), axis=1, keepdims=True).astype(jnp.int32)
    pick = jnp.where(lax.broadcasted_iota(jnp.int32, (PL, ROWS), 1) == own_p - s * ROWS,
                     1.0, 0.0).astype(BF16)
    lane = lax.broadcasted_iota(jnp.int32, (1, HD), 1)
    freq_l = jnp.exp(jnp.where(lane < 64, lane, lane - 64).astype(F32) * STEP)
    angle_p = (own_p - openings(own_p, doc)).astype(F32) * freq_l
    cos_p = jnp.cos(angle_p)
    sin_p = jnp.where(lane < 64, 1.0, -1.0) * jnp.sin(angle_p)

    def back(u):
        return u * cos_p + pltpu.roll(u, 64, 1) * sin_p

    half = ROWS // 2

    def forward(step):
        up, dn = (z + Z - step) % Z, (z + step) % Z
        for e in range(YH):
            yy = (yh + e) % YH
            if step == 0:
                if e == 0:
                    continue
                recv(hblock(z, yy), r_h.at[z * YH + yy])
                w.send(hblock(z, yy), hblock(z, yy), s_hz.at[0, step, e], r_h.at[z * YH + yy], s, d.fid(zup, yh, c))
                w.send(hblock(z, yy), hblock(z, yy), s_hz.at[1, step, e], r_h.at[z * YH + yy], s, d.fid(zdn, yh, c))
            elif step < 3:
                recv(hblock(up, yy), r_h.at[up * YH + yy])
                w.send(hblock(up, yy), hblock(up, yy), s_hz.at[0, step, e], r_h.at[up * YH + yy], s, d.fid(zup, yh, c))
                recv(hblock(dn, yy), r_h.at[dn * YH + yy])
                w.send(hblock(dn, yy), hblock(dn, yy), s_hz.at[1, step, e], r_h.at[dn * YH + yy], s, d.fid(zdn, yh, c))
            else:
                top = H.at[pl.ds(0, half), lanes(up * YH + yy)]
                recv(hblock(up, yy), r_h.at[up * YH + yy])
                w.send(top, top, s_hz.at[0, step, e], r_h.at[up * YH + yy], s, d.fid(zup, yh, c))
                bot = H.at[pl.ds(half, half), lanes(dn * YH + yy)]
                recv(hblock(dn, yy), r_h.at[dn * YH + yy])
                w.send(bot, bot, s_hz.at[1, step, e], r_h2.at[yy], s, d.fid(zdn, yh, c))

    def gain(zz):
        cols = pl.ds(pl.multiple_of(zz * 512, 512), 512)
        part = nt(W2[:, cols], H[:, cols])
        QP[0] = QP[0] + part[:128]
        QP[1] = QP[1] + part[128:]

    forward(0)
    mine_w, other_w = W2.at[pl.ds(c * 128, 128)], W2.at[pl.ds(o * 128, 128)]
    pltpu.make_async_copy(mine_w, mine_w, l_w).wait()
    recv(other_w, r_w)
    w.make(other_w, other_w, s_w, r_w, s, mate).wait_send()
    QP[...] = jnp.zeros_like(QP)
    gain(z)
    forward(1)
    gain((z + 1) % Z)
    gain((z + Z - 1) % Z)
    forward(2)
    gain((z + 2) % Z)
    gain((z + Z - 2) % Z)
    kown.wait()
    for e in range(1, YH):
        yy = (yh + e) % YH
        recv(KW.at[:, :, :, lanes(yy)], r_k.at[yy])
    mine = pl.ds(pl.multiple_of(z * 512, 512), 512)
    for g in range(Z):
        part = nt(KW[g].reshape(64, 512), H[:, mine]).reshape(2, 2, 16, ROWS)
        PS[0, g] = part[:, 0]
        PS[1, g] = part[:, 1]
    w.send(PS.at[o], PR, s_p, r_p, s, mate)
    forward(3)
    recv(PR, r_p)
    SS[...] = PS[c] + PR[...]
    for e, zz in enumerate(zpeers):
        w.send(SS.at[zz], SR.at[z], s_s.at[e], r_s.at[z], s, d.fid(zz, yh, c))
    SR[z] = SS[z]
    gain((z + 3) % Z)
    gain((z + Z - 3) % Z)
    for zz in zpeers:
        recv(SR.at[zz], r_s.at[zz])
    total = SR[0]
    for i in range(1, Z):
        total = total + SR[i]
    kvb = total.astype(BF16)
    kf = kvb.astype(F32)
    b16 = pl.ds(pl.multiple_of((yh % 2) * 32 + c * 16, 16), 16)
    ck, sk = COS[b16, :], SIN[b16, :]
    iskey = yh < 2
    KB[0] = jnp.where(iskey, kf[0] * ck - kf[1] * sk, kf[0]).astype(BF16)
    KB[1] = jnp.where(iskey, kf[1] * ck + kf[0] * sk, kf[1]).astype(BF16)

    def kblock(yy, ll, xx):
        return KVT.at[yy // 2, :, yy % 2, c, :, lanes(ll * X + xx, ROWS)]

    for e, (yy, ll) in enumerate(ypeers):
        w.send(KB, kblock(yh, yl, x), s_b.at[e], r_b.at[yh, yl], ll * X + x, d.fid(z, yy, c))
    KVT[yh // 2, :, yh % 2, c, :, lanes(s, ROWS)] = KB[...]
    for i, xx in enumerate(xpeers):
        w.send(KB, kblock(yh, yl, x), s_x.at[0, i], r_x.at[x, yh, yl], yl * X + xx, f)
    far = (z + 4) % Z
    for e in range(YH):
        yy = (yh + e) % YH
        recv(H.at[pl.ds(0, half), lanes(far * YH + yy)], r_h.at[far * YH + yy])
        recv(H.at[pl.ds(half, half), lanes(far * YH + yy)], r_h2.at[yy])
    gain(far)
    w.send(QP.at[o], QR, s_q, r_q, s, mate)

    for e, (yy, ll) in enumerate(ypeers):
        block = kblock(yy, ll, x)
        recv(block, r_b.at[yy, ll])
        for i, xx in enumerate(xpeers):
            w.send(block, block, s_x.at[e + 1, i], r_x.at[x, yy, ll], yl * X + xx, f)
    for ll in range(YL):
        part = KVT.at[:, :, :, c, :, lanes(ll * X + x, ROWS)]
        w.send(part, part, s_c.at[0, ll], r_c.at[x, ll], s, mate)
    recv(QR, r_q)
    q = QP[c] + QR[...]
    q1, q2 = q[:64], q[64:]
    co, si = COS[...], SIN[...]
    qt = jnp.concatenate([q1 * co - q2 * si, q2 * co + q1 * si], axis=0)
    QB[...] = jnp.transpose(qt).astype(BF16)
    for i, xx in enumerate(xpeers):
        for ll in range(YL):
            for yy in range(YH):
                recv(kblock(yy, ll, xx), r_x.at[xx, yy, ll])
            part = KVT.at[:, :, :, c, :, lanes(ll * X + xx, ROWS)]
            w.send(part, part, s_c.at[i + 1, ll], r_c.at[xx, ll], s, mate)
    for xx in range(X):
        for ll in range(YL):
            recv(KVT.at[:, :, :, o, :, lanes(ll * X + xx, ROWS)], r_c.at[xx, ll])

    kt = KVT[0].reshape(HD, SEQ)
    vt = KVT[1].reshape(HD, SEQ)
    CH = 64

    def chunk(i, _):
        rows = pl.ds(pl.multiple_of(i * CH, CH), CH)
        raw = nn(QB[rows, :], KVT[0].reshape(HD, SEQ)) * SCALE
        t = s * ROWS + i * CH + lax.broadcasted_iota(jnp.int32, (CH, 1), 0)
        start = openings(t, doc)
        j = lax.broadcasted_iota(jnp.int32, (CH, SEQ), 1)
        raw = jnp.where((j >= start) & (j <= t), raw, -jnp.inf)
        top = jnp.max(raw, axis=1, keepdims=True)
        e = jnp.exp(raw - top)
        probs = (e * (1.0 / jnp.sum(e, axis=1, keepdims=True))).astype(BF16)
        PB[rows, :] = probs
        att_out[rows, :] = nt(probs, KVT[1].reshape(HD, SEQ)).astype(BF16)
        return 0
    lax.fori_loop(0, ROWS // CH, chunk, 0)

    att = att_out[...]
    da = dat[...]
    row_up = nn(pick, da)
    row_dot = jnp.sum(row_up * nn(pick, att), axis=1, keepdims=True)
    row_dp = nn(row_up.astype(BF16), vt)
    row_ds = (nn(pick, PB[...]) * (row_dp - row_dot)).astype(BF16)
    QG[c] = back(nt(row_ds, kt) * SCALE).astype(BF16)
    w.send(QG.at[c], QG.at[c], s_g, r_g, s, mate)
    rowdot = jnp.sum(da.astype(F32) * att.astype(F32), axis=1, keepdims=True)
    colp = nn(PB[...], CM[...])
    cv = nn(vt, CM[...]).astype(BF16)
    cds = (colp * (nn(da, cv) - rowdot)).astype(BF16)
    GP[0] = tn(cds, QB[...]).reshape(YL, X, PL, HD)
    GP[1] = tn(colp.astype(BF16), da).reshape(YL, X, PL, HD)
    w.send(GP.at[o], GR, s_d1, r_d1, s, mate)

    recv(QG.at[o], r_g)
    both = jnp.concatenate([QG[0], QG[1]], axis=1)

    def spread(zz, _):
        part = nn(both, W2[:, pl.ds(pl.multiple_of(zz * 512, 512), 512)])
        for yy in range(YH):
            QF[yy, zz] = part[:, yy * 128:(yy + 1) * 128].astype(BF16)
        QS[zz] = jnp.zeros((PL, HD), F32)
        for yy in range(YH):
            QS[zz] = QS[zz] + jnp.where(yy == yh, part[:, yy * 128:(yy + 1) * 128], 0.0)
        return 0
    lax.fori_loop(0, Z, spread, 0)

    recv(GR, r_d1)
    G1[...] = GP[c] + GR[...]
    for e, xx in enumerate(xpeers):
        w.send(G1.at[:, xx], GX.at[x], s_d2.at[e], r_d2.at[x], yl * X + xx, f)
    for e in range(1, YH):
        yy = (yh + e) % YH
        w.send(QF.at[yy], QY.at[yh], s_e2.at[e - 1], r_e2.at[yh], s, d.fid(z, yy, c))
    acc = G1[:, x]
    for xx in xpeers:
        recv(GX.at[xx], r_d2.at[xx])
        acc = acc + GX[xx]
    G2[...] = acc
    for e, (yy, ll) in enumerate(ypeers):
        w.send(G2.at[ll], GY.at[yh, yl], s_d3.at[e], r_d3.at[yh, yl], ll * X + x, d.fid(z, yy, c))
    for e in range(1, YH):
        yy = (yh + e) % YH
        recv(QY.at[yy], r_e2.at[yy])
        QS[...] = QS[...] + QY[yy].astype(F32)
    for e, zz in enumerate(zpeers):
        w.send(QS.at[zz], QZ.at[z], s_e3.at[e], r_e3.at[z], s, d.fid(zz, yh, c))
    acc = G2[yl]
    for yy, ll in ypeers:
        recv(GY.at[yy, ll], r_d3.at[yy, ll])
        acc = acc + GY[yy, ll]
    dkv = jnp.where(c == 0, back(acc * SCALE), acc).astype(BF16)
    DK[...] = dkv
    DKV[z, c] = dkv
    w.send(DK, DKV.at[z, c], s_d4.at[Z - 1, 0], r_d4.at[z, c], s, mate)
    for e, zz in enumerate(zpeers):
        for i, cc in enumerate((c, o)):
            w.send(DK, DKV.at[z, c], s_d4.at[e, i], r_d4.at[z, c], s, d.fid(zz, yh, cc))
    out = QS[z]
    for zz in zpeers:
        recv(QZ.at[zz], r_e3.at[zz])
        out = out + QZ[zz]
    kvload.wait()
    recv(DKV.at[z, o], r_d4.at[z, o])
    for zz in zpeers:
        recv(DKV.at[zz, 0], r_d4.at[zz, 0])
        recv(DKV.at[zz, 1], r_d4.at[zz, 1])
    wide = jnp.concatenate([DKV[g, p] for g in range(Z) for p in range(2)], axis=1)
    pg_out[...] = out + nn(wide, KVL[...])
    w.finish()


def per_device(hidden, q_weight, kv_weight, d_attended, doc_lengths, prompt_pos):
    vm = pl.BlockSpec(memory_space=pltpu.VMEM)
    anyspace = pl.BlockSpec(memory_space=pl.ANY)
    smem = pl.BlockSpec(memory_space=pltpu.SMEM)
    return pl.pallas_call(
        whole,
        out_shape=(jax.ShapeDtypeStruct((ROWS, HD), BF16),
                   jax.ShapeDtypeStruct((PL, HD), F32)),
        in_specs=[vm, anyspace, anyspace, anyspace, vm, smem, vm],
        out_specs=(vm, vm),
        scratch_shapes=[
            VMEM((ROWS, 4096), BF16),
            VMEM((256, 4096), BF16),
            VMEM((Z, 2, 32, 512), BF16),
            VMEM((2, Z, 2, 16, ROWS), F32),
            VMEM((Z, 2, 16, ROWS), F32),
            VMEM((Z, 2, 16, ROWS), F32),
            VMEM((Z, 2, 16, ROWS), F32),
            VMEM((2, 16, ROWS), BF16),
            VMEM((2, HD, ROWS), F32),
            VMEM((HD, ROWS), F32),
            VMEM((2, 2, 2, 2, 16, SEQ), BF16),
            VMEM((HD // 2, ROWS), F32),
            VMEM((HD // 2, ROWS), F32),
            VMEM((ROWS, HD), BF16),
            VMEM((ROWS, SEQ), BF16),
            VMEM((SEQ, NP), BF16),
            VMEM((SEQ, FB), BF16),
            VMEM((2, PL, HD), BF16),
            VMEM((2, YL, X, PL, HD), F32),
            VMEM((YL, X, PL, HD), F32),
            VMEM((YL, X, PL, HD), F32),
            VMEM((X, YL, PL, HD), F32),
            VMEM((YL, PL, HD), F32),
            VMEM((YH, YL, PL, HD), F32),
            VMEM((PL, HD), BF16),
            VMEM((Z, 2, PL, HD), BF16),
            VMEM((YH, Z, PL, HD), BF16),
            VMEM((YH, Z, PL, HD), BF16),
            VMEM((Z, PL, HD), F32),
            VMEM((Z, PL, HD), F32),
            DMA((3,)), DMA((Z * YH,)), DMA((YH,)), DMA((2, 4, YH)),
            DMA(()), DMA(()), DMA(()),
            DMA((3,)), DMA((YH,)), DMA(()),
            DMA(()), DMA(()),
            DMA((Z - 1,)), DMA((Z,)),
            DMA((YH * YL - 1,)), DMA((YH, YL)),
            DMA((YH * YL, X - 1)), DMA((X, YH, YL)),
            DMA((X, YL)), DMA((X, YL)),
            DMA(()), DMA(()), DMA(()),
            DMA(()), DMA(()),
            DMA(()), DMA(()),
            DMA((X - 1,)), DMA((X,)),
            DMA((YH * YL - 1,)), DMA((YH, YL)),
            DMA((Z, 2)), DMA((Z, 2)),
            DMA((YH - 1,)), DMA((YH,)),
            DMA((Z - 1,)), DMA((Z,)),
        ],
        compiler_params=pltpu.CompilerParams(
            collective_id=0, has_side_effects=True, vmem_limit_bytes=48 << 20),
        name="whole",
    )(hidden, q_weight, kv_weight.reshape(Z, 2, 2, 2, 32, FB), kv_weight, d_attended,
      doc_lengths, prompt_pos.reshape(1, NP))


def solution(mesh):
    placed = (P("seq", "fsdp"), P("fsdp", None), P(None, "fsdp"), P("seq", "fsdp"), P(), P())
    return jax.shard_map(
        per_device,
        mesh=mesh,
        in_specs=placed,
        out_specs=(P("seq", "fsdp"), P("seq", "fsdp")),
        check_vma=False,
    )
```

```python
import functools
import math

import jax
import jax.numpy as jnp
from jax import lax
from jax.experimental import pallas as pl
from jax.experimental.pallas import tpu as pltpu
from jax.sharding import PartitionSpec as P

ROPE_THETA = 1000000.0
MESH = pl.DeviceIdType.MESH
F32 = jnp.float32
BF16 = jnp.bfloat16
VMEM = pltpu.VMEM
DMA = pltpu.SemaphoreType.DMA

X, YL, YH, Z, C = 4, 2, 4, 8, 2
ROWS, HD, FB = 256, 128, 128


def nt(a, b):
    return lax.dot_general(a, b, (((1,), (1,)), ((), ())), preferred_element_type=F32)


class Place:
    def __init__(self):
        self.s = lax.axis_index("seq")
        self.f = lax.axis_index("fsdp")
        self.x = self.s % X
        self.yl = self.s // X
        self.z = self.f // (YH * C)
        self.yh = (self.f // C) % YH
        self.c = self.f % C
        self.o = 1 - self.c

    def fid(self, z, yh, c):
        return (z * YH + yh) * C + c


class Wires:
    def __init__(self):
        self.open = []

    def make(self, src, dst, ss, rs, seq, fs):
        return pltpu.make_async_remote_copy(
            src_ref=src, dst_ref=dst, send_sem=ss, recv_sem=rs,
            device_id={"seq": seq, "fsdp": fs}, device_id_type=MESH)

    def send(self, *args):
        copy = self.make(*args)
        copy.start()
        self.open.append(copy)

    def finish(self):
        for copy in self.open:
            copy.wait_send()


def nn(a, b):
    return lax.dot_general(a, b, (((1,), (0,)), ((), ())), preferred_element_type=F32)


def tn(a, b):
    return lax.dot_general(a, b, (((0,), (0,)), ((), ())), preferred_element_type=F32)


def lanes(k, n=128):
    return pl.ds(pl.multiple_of(k * n, n), n)


STEP = -2.0 * math.log(ROPE_THETA) / HD
SCALE = 1.0 / math.sqrt(HD)
SEQ, NP, PL = 2048, 128, 16


def openings(tokens, doc):
    end = jnp.int32(0)
    start = jnp.zeros_like(tokens)
    for i in range(4):
        end = end + doc[i]
        start = start + jnp.where(tokens >= end, doc[i], 0)
    return start


def whole(hid, qw, kvw, kvflat, dhbm, dochbm, phbm, att_out, pg_out,
          H, W2, KZ, KY, KW, KWF, KP, KR, KB, QP, QR, KVT, COS, SIN, QB, PB, CM, KVL,
          QG, GP, GX, G2, GY, DK, DKV, QF, QY, QS, QZ, dat, doc, prow,
          s_h, r_h, r_h2, s_hz, s_w, r_w, l_w, s_kz, r_kz, s_ky, r_ky, s_kl, r_kl, s_kx, r_kx,
          s_p, r_p, s_b, r_b, s_x, r_x, s_c, r_c, s_q, r_q, l_v, l_in,
          s_g, r_g, s_d2, r_d2, s_d3, r_d3, s_d4, r_d4, s_e2, r_e2, s_e3, r_e3):
    d = Place()
    s, f, x, yl, z, yh, c, o = d.s, d.f, d.x, d.yl, d.z, d.yh, d.c, d.o
    mate = d.fid(z, yh, o)
    zup, zdn = (z + 1) % Z, (z + Z - 1) % Z
    w = Wires()

    loads = [pltpu.make_async_copy(a, b, l_in.at[i]) for i, (a, b) in enumerate(
        ((dochbm, doc), (phbm, prow), (dhbm, dat)))]
    for load in loads:
        load.start()
    bar = pltpu.get_barrier_semaphore()
    peers = [(s, mate)]
    ypeers = []
    for e in range(1, YH * YL):
        y = (yh * YL + yl + e) % (YH * YL)
        ypeers.append((y // YL, y % YL))
        peers.append(((y % YL) * X + x, d.fid(z, y // YL, c)))
    xpeers = [(x + e) % X for e in range(1, X)]
    for xx in xpeers:
        peers.append((yl * X + xx, f))
        peers.append((yl * X + xx, mate))
    zpeers = [(z + e) % Z for e in range(1, Z)]
    for zz in zpeers:
        peers.append((s, d.fid(zz, yh, c)))
        peers.append((s, d.fid(zz, yh, o)))
    for ps, pf in peers:
        pl.semaphore_signal(bar, inc=1, device_id={"seq": ps, "fsdp": pf}, device_id_type=MESH)
    pl.semaphore_wait(bar, len(peers))

    def hblock(zz, yy):
        return H.at[:, lanes(zz * YH + yy)]

    def recv(ref, sem):
        w.make(ref, ref, s_q, sem, s, mate).wait_recv()

    def eighth(g):
        return kvw.at[g, :, s // 4, :, pl.ds(pl.multiple_of((s % 4) * 8, 8), 8), :]
    for e, zz in enumerate(zpeers):
        w.send(eighth(zz), KZ.at[z], s_kz.at[e], r_kz.at[z], s, d.fid(zz, yh, c))
    kzown = pltpu.make_async_copy(eighth(z), KZ.at[z], l_in.at[3])
    kzown.start()
    hown = pltpu.make_async_copy(hid, hblock(z, yh), l_in.at[4])
    hown.start()
    for e in range(1, YH):
        yy = (yh + e) % YH
        w.send(hid, hblock(z, yh), s_h.at[e - 1], r_h.at[z * YH + yh], s, d.fid(z, yy, c))
    for i, zz in enumerate((zup, zdn)):
        w.send(hid, hblock(z, yh), s_hz.at[i, 0, 0], r_h.at[z * YH + yh], s, d.fid(zz, yh, c))
    def wload(k, _):
        pltpu.make_async_copy(qw.at[:, pl.ds(pl.multiple_of(k * 256 + c * 128, 128), 128)],
                              W2.at[pl.ds(c * 128, 128), lanes(k)], l_w).start()
        w.make(qw.at[:, pl.ds(pl.multiple_of(k * 256 + o * 128, 128), 128)],
               W2.at[pl.ds(c * 128, 128), lanes(k)], s_w, r_w, s, mate).start()
        return 0
    lax.fori_loop(0, Z * YH, wload, 0)
    kvload = pltpu.make_async_copy(kvflat, KVL, l_v)
    kvload.start()
    for load in loads:
        load.wait()

    tok = s * ROWS + lax.broadcasted_iota(jnp.int32, (1, ROWS), 1)
    place = (tok - openings(tok, doc)).astype(F32)
    freq = jnp.exp(lax.broadcasted_iota(jnp.int32, (HD // 2, 1), 0).astype(F32) * STEP)
    angle = freq * place
    COS[...] = jnp.cos(angle)
    SIN[...] = jnp.sin(angle)
    prompts = prow[...]
    for i in range(8):
        at = i * 256 + lax.broadcasted_iota(jnp.int32, (256, NP), 0)
        CM[pl.ds(i * 256, 256), :] = jnp.where(at == prompts, 1.0, 0.0).astype(BF16)
    near = lax.broadcasted_iota(jnp.int32, (PL, NP), 1) == (
        s * PL + lax.broadcasted_iota(jnp.int32, (PL, NP), 0))
    own_p = jnp.sum(jnp.where(near, prompts.astype(F32), 0.0), axis=1, keepdims=True).astype(jnp.int32)
    pick = jnp.where(lax.broadcasted_iota(jnp.int32, (PL, ROWS), 1) == own_p - s * ROWS,
                     1.0, 0.0).astype(BF16)
    lane = lax.broadcasted_iota(jnp.int32, (1, HD), 1)
    freq_l = jnp.exp(jnp.where(lane < 64, lane, lane - 64).astype(F32) * STEP)
    angle_p = (own_p - openings(own_p, doc)).astype(F32) * freq_l
    cos_p = jnp.cos(angle_p)
    sin_p = jnp.where(lane < 64, 1.0, -1.0) * jnp.sin(angle_p)

    def back(u):
        return u * cos_p + pltpu.roll(u, 64, 1) * sin_p

    half = ROWS // 2

    def forward(step):
        up, dn = (z + Z - step) % Z, (z + step) % Z
        for e in range(YH):
            yy = (yh + e) % YH
            if step == 0:
                if e == 0:
                    continue
                recv(hblock(z, yy), r_h.at[z * YH + yy])
                w.send(hblock(z, yy), hblock(z, yy), s_hz.at[0, step, e], r_h.at[z * YH + yy], s, d.fid(zup, yh, c))
                w.send(hblock(z, yy), hblock(z, yy), s_hz.at[1, step, e], r_h.at[z * YH + yy], s, d.fid(zdn, yh, c))
            elif step < 3:
                recv(hblock(up, yy), r_h.at[up * YH + yy])
                w.send(hblock(up, yy), hblock(up, yy), s_hz.at[0, step, e], r_h.at[up * YH + yy], s, d.fid(zup, yh, c))
                recv(hblock(dn, yy), r_h.at[dn * YH + yy])
                w.send(hblock(dn, yy), hblock(dn, yy), s_hz.at[1, step, e], r_h.at[dn * YH + yy], s, d.fid(zdn, yh, c))
            else:
                top = H.at[pl.ds(0, half), lanes(up * YH + yy)]
                recv(hblock(up, yy), r_h.at[up * YH + yy])
                w.send(top, top, s_hz.at[0, step, e], r_h.at[up * YH + yy], s, d.fid(zup, yh, c))
                bot = H.at[pl.ds(half, half), lanes(dn * YH + yy)]
                recv(hblock(dn, yy), r_h.at[dn * YH + yy])
                w.send(bot, bot, s_hz.at[1, step, e], r_h2.at[yy], s, d.fid(zdn, yh, c))

    def gain(zz):
        cols = pl.ds(pl.multiple_of(zz * 512, 512), 512)
        part = nt(W2[:, cols], H[:, cols])
        QP[0] = QP[0] + part[:128]
        QP[1] = QP[1] + part[128:]

    def gain_kv(zz):
        cols = pl.ds(pl.multiple_of(zz * 512, 512), 512)
        part = nt(KWF[:, cols], H[:, cols]).reshape(2, 2, 16, ROWS)
        KP[0] = KP[0] + part[:, 0]
        KP[1] = KP[1] + part[:, 1]

    kzown.wait()
    for zz in zpeers:
        recv(KZ.at[zz], r_kz.at[zz])
    for e in range(1, YH):
        yy = (yh + e) % YH
        w.send(KZ.at[:, yy // 2, yy % 2], KY.at[yh], s_ky.at[e - 1], r_ky.at[yh], s, d.fid(z, yy, c))
    KY[yh] = KZ[:, yh // 2, yh % 2]
    forward(0)
    for e in range(1, YH):
        yy = (yh + e) % YH
        recv(KY.at[yy], r_ky.at[yy])
    for zz in range(Z):
        for yy in range(YH):
            KW[s, :, pl.ds((zz * YH + yy) * 128, 128)] = KY[yy, zz]
    sx = (1 - yl) * X + x
    w.send(KW.at[s], KW.at[s], s_kl, r_kl, sx, f)
    mine_w, other_w = W2.at[pl.ds(c * 128, 128)], W2.at[pl.ds(o * 128, 128)]
    pltpu.make_async_copy(mine_w, mine_w, l_w).wait()
    recv(other_w, r_w)
    w.make(other_w, other_w, s_w, r_w, s, mate).wait_send()
    hown.wait()
    QP[...] = jnp.zeros_like(QP)
    KP[...] = jnp.zeros_like(KP)
    gain(z)
    forward(1)
    recv(KW.at[sx], r_kl)
    for i, xx in enumerate(xpeers):
        for ll in range(YL):
            w.send(KW.at[ll * X + x], KW.at[ll * X + x], s_kx.at[i, ll], r_kx.at[x, ll], yl * X + xx, f)
    gain((z + 1) % Z)
    gain((z + Z - 1) % Z)
    forward(2)
    gain((z + 2) % Z)
    gain((z + Z - 2) % Z)
    forward(3)
    gain((z + 3) % Z)
    gain((z + Z - 3) % Z)
    for xx in xpeers:
        for ll in range(YL):
            recv(KW.at[ll * X + xx], r_kx.at[xx, ll])
    for i in range(X * YL):
        KWF[pl.ds(i * 8, 8), :] = KW[i]
    for i in range(Z):
        if i != 4:
            gain_kv((z + i) % Z)
    far = (z + 4) % Z
    for e in range(YH):
        yy = (yh + e) % YH
        recv(H.at[pl.ds(0, half), lanes(far * YH + yy)], r_h.at[far * YH + yy])
        recv(H.at[pl.ds(half, half), lanes(far * YH + yy)], r_h2.at[yy])
    gain_kv(far)
    w.send(KP.at[o], KR, s_p, r_p, s, mate)
    gain(far)
    w.send(QP.at[o], QR, s_q, r_q, s, mate)
    recv(KR, r_p)
    total = KP[c] + KR[...]
    kvb = total.astype(BF16)
    kf = kvb.astype(F32)
    b16 = pl.ds(pl.multiple_of((yh % 2) * 32 + c * 16, 16), 16)
    ck, sk = COS[b16, :], SIN[b16, :]
    iskey = yh < 2
    KB[0] = jnp.where(iskey, kf[0] * ck - kf[1] * sk, kf[0]).astype(BF16)
    KB[1] = jnp.where(iskey, kf[1] * ck + kf[0] * sk, kf[1]).astype(BF16)

    def kblock(yy, ll, xx):
        return KVT.at[yy // 2, :, yy % 2, c, :, lanes(ll * X + xx, ROWS)]

    for e, (yy, ll) in enumerate(ypeers):
        w.send(KB, kblock(yh, yl, x), s_b.at[e], r_b.at[yh, yl], ll * X + x, d.fid(z, yy, c))
    KVT[yh // 2, :, yh % 2, c, :, lanes(s, ROWS)] = KB[...]
    for i, xx in enumerate(xpeers):
        w.send(KB, kblock(yh, yl, x), s_x.at[0, i], r_x.at[x, yh, yl], yl * X + xx, f)
    for e, (yy, ll) in enumerate(ypeers):
        block = kblock(yy, ll, x)
        recv(block, r_b.at[yy, ll])
        for i, xx in enumerate(xpeers):
            w.send(block, block, s_x.at[e + 1, i], r_x.at[x, yy, ll], yl * X + xx, f)
    for ll in range(YL):
        part = KVT.at[:, :, :, c, :, lanes(ll * X + x, ROWS)]
        w.send(part, part, s_c.at[0, ll], r_c.at[x, ll], s, mate)
    recv(QR, r_q)
    q = QP[c] + QR[...]
    q1, q2 = q[:64], q[64:]
    co, si = COS[...], SIN[...]
    qt = jnp.concatenate([q1 * co - q2 * si, q2 * co + q1 * si], axis=0)
    QB[...] = jnp.transpose(qt).astype(BF16)
    for i, xx in enumerate(xpeers):
        for ll in range(YL):
            for yy in range(YH):
                recv(kblock(yy, ll, xx), r_x.at[xx, yy, ll])
            part = KVT.at[:, :, :, c, :, lanes(ll * X + xx, ROWS)]
            w.send(part, part, s_c.at[i + 1, ll], r_c.at[xx, ll], s, mate)
    for xx in range(X):
        for ll in range(YL):
            recv(KVT.at[:, :, :, o, :, lanes(ll * X + xx, ROWS)], r_c.at[xx, ll])

    kt = KVT[0].reshape(HD, SEQ)
    vt = KVT[1].reshape(HD, SEQ)
    CH = 64

    def chunk(i, _):
        rows = pl.ds(pl.multiple_of(i * CH, CH), CH)
        raw = nn(QB[rows, :], KVT[0].reshape(HD, SEQ)) * SCALE
        t = s * ROWS + i * CH + lax.broadcasted_iota(jnp.int32, (CH, 1), 0)
        start = openings(t, doc)
        j = lax.broadcasted_iota(jnp.int32, (CH, SEQ), 1)
        raw = jnp.where((j >= start) & (j <= t), raw, -jnp.inf)
        top = jnp.max(raw, axis=1, keepdims=True)
        e = jnp.exp(raw - top)
        probs = (e * (1.0 / jnp.sum(e, axis=1, keepdims=True))).astype(BF16)
        PB[rows, :] = probs
        att_out[rows, :] = nt(probs, KVT[1].reshape(HD, SEQ)).astype(BF16)
        return 0
    lax.fori_loop(0, ROWS // CH, chunk, 0)

    att = att_out[...]
    da = dat[...]
    rowdot = jnp.sum(da.astype(F32) * att.astype(F32), axis=1, keepdims=True)
    colp = nn(PB[...], CM[...])
    cv = nn(vt, CM[...]).astype(BF16)
    cds = (colp * (nn(da, cv) - rowdot)).astype(BF16)
    GP[0] = tn(cds, QB[...]).reshape(YL, X, PL, HD)
    GP[1] = tn(colp.astype(BF16), da).reshape(YL, X, PL, HD)
    for e in range(X):
        xx = (x + e) % X
        for i, (pp, ff) in enumerate(((c, f), (o, mate))):
            if e or i:
                w.send(GP.at[pp, :, xx], GX.at[x, c], s_d2.at[e, i], r_d2.at[x, c], yl * X + xx, ff)
    row_up = nn(pick, da)
    row_dot = jnp.sum(row_up * nn(pick, att), axis=1, keepdims=True)
    row_dp = nn(row_up.astype(BF16), vt)
    row_ds = (nn(pick, PB[...]) * (row_dp - row_dot)).astype(BF16)
    QG[c] = back(nt(row_ds, kt) * SCALE).astype(BF16)
    w.send(QG.at[c], QG.at[c], s_g, r_g, s, mate)
    recv(QG.at[o], r_g)
    both = jnp.concatenate([QG[0], QG[1]], axis=1)

    def spread(zz, _):
        part = nn(both, W2[:, pl.ds(pl.multiple_of(zz * 512, 512), 512)])
        for yy in range(YH):
            QF[yy, zz] = part[:, yy * 128:(yy + 1) * 128].astype(BF16)
        QS[zz] = jnp.zeros((PL, HD), F32)
        for yy in range(YH):
            QS[zz] = QS[zz] + jnp.where(yy == yh, part[:, yy * 128:(yy + 1) * 128], 0.0)
        return 0
    lax.fori_loop(0, Z, spread, 0)

    for e in range(1, YH):
        yy = (yh + e) % YH
        w.send(QF.at[yy], QY.at[yh], s_e2.at[e - 1], r_e2.at[yh], s, d.fid(z, yy, c))
    recv(GX.at[x, o], r_d2.at[x, o])
    acc = GP[c, :, x] + GX[x, o]
    for xx in xpeers:
        for cc in range(C):
            recv(GX.at[xx, cc], r_d2.at[xx, cc])
            acc = acc + GX[xx, cc]
    G2[...] = acc
    for e, (yy, ll) in enumerate(ypeers):
        w.send(G2.at[ll], GY.at[yh, yl], s_d3.at[e], r_d3.at[yh, yl], ll * X + x, d.fid(z, yy, c))
    for e in range(1, YH):
        yy = (yh + e) % YH
        recv(QY.at[yy], r_e2.at[yy])
        QS[...] = QS[...] + QY[yy].astype(F32)
    for e, zz in enumerate(zpeers):
        w.send(QS.at[zz], QZ.at[z], s_e3.at[e], r_e3.at[z], s, d.fid(zz, yh, c))
    acc = G2[yl]
    for yy, ll in ypeers:
        recv(GY.at[yy, ll], r_d3.at[yy, ll])
        acc = acc + GY[yy, ll]
    dkv = jnp.where(c == 0, back(acc * SCALE), acc).astype(BF16)
    DK[...] = dkv
    DKV[z, c] = dkv
    w.send(DK, DKV.at[z, c], s_d4.at[Z - 1, 0], r_d4.at[z, c], s, mate)
    for e, zz in enumerate(zpeers):
        for i, cc in enumerate((c, o)):
            w.send(DK, DKV.at[z, c], s_d4.at[e, i], r_d4.at[z, c], s, d.fid(zz, yh, cc))
    out = QS[z]
    for zz in zpeers:
        recv(QZ.at[zz], r_e3.at[zz])
        out = out + QZ[zz]
    kvload.wait()
    recv(DKV.at[z, o], r_d4.at[z, o])
    for zz in zpeers:
        recv(DKV.at[zz, 0], r_d4.at[zz, 0])
        recv(DKV.at[zz, 1], r_d4.at[zz, 1])
    wide = jnp.concatenate([DKV[g, p] for g in range(Z) for p in range(2)], axis=1)
    pg_out[...] = out + nn(wide, KVL[...])
    w.finish()


def per_device(hidden, q_weight, kv_weight, d_attended, doc_lengths, prompt_pos):
    vm = pl.BlockSpec(memory_space=pltpu.VMEM)
    hbm = pl.BlockSpec(memory_space=pltpu.HBM)
    return pl.pallas_call(
        whole,
        out_shape=(jax.ShapeDtypeStruct((ROWS, HD), BF16),
                   jax.ShapeDtypeStruct((PL, HD), F32)),
        in_specs=[hbm] * 7,
        out_specs=(vm, vm),
        scratch_shapes=[
            VMEM((ROWS, 4096), BF16),
            VMEM((256, 4096), BF16),
            VMEM((Z, 2, 2, 8, FB), BF16),
            VMEM((YH, Z, 8, FB), BF16),
            VMEM((X * YL, 8, 4096), BF16),
            VMEM((64, 4096), BF16),
            VMEM((2, 2, 16, ROWS), F32),
            VMEM((2, 16, ROWS), F32),
            VMEM((2, 16, ROWS), BF16),
            VMEM((2, HD, ROWS), F32),
            VMEM((HD, ROWS), F32),
            VMEM((2, 2, 2, 2, 16, SEQ), BF16),
            VMEM((HD // 2, ROWS), F32),
            VMEM((HD // 2, ROWS), F32),
            VMEM((ROWS, HD), BF16),
            VMEM((ROWS, SEQ), BF16),
            VMEM((SEQ, NP), BF16),
            VMEM((SEQ, FB), BF16),
            VMEM((2, PL, HD), BF16),
            VMEM((2, YL, X, PL, HD), F32),
            VMEM((X, C, YL, PL, HD), F32),
            VMEM((YL, PL, HD), F32),
            VMEM((YH, YL, PL, HD), F32),
            VMEM((PL, HD), BF16),
            VMEM((Z, 2, PL, HD), BF16),
            VMEM((YH, Z, PL, HD), BF16),
            VMEM((YH, Z, PL, HD), BF16),
            VMEM((Z, PL, HD), F32),
            VMEM((Z, PL, HD), F32),
            VMEM((ROWS, FB), BF16),
            pltpu.SMEM((4,), jnp.int32),
            VMEM((1, NP), jnp.int32),
            DMA((3,)), DMA((Z * YH,)), DMA((YH,)), DMA((2, 4, YH)),
            DMA(()), DMA(()), DMA(()),
            DMA((Z - 1,)), DMA((Z,)), DMA((YH - 1,)), DMA((YH,)),
            DMA(()), DMA(()), DMA((X - 1, YL)), DMA((X, YL)),
            DMA(()), DMA(()),
            DMA((YH * YL - 1,)), DMA((YH, YL)),
            DMA((YH * YL, X - 1)), DMA((X, YH, YL)),
            DMA((X, YL)), DMA((X, YL)),
            DMA(()), DMA(()), DMA(()), DMA((5,)),
            DMA(()), DMA(()),
            DMA((X, C)), DMA((X, C)),
            DMA((YH * YL - 1,)), DMA((YH, YL)),
            DMA((Z, 2)), DMA((Z, 2)),
            DMA((YH - 1,)), DMA((YH,)),
            DMA((Z - 1,)), DMA((Z,)),
        ],
        compiler_params=pltpu.CompilerParams(
            collective_id=0, has_side_effects=True, vmem_limit_bytes=67043328),
        name="whole",
    )(hidden, q_weight, kv_weight.reshape(Z, 2, 2, 2, 32, FB), kv_weight, d_attended,
      doc_lengths, prompt_pos.reshape(1, NP))


def solution(mesh):
    placed = (P("seq", "fsdp"), P("fsdp", None), P(None, "fsdp"), P("seq", "fsdp"), P(), P())
    return jax.shard_map(
        per_device,
        mesh=mesh,
        in_specs=placed,
        out_specs=(P("seq", "fsdp"), P("seq", "fsdp")),
        check_vma=False,
    )
```

```python
import functools
import math

import jax
import jax.numpy as jnp
from jax import lax
from jax.experimental import pallas as pl
from jax.experimental.pallas import tpu as pltpu
from jax.sharding import PartitionSpec as P

ROPE_THETA = 1000000.0
MESH = pl.DeviceIdType.MESH
F32 = jnp.float32
BF16 = jnp.bfloat16
VMEM = pltpu.VMEM
DMA = pltpu.SemaphoreType.DMA

X, YL, YH, Z, C = 4, 2, 4, 8, 2
ROWS, HD, FB = 256, 128, 128


def nt(a, b):
    return lax.dot_general(a, b, (((1,), (1,)), ((), ())), preferred_element_type=F32)


class Place:
    def __init__(self):
        self.s = lax.axis_index("seq")
        self.f = lax.axis_index("fsdp")
        self.x = self.s % X
        self.yl = self.s // X
        self.z = self.f // (YH * C)
        self.yh = (self.f // C) % YH
        self.c = self.f % C
        self.o = 1 - self.c

    def fid(self, z, yh, c):
        return (z * YH + yh) * C + c


class Wires:
    def __init__(self):
        self.open = []

    def make(self, src, dst, ss, rs, seq, fs):
        return pltpu.make_async_remote_copy(
            src_ref=src, dst_ref=dst, send_sem=ss, recv_sem=rs,
            device_id={"seq": seq, "fsdp": fs}, device_id_type=MESH)

    def send(self, *args):
        copy = self.make(*args)
        copy.start()
        self.open.append(copy)

    def finish(self):
        for copy in self.open:
            copy.wait_send()


def nn(a, b):
    return lax.dot_general(a, b, (((1,), (0,)), ((), ())), preferred_element_type=F32)


def tn(a, b):
    return lax.dot_general(a, b, (((0,), (0,)), ((), ())), preferred_element_type=F32)


class Flow:
    RATE = {"z+": 45.0, "z-": 45.0, "y+": 22.0, "y-": 22.0, "x+": 45.0, "x-": 45.0, "m": 300.0, "n": 1e9}
    LAG = {"z+": 1.7, "z-": 1.7, "y+": 2.5, "y-": 2.5, "x+": 1.7, "x-": 1.7, "m": 0.9, "n": 4.0}

    def __init__(self):
        self.tasks = {}
        self.recvs = {}

    def arrival(self, key, ref, sem):
        self.recvs[key] = (ref, sem)

    def task(self, name, needs=(), after=(), sends=(), work=None, cost=0.05, rank=0):
        self.tasks[name] = (set(needs), set(after), list(sends), work, cost, rank)

    def order(self):
        at, done, free, now, out = {}, {}, {}, 0.0, []
        todo = list(self.tasks)
        while todo:
            best = None
            for i, name in enumerate(todo):
                needs, after, _, _, _, rank = self.tasks[name]
                if all(n in at for n in needs) and all(a in done for a in after):
                    ready = max([at[n] for n in needs] + [done[a] for a in after] + [0.0])
                    cand = (max(ready, now), rank, i)
                    if best is None or cand < best:
                        best = cand
            assert best is not None, todo
            name = todo.pop(best[2])
            _, _, sends, _, cost, _ = self.tasks[name]
            now = best[0] + cost
            done[name] = now
            for link, size, key, _ in sends:
                start = max(free.get(link, 0.0), now)
                free[link] = start + size / self.RATE[link]
                if key is not None:
                    at[key] = max(at.get(key, 0.0), free[link] + self.LAG[link])
            out.append(name)
        self.model = done
        return out

    def emit(self, recv):
        for name in self.order():
            needs, _, sends, work, _, _ = self.tasks[name]
            for key in sorted(needs, key=repr):
                recv(*self.recvs[key])
            if work is not None:
                work()
            for _, _, _, go in sends:
                go()


def lanes(k, n=128):
    return pl.ds(pl.multiple_of(k * n, n), n)


STEP = -2.0 * math.log(ROPE_THETA) / HD
SCALE = 1.0 / math.sqrt(HD)
SEQ, NP, PL = 2048, 128, 16


def openings(tokens, doc):
    end = jnp.int32(0)
    start = jnp.zeros_like(tokens)
    for i in range(4):
        end = end + doc[i]
        start = start + jnp.where(tokens >= end, doc[i], 0)
    return start


def whole(hid, qw, kvw, kvflat, dhbm, dochbm, phbm, att_out, pg_out,
          H, W2, KZ, KY, KW, KWF, KP, KR, KB, QP, QR, KVT, COS, SIN, QB, PB, CM, KVL,
          QG, GP, GX, G2, GY, DK, DKV, QF, QY, QS, QZ, dat, doc, prow,
          s_h, r_h, s_w, r_w, l_w, s_kz, r_kz, s_ky, r_ky, s_kl, r_kl, s_kx, r_kx,
          s_p, r_p, s_b, r_b, s_x, r_x, s_c, r_c, s_q, r_q, l_v, l_in,
          s_g, r_g, s_d2, r_d2, s_d3, r_d3, s_d4, r_d4, s_e2, r_e2, s_e3, r_e3):
    d = Place()
    s, f, x, yl, z, yh, c, o = d.s, d.f, d.x, d.yl, d.z, d.yh, d.c, d.o
    mate = d.fid(z, yh, o)
    zup, zdn = (z + 1) % Z, (z + Z - 1) % Z
    w = Wires()

    loads = [pltpu.make_async_copy(a, b, l_in.at[i]) for i, (a, b) in enumerate(
        ((dochbm, doc), (phbm, prow), (dhbm, dat)))]
    for load in loads:
        load.start()
    bar = pltpu.get_barrier_semaphore()
    peers = [(s, mate)]
    ypeers = []
    for e in range(1, YH * YL):
        y = (yh * YL + yl + e) % (YH * YL)
        ypeers.append((y // YL, y % YL))
        peers.append(((y % YL) * X + x, d.fid(z, y // YL, c)))
    xpeers = [(x + e) % X for e in range(1, X)]
    for xx in xpeers:
        peers.append((yl * X + xx, f))
        peers.append((yl * X + xx, mate))
    zpeers = [(z + e) % Z for e in range(1, Z)]
    for zz in zpeers:
        peers.append((s, d.fid(zz, yh, c)))
        peers.append((s, d.fid(zz, yh, o)))
    for ps, pf in peers:
        pl.semaphore_signal(bar, inc=1, device_id={"seq": ps, "fsdp": pf}, device_id_type=MESH)
    pl.semaphore_wait(bar, len(peers))

    def hblock(zz, yy):
        return H.at[:, lanes(zz * YH + yy)]

    def recv(ref, sem):
        w.make(ref, ref, s_q, sem, s, mate).wait_recv()

    def eighth(g):
        return kvw.at[g, :, s // 4, :, pl.ds(pl.multiple_of((s % 4) * 8, 8), 8), :]
    for e, zz in enumerate(zpeers):
        w.send(eighth(zz), KZ.at[z], s_kz.at[e], r_kz.at[z], s, d.fid(zz, yh, c))
    kzown = pltpu.make_async_copy(eighth(z), KZ.at[z], l_in.at[3])
    kzown.start()
    hown = pltpu.make_async_copy(hid, hblock(z, yh), l_in.at[4])
    hown.start()
    flow = Flow()
    used = [0]
    ROW = {"Y": {"F": (0, 192), "A": (0, 96), "B": (96, 96)},
           "Z": {"F": (192, 64), "A": (192, 32), "B": (224, 32)}}

    def hpiece(kind, dz, dy, h):
        r0, n = ROW[kind][h]
        return H.at[pl.ds(r0, n), lanes((z + dz) % Z * YH + (yh + dy) % YH)]

    def hsem(kind, dz, dy, h):
        return r_h.at[0 if kind == "Y" else 1, 1 if h == "B" else 0, (z + dz) % Z * YH + (yh + dy) % YH]

    def hsend(kind, dz, dy, h, way):
        ez, ey = {"z+": (1, 0), "z-": (-1, 0), "y+": (0, 1), "y-": (0, -1)}[way]
        r0, n = ROW[kind][h]
        slot = s_h.at[used[0]]
        used[0] += 1
        src = hid.at[pl.ds(r0, n), :] if (dz, dy) == (0, 0) else hpiece(kind, dz, dy, h)

        def go():
            w.send(src, hpiece(kind, dz, dy, h), slot, hsem(kind, dz, dy, h),
                   s, d.fid((z + ez) % Z, (yh + ey) % YH, c))
        return (way, n / 4, (kind, (dz - ez) % Z, (dy - ey) % YH, h), go)

    def hidden_tasks():
        for kind in "YZ":
            for dz in range(Z):
                for dy in range(YH):
                    two = dy == 2 and (kind == "Z" or dz == 0) or dz == 4 and (kind == "Y" or dy == 0)
                    needs = [(kind, dz, dy, h) for h in ("AB" if two else "F")] if dz or dy else []
                    for key in needs:
                        flow.arrival(key, hpiece(*key), hsem(*key))
                    sends = []
                    if kind == "Y":
                        if dz == 0:
                            if dy == 0:
                                sends += [("y+", "F"), ("y-", "F")]
                            if dy == 3:
                                sends.append(("y+", "A"))
                            if dy == 1:
                                sends.append(("y-", "B"))
                            sends += [("z+", "F"), ("z-", "F")]
                        elif dz > 4:
                            sends.append(("z+", "A" if dz == 5 else "F"))
                        elif dz < 4:
                            sends.append(("z-", "B" if dz == 3 else "F"))
                    elif dy == 0:
                        if dz == 0:
                            sends += [("z+", "F"), ("z-", "F")]
                        elif dz > 4:
                            sends.append(("z+", "A" if dz == 5 else "F"))
                        elif dz < 4:
                            sends.append(("z-", "B" if dz == 3 else "F"))
                        sends += [("y+", "F"), ("y-", "F")]
                    elif dy == 3:
                        sends.append(("y+", "A"))
                    elif dy == 1:
                        sends.append(("y-", "B"))
                    flow.task((kind, dz, dy), needs=needs,
                              sends=[hsend(kind, dz, dy, h, way) for way, h in sends],
                              rank=0 if dz or dy else (-2 if kind == "Z" else -1))
    hidden_tasks()

    T = {}

    def setup():
        def wload(k, _):
            pltpu.make_async_copy(qw.at[:, pl.ds(pl.multiple_of(k * 256 + c * 128, 128), 128)],
                                  W2.at[pl.ds(c * 128, 128), lanes(k)], l_w).start()
            w.make(qw.at[:, pl.ds(pl.multiple_of(k * 256 + o * 128, 128), 128)],
                   W2.at[pl.ds(c * 128, 128), lanes(k)], s_w, r_w, s, mate).start()
            return 0
        lax.fori_loop(0, Z * YH, wload, 0)
        kvload = pltpu.make_async_copy(kvflat, KVL, l_v)
        kvload.start()
        for load in loads:
            load.wait()

        tok = s * ROWS + lax.broadcasted_iota(jnp.int32, (1, ROWS), 1)
        place = (tok - openings(tok, doc)).astype(F32)
        freq = jnp.exp(lax.broadcasted_iota(jnp.int32, (HD // 2, 1), 0).astype(F32) * STEP)
        angle = freq * place
        COS[...] = jnp.cos(angle)
        SIN[...] = jnp.sin(angle)
        prompts = prow[...]
        for i in range(8):
            at = i * 256 + lax.broadcasted_iota(jnp.int32, (256, NP), 0)
            CM[pl.ds(i * 256, 256), :] = jnp.where(at == prompts, 1.0, 0.0).astype(BF16)
        near = lax.broadcasted_iota(jnp.int32, (PL, NP), 1) == (
            s * PL + lax.broadcasted_iota(jnp.int32, (PL, NP), 0))
        own_p = jnp.sum(jnp.where(near, prompts.astype(F32), 0.0), axis=1, keepdims=True).astype(jnp.int32)
        pick = jnp.where(lax.broadcasted_iota(jnp.int32, (PL, ROWS), 1) == own_p - s * ROWS,
                         1.0, 0.0).astype(BF16)
        lane = lax.broadcasted_iota(jnp.int32, (1, HD), 1)
        freq_l = jnp.exp(jnp.where(lane < 64, lane, lane - 64).astype(F32) * STEP)
        angle_p = (own_p - openings(own_p, doc)).astype(F32) * freq_l
        cos_p = jnp.cos(angle_p)
        sin_p = jnp.where(lane < 64, 1.0, -1.0) * jnp.sin(angle_p)
        T.update(kvload=kvload, pick=pick, cos_p=cos_p, sin_p=sin_p)

    def back(u):
        return u * T["cos_p"] + pltpu.roll(u, 64, 1) * T["sin_p"]

    flow.task("setup", after=[("Y", 0, 0)], work=setup, cost=1.0, rank=-1)

    def gain(zz):
        cols = pl.ds(pl.multiple_of(zz * 512, 512), 512)
        part = nt(W2[:, cols], H[:, cols])
        QP[0] = QP[0] + part[:128]
        QP[1] = QP[1] + part[128:]

    def gain_kv(zz):
        cols = pl.ds(pl.multiple_of(zz * 512, 512), 512)
        part = nt(KWF[:, cols], H[:, cols]).reshape(2, 2, 16, ROWS)
        KP[0] = KP[0] + part[:, 0]
        KP[1] = KP[1] + part[:, 1]

    kz_keys = [("kz", i) for i in range(Z - 1)]
    for key, zz in zip(kz_keys, zpeers):
        flow.arrival(key, KZ.at[zz], r_kz.at[zz])
    ysides = [(yh + e) % YH for e in range(1, YH)]

    def ky_go(e, yy):
        return lambda: w.send(KZ.at[:, yy // 2, yy % 2], KY.at[yh], s_ky.at[e], r_ky.at[yh], s, d.fid(z, yy, c))

    def kz_work():
        kzown.wait()
        KY[yh] = KZ[:, yh // 2, yh % 2]
    flow.task("kz0", sends=[("n", 8, key, lambda: None) for key in kz_keys], rank=-3)
    flow.task("kz", needs=kz_keys, work=kz_work,
              sends=[(("y+", "y-", "y+")[e], 16, ("ky", e), ky_go(e, yy)) for e, yy in enumerate(ysides)])
    for e, yy in enumerate(ysides):
        flow.arrival(("ky", e), KY.at[yy], r_ky.at[yy])
    sx = (1 - yl) * X + x
    kx_row = lambda dx, ep: (yl + ep) % YL * X + (x + dx) % X

    def ky_work():
        for zz in range(Z):
            for yy in range(YH):
                KW[s, :, pl.ds((zz * YH + yy) * 128, 128)] = KY[yy, zz]

    def kx_send(dx, ep, way):
        ex = 1 if way == "x+" else -1
        row = kx_row(dx, ep)
        slot = s_kx.at[used[1]]
        used[1] += 1
        return (way, 64, ("kx", (dx - ex) % X, ep), lambda: w.send(
            KW.at[row], KW.at[row], slot, r_kx.at[row], yl * X + (x + ex) % X, f))
    used.append(0)
    flow.task("ky", needs=[("ky", e) for e in range(YH - 1)], work=ky_work, cost=0.2,
              sends=[("y+", 64, ("kl",), lambda: w.send(KW.at[s], KW.at[s], s_kl, r_kl, sx, f)),
                     kx_send(0, 0, "x+"), kx_send(0, 0, "x-")])
    flow.arrival(("kl",), KW.at[sx], r_kl)
    flow.task("kl", needs=[("kl",)], sends=[kx_send(0, 1, "x+"), kx_send(0, 1, "x-")])
    for ep in range(YL):
        for dx in range(1, X):
            flow.arrival(("kx", dx, ep), KW.at[kx_row(dx, ep)], r_kx.at[kx_row(dx, ep)])
            sends = []
            if dx == 3 and ep == 0:
                sends = [kx_send(dx, ep, "x+")]
            if dx == 1 and ep == 1:
                sends = [kx_send(dx, ep, "x-")]
            flow.task(("kx", dx, ep), needs=[("kx", dx, ep)], sends=sends)

    def kwf_work():
        for i in range(X * YL):
            KWF[pl.ds(i * 8, 8), :] = KW[i]
    flow.task("kwf", after=["ky", "kl"] + [("kx", dx, ep) for dx in range(1, X) for ep in range(YL)],
              work=kwf_work, cost=0.2, rank=1)

    def wq_work():
        mine_w, other_w = W2.at[pl.ds(c * 128, 128)], W2.at[pl.ds(o * 128, 128)]
        pltpu.make_async_copy(mine_w, mine_w, l_w).wait()
        recv(other_w, r_w)
        w.make(other_w, other_w, s_w, r_w, s, mate).wait_send()
        hown.wait()
        QP[...] = jnp.zeros_like(QP)
        KP[...] = jnp.zeros_like(KP)
    flow.task("wq0", sends=[("n", 8, ("wq",), lambda: None)], rank=-3)
    flow.task("wq", after=["wq0", ("Y", 0, 2)], work=wq_work, cost=0.3, rank=1)
    for dz in range(Z):
        chunk_of = [(kind, dz, dy) for kind in "YZ" for dy in range(YH)]
        flow.task(("gkv", dz), after=chunk_of + ["wq", "kwf"], cost=0.15, rank=1,
                  work=functools.partial(lambda i: gain_kv((z + i) % Z), dz))
        flow.task(("gq", dz), after=chunk_of + ["wq"], cost=0.32, rank=2,
                  work=functools.partial(lambda i: gain((z + i) % Z), dz))
    flow.task("kvx", after=[("gkv", dz) for dz in range(Z)], rank=1,
              sends=[("m", 32, ("kr",), lambda: w.send(KP.at[o], KR, s_p, r_p, s, mate))])
    flow.task("qx", after=[("gq", dz) for dz in range(Z)], rank=1,
              sends=[("m", 128, ("qr",), lambda: w.send(QP.at[o], QR, s_q, r_q, s, mate))])

    def kblock(yy, ll, xx):
        return KVT.at[yy // 2, :, yy % 2, c, :, lanes(ll * X + xx, ROWS)]

    def kr_work():
        total = KP[c] + KR[...]
        kvb = total.astype(BF16)
        kf = kvb.astype(F32)
        b16 = pl.ds(pl.multiple_of((yh % 2) * 32 + c * 16, 16), 16)
        ck, sk = COS[b16, :], SIN[b16, :]
        iskey = yh < 2
        KB[0] = jnp.where(iskey, kf[0] * ck - kf[1] * sk, kf[0]).astype(BF16)
        KB[1] = jnp.where(iskey, kf[1] * ck + kf[0] * sk, kf[1]).astype(BF16)
        KVT[yh // 2, :, yh % 2, c, :, lanes(s, ROWS)] = KB[...]

    yrel = [(yh, yl)] + ypeers
    used.append(0)

    def x_send(dx, e, way):
        ex = 1 if way == "x+" else -1
        yy, ll = yrel[e]
        block = kblock(yy, ll, (x + dx) % X)
        src = KB if (dx, e) == (0, 0) else block
        slot = s_x.at[used[2]]
        used[2] += 1
        return (way, 16, ("x", (dx - ex) % X, e), lambda: w.send(
            src, block, slot, r_x.at[(x + dx) % X, yy, ll], yl * X + (x + ex) % X, f))

    def b_send(e):
        yy, ll = ypeers[e]
        return ("y+" if e < 4 else "y-", 16 * min(e + 1, 7 - e) / 4, ("b", 7 - e), lambda: w.send(
            KB, kblock(yh, yl, x), s_b.at[e], r_b.at[yh, yl], ll * X + x, d.fid(z, yy, c)))

    flow.arrival(("kr",), KR, r_p)
    flow.task("kr", needs=[("kr",)], work=kr_work, cost=0.2,
              sends=[b_send(e) for e in (3, 2, 4, 1, 5, 0, 6)] + [x_send(0, 0, "x+"), x_send(0, 0, "x-")])
    for e in range(1, YH * YL):
        yy, ll = yrel[e]
        flow.arrival(("b", e), kblock(yy, ll, x), r_b.at[yy, ll])
        flow.task(("b", e), needs=[("b", e)], sends=[x_send(0, e, "x+"), x_send(0, e, "x-")])
    for e in range(YH * YL):
        yy, ll = yrel[e]
        for dx in range(1, X):
            xx = (x + dx) % X
            flow.arrival(("x", dx, e), kblock(yy, ll, xx), r_x.at[xx, yy, ll])
            sends = []
            if dx == 3 and e % 2 == 0:
                sends = [x_send(dx, e, "x+")]
            if dx == 1 and e % 2 == 1:
                sends = [x_send(dx, e, "x-")]
            flow.task(("x", dx, e), needs=[("x", dx, e)], sends=sends)

    def c_send(dx, ep):
        col = (yl + ep) % YL * X + (x + dx) % X
        part = KVT.at[:, :, :, c, :, lanes(col, ROWS)]
        other = KVT.at[:, :, :, o, :, lanes(col, ROWS)]
        flow.arrival(("c", dx, ep), other, r_c.at[col])
        return ("m", 64, ("c", dx, ep), lambda: w.send(part, part, s_c.at[dx, ep], r_c.at[col], s, mate))
    for dx in range(X):
        for ep in range(YL):
            if dx:
                after = [("x", dx, e) for e in range(ep, 8, 2)]
            else:
                after = [("b", e) if e else "kr" for e in range(ep, 8, 2)]
            flow.task(("cs", dx, ep), after=after, sends=[c_send(dx, ep)])
            flow.task(("c", dx, ep), needs=[("c", dx, ep)])

    def q_work():
        q = QP[c] + QR[...]
        q1, q2 = q[:64], q[64:]
        co, si = COS[...], SIN[...]
        qt = jnp.concatenate([q1 * co - q2 * si, q2 * co + q1 * si], axis=0)
        QB[...] = jnp.transpose(qt).astype(BF16)
    flow.arrival(("qr",), QR, r_q)
    flow.task("q", needs=[("qr",)], work=q_work, cost=0.3, rank=1)
    flow.emit(recv)

    pick = T["pick"]
    kt = KVT[0].reshape(HD, SEQ)
    vt = KVT[1].reshape(HD, SEQ)
    CH = 64

    def chunk(i, _):
        rows = pl.ds(pl.multiple_of(i * CH, CH), CH)
        raw = nn(QB[rows, :], KVT[0].reshape(HD, SEQ)) * SCALE
        t = s * ROWS + i * CH + lax.broadcasted_iota(jnp.int32, (CH, 1), 0)
        start = openings(t, doc)
        j = lax.broadcasted_iota(jnp.int32, (CH, SEQ), 1)
        raw = jnp.where((j >= start) & (j <= t), raw, -jnp.inf)
        top = jnp.max(raw, axis=1, keepdims=True)
        e = jnp.exp(raw - top)
        probs = (e * (1.0 / jnp.sum(e, axis=1, keepdims=True))).astype(BF16)
        PB[rows, :] = probs
        att_out[rows, :] = nt(probs, KVT[1].reshape(HD, SEQ)).astype(BF16)
        return 0
    lax.fori_loop(0, ROWS // CH, chunk, 0)

    att = att_out[...]
    da = dat[...]
    rowdot = jnp.sum(da.astype(F32) * att.astype(F32), axis=1, keepdims=True)
    colp = nn(PB[...], CM[...])
    cv = nn(vt, CM[...]).astype(BF16)
    cds = (colp * (nn(da, cv) - rowdot)).astype(BF16)
    GP[0] = tn(cds, QB[...]).reshape(YL, X, PL, HD)
    GP[1] = tn(colp.astype(BF16), da).reshape(YL, X, PL, HD)
    for e in range(X):
        xx = (x + e) % X
        for i, (pp, ff) in enumerate(((c, f), (o, mate))):
            if e or i:
                w.send(GP.at[pp, :, xx], GX.at[x, c], s_d2.at[e, i], r_d2.at[x, c], yl * X + xx, ff)
    row_up = nn(pick, da)
    row_dot = jnp.sum(row_up * nn(pick, att), axis=1, keepdims=True)
    row_dp = nn(row_up.astype(BF16), vt)
    row_ds = (nn(pick, PB[...]) * (row_dp - row_dot)).astype(BF16)
    QG[c] = back(nt(row_ds, kt) * SCALE).astype(BF16)
    w.send(QG.at[c], QG.at[c], s_g, r_g, s, mate)
    recv(QG.at[o], r_g)
    both = jnp.concatenate([QG[0], QG[1]], axis=1)

    def spread(zz, _):
        part = nn(both, W2[:, pl.ds(pl.multiple_of(zz * 512, 512), 512)])
        for yy in range(YH):
            QF[yy, zz] = part[:, yy * 128:(yy + 1) * 128].astype(BF16)
        QS[zz] = jnp.zeros((PL, HD), F32)
        for yy in range(YH):
            QS[zz] = QS[zz] + jnp.where(yy == yh, part[:, yy * 128:(yy + 1) * 128], 0.0)
        return 0
    lax.fori_loop(0, Z, spread, 0)

    for e in range(1, YH):
        yy = (yh + e) % YH
        w.send(QF.at[yy], QY.at[yh], s_e2.at[e - 1], r_e2.at[yh], s, d.fid(z, yy, c))
    recv(GX.at[x, o], r_d2.at[x, o])
    acc = GP[c, :, x] + GX[x, o]
    for xx in xpeers:
        for cc in range(C):
            recv(GX.at[xx, cc], r_d2.at[xx, cc])
            acc = acc + GX[xx, cc]
    G2[...] = acc
    for e, (yy, ll) in enumerate(ypeers):
        w.send(G2.at[ll], GY.at[yh, yl], s_d3.at[e], r_d3.at[yh, yl], ll * X + x, d.fid(z, yy, c))
    for e in range(1, YH):
        yy = (yh + e) % YH
        recv(QY.at[yy], r_e2.at[yy])
        QS[...] = QS[...] + QY[yy].astype(F32)
    for e, zz in enumerate(zpeers):
        w.send(QS.at[zz], QZ.at[z], s_e3.at[e], r_e3.at[z], s, d.fid(zz, yh, c))
    acc = G2[yl]
    for yy, ll in ypeers:
        recv(GY.at[yy, ll], r_d3.at[yy, ll])
        acc = acc + GY[yy, ll]
    dkv = jnp.where(c == 0, back(acc * SCALE), acc).astype(BF16)
    DK[...] = dkv
    DKV[z, c] = dkv
    w.send(DK, DKV.at[z, c], s_d4.at[Z - 1, 0], r_d4.at[z, c], s, mate)
    for e, zz in enumerate(zpeers):
        for i, cc in enumerate((c, o)):
            w.send(DK, DKV.at[z, c], s_d4.at[e, i], r_d4.at[z, c], s, d.fid(zz, yh, cc))
    out = QS[z]
    for zz in zpeers:
        recv(QZ.at[zz], r_e3.at[zz])
        out = out + QZ[zz]
    T["kvload"].wait()
    recv(DKV.at[z, o], r_d4.at[z, o])
    for zz in zpeers:
        recv(DKV.at[zz, 0], r_d4.at[zz, 0])
        recv(DKV.at[zz, 1], r_d4.at[zz, 1])
    wide = jnp.concatenate([DKV[g, p] for g in range(Z) for p in range(2)], axis=1)
    pg_out[...] = out + nn(wide, KVL[...])
    w.finish()


def per_device(hidden, q_weight, kv_weight, d_attended, doc_lengths, prompt_pos):
    vm = pl.BlockSpec(memory_space=pltpu.VMEM)
    hbm = pl.BlockSpec(memory_space=pltpu.HBM)
    return pl.pallas_call(
        whole,
        out_shape=(jax.ShapeDtypeStruct((ROWS, HD), BF16),
                   jax.ShapeDtypeStruct((PL, HD), F32)),
        in_specs=[hbm] * 7,
        out_specs=(vm, vm),
        scratch_shapes=[
            VMEM((ROWS, 4096), BF16),
            VMEM((256, 4096), BF16),
            VMEM((Z, 2, 2, 8, FB), BF16),
            VMEM((YH, Z, 8, FB), BF16),
            VMEM((X * YL, 8, 4096), BF16),
            VMEM((64, 4096), BF16),
            VMEM((2, 2, 16, ROWS), F32),
            VMEM((2, 16, ROWS), F32),
            VMEM((2, 16, ROWS), BF16),
            VMEM((2, HD, ROWS), F32),
            VMEM((HD, ROWS), F32),
            VMEM((2, 2, 2, 2, 16, SEQ), BF16),
            VMEM((HD // 2, ROWS), F32),
            VMEM((HD // 2, ROWS), F32),
            VMEM((ROWS, HD), BF16),
            VMEM((ROWS, SEQ), BF16),
            VMEM((SEQ, NP), BF16),
            VMEM((SEQ, FB), BF16),
            VMEM((2, PL, HD), BF16),
            VMEM((2, YL, X, PL, HD), F32),
            VMEM((X, C, YL, PL, HD), F32),
            VMEM((YL, PL, HD), F32),
            VMEM((YH, YL, PL, HD), F32),
            VMEM((PL, HD), BF16),
            VMEM((Z, 2, PL, HD), BF16),
            VMEM((YH, Z, PL, HD), BF16),
            VMEM((YH, Z, PL, HD), BF16),
            VMEM((Z, PL, HD), F32),
            VMEM((Z, PL, HD), F32),
            VMEM((ROWS, FB), BF16),
            pltpu.SMEM((4,), jnp.int32),
            VMEM((1, NP), jnp.int32),
            DMA((76,)), DMA((2, 2, Z * YH)),
            DMA(()), DMA(()), DMA(()),
            DMA((Z - 1,)), DMA((Z,)), DMA((YH - 1,)), DMA((YH,)),
            DMA(()), DMA(()), DMA((6,)), DMA((X * YL,)),
            DMA(()), DMA(()),
            DMA((YH * YL - 1,)), DMA((YH, YL)),
            DMA((24,)), DMA((X, YH, YL)),
            DMA((X, YL)), DMA((X * YL,)),
            DMA(()), DMA(()), DMA(()), DMA((5,)),
            DMA(()), DMA(()),
            DMA((X, C)), DMA((X, C)),
            DMA((YH * YL - 1,)), DMA((YH, YL)),
            DMA((Z, 2)), DMA((Z, 2)),
            DMA((YH - 1,)), DMA((YH,)),
            DMA((Z - 1,)), DMA((Z,)),
        ],
        compiler_params=pltpu.CompilerParams(
            collective_id=0, has_side_effects=True, vmem_limit_bytes=67043328),
        name="whole",
    )(hidden, q_weight, kv_weight.reshape(Z, 2, 2, 2, 32, FB), kv_weight, d_attended,
      doc_lengths, prompt_pos.reshape(1, NP))


def solution(mesh):
    placed = (P("seq", "fsdp"), P("fsdp", None), P(None, "fsdp"), P("seq", "fsdp"), P(), P())
    return jax.shard_map(
        per_device,
        mesh=mesh,
        in_specs=placed,
        out_specs=(P("seq", "fsdp"), P("seq", "fsdp")),
        check_vma=False,
    )
```

```python
import functools
import math

import jax
import jax.numpy as jnp
from jax import lax
from jax.experimental import pallas as pl
from jax.experimental.pallas import tpu as pltpu
from jax.sharding import PartitionSpec as P

ROPE_THETA = 1000000.0
MESH = pl.DeviceIdType.MESH
F32 = jnp.float32
BF16 = jnp.bfloat16
VMEM = pltpu.VMEM
DMA = pltpu.SemaphoreType.DMA

X, YL, YH, Z, C = 4, 2, 4, 8, 2
ZROWS = 32
KINDS = "YZ" if ZROWS else "Y"
ROWS, HD, FB = 256, 128, 128


def nt(a, b):
    return lax.dot_general(a, b, (((1,), (1,)), ((), ())), preferred_element_type=F32)


class Place:
    def __init__(self):
        self.s = lax.axis_index("seq")
        self.f = lax.axis_index("fsdp")
        self.x = self.s % X
        self.yl = self.s // X
        self.z = self.f // (YH * C)
        self.yh = (self.f // C) % YH
        self.c = self.f % C
        self.o = 1 - self.c

    def fid(self, z, yh, c):
        return (z * YH + yh) * C + c


class Wires:
    def __init__(self):
        self.open = []

    def make(self, src, dst, ss, rs, seq, fs):
        return pltpu.make_async_remote_copy(
            src_ref=src, dst_ref=dst, send_sem=ss, recv_sem=rs,
            device_id={"seq": seq, "fsdp": fs}, device_id_type=MESH)

    def send(self, *args):
        copy = self.make(*args)
        copy.start()
        self.open.append(copy)

    def finish(self):
        for copy in self.open:
            copy.wait_send()


def nn(a, b):
    return lax.dot_general(a, b, (((1,), (0,)), ((), ())), preferred_element_type=F32)


def tn(a, b):
    return lax.dot_general(a, b, (((0,), (0,)), ((), ())), preferred_element_type=F32)


class Flow:
    RATE = {"z+": 45.0, "z-": 45.0, "y+": 22.0, "y-": 22.0, "x+": 45.0, "x-": 45.0, "m": 300.0, "n": 1e9}
    LAG = {"z+": 1.7, "z-": 1.7, "y+": 2.5, "y-": 2.5, "x+": 1.7, "x-": 1.7, "m": 0.9, "n": 4.0}

    def __init__(self):
        self.tasks = {}
        self.recvs = {}

    def arrival(self, key, ref, sem):
        self.recvs[key] = (ref, sem)

    def task(self, name, needs=(), after=(), sends=(), work=None, cost=0.05, rank=0):
        self.tasks[name] = (set(needs), set(after), list(sends), work, cost, rank)

    def order(self):
        at, done, free, now, out = {}, {}, {}, 0.0, []
        todo = list(self.tasks)
        while todo:
            best = None
            for i, name in enumerate(todo):
                needs, after, _, _, _, rank = self.tasks[name]
                if all(n in at for n in needs) and all(a in done for a in after):
                    ready = max([at[n] for n in needs] + [done[a] for a in after] + [0.0])
                    cand = (max(ready, now), rank, i)
                    if best is None or cand < best:
                        best = cand
            assert best is not None, todo
            name = todo.pop(best[2])
            _, _, sends, _, cost, _ = self.tasks[name]
            now = best[0] + cost
            done[name] = now
            for link, size, key, _ in sends:
                start = max(free.get(link, 0.0), now)
                free[link] = start + size / self.RATE[link]
                if key is not None:
                    at[key] = max(at.get(key, 0.0), free[link] + self.LAG[link])
            out.append(name)
        self.model = done
        return out

    def emit(self, recv):
        for name in self.order():
            needs, _, sends, work, _, _ = self.tasks[name]
            for key in sorted(needs, key=repr):
                recv(*self.recvs[key])
            if work is not None:
                work()
            for _, _, _, go in sends:
                go()


def lanes(k, n=128):
    return pl.ds(pl.multiple_of(k * n, n), n)


STEP = -2.0 * math.log(ROPE_THETA) / HD
SCALE = 1.0 / math.sqrt(HD)
SEQ, NP, PL = 2048, 128, 16


def openings(tokens, doc):
    end = jnp.int32(0)
    start = jnp.zeros_like(tokens)
    for i in range(4):
        end = end + doc[i]
        start = start + jnp.where(tokens >= end, doc[i], 0)
    return start


def whole(hid, qw, kvw, kvflat, dhbm, dochbm, phbm, att_out, pg_out,
          H, W2, KZ, KY, KW, KWF, KP, KR, KB, QP, QR, KVT, COS, SIN, QB, PB, CM, KVL,
          QG, GP, GX, G2, GY, DK, DKV, QF, QY, QS, QZ, dat, doc, prow,
          s_h, r_h, s_w, r_w, l_w, s_kz, r_kz, s_ky, r_ky, s_kl, r_kl, s_kx, r_kx,
          s_p, r_p, s_b, r_b, s_x, r_x, s_c, r_c, s_q, r_q, l_v, l_in,
          s_g, r_g, s_d2, r_d2, s_d3, r_d3, s_d4, r_d4, s_e2, r_e2, s_e3, r_e3):
    d = Place()
    s, f, x, yl, z, yh, c, o = d.s, d.f, d.x, d.yl, d.z, d.yh, d.c, d.o
    mate = d.fid(z, yh, o)
    zup, zdn = (z + 1) % Z, (z + Z - 1) % Z
    w = Wires()

    loads = [pltpu.make_async_copy(a, b, l_in.at[i]) for i, (a, b) in enumerate(
        ((dochbm, doc), (phbm, prow), (dhbm, dat)))]
    for load in loads:
        load.start()
    bar = pltpu.get_barrier_semaphore()
    peers = [(s, mate)]
    ypeers = []
    for e in range(1, YH * YL):
        y = (yh * YL + yl + e) % (YH * YL)
        ypeers.append((y // YL, y % YL))
        peers.append(((y % YL) * X + x, d.fid(z, y // YL, c)))
    xpeers = [(x + e) % X for e in range(1, X)]
    for xx in xpeers:
        peers.append((yl * X + xx, f))
        peers.append((yl * X + xx, mate))
    zpeers = [(z + e) % Z for e in range(1, Z)]
    for zz in zpeers:
        peers.append((s, d.fid(zz, yh, c)))
        peers.append((s, d.fid(zz, yh, o)))
    for ps, pf in peers:
        pl.semaphore_signal(bar, inc=1, device_id={"seq": ps, "fsdp": pf}, device_id_type=MESH)
    pl.semaphore_wait(bar, len(peers))

    def hblock(zz, yy):
        return H.at[:, lanes(zz * YH + yy)]

    def recv(ref, sem):
        w.make(ref, ref, s_q, sem, s, mate).wait_recv()

    def eighth(g):
        return kvw.at[g, :, s // 4, :, pl.ds(pl.multiple_of((s % 4) * 8, 8), 8), :]
    for e, zz in enumerate(zpeers):
        w.send(eighth(zz), KZ.at[z], s_kz.at[e], r_kz.at[z], s, d.fid(zz, yh, c))
    kzown = pltpu.make_async_copy(eighth(z), KZ.at[z], l_in.at[3])
    kzown.start()
    hown = pltpu.make_async_copy(hid, hblock(z, yh), l_in.at[4])
    hown.start()
    flow = Flow()
    used = [0]
    ny, nz = ROWS - ZROWS, ZROWS
    ROW = {"Y": {"F": (0, ny), "A": (0, ny // 2), "B": (ny // 2, ny // 2)},
           "Z": {"F": (ny, nz), "A": (ny, nz // 2), "B": (ny + nz // 2, nz // 2)}}

    def hpiece(kind, dz, dy, h):
        r0, n = ROW[kind][h]
        return H.at[pl.ds(r0, n), lanes((z + dz) % Z * YH + (yh + dy) % YH)]

    def hsem(kind, dz, dy, h):
        return r_h.at[0 if kind == "Y" else 1, 1 if h == "B" else 0, (z + dz) % Z * YH + (yh + dy) % YH]

    def hsend(kind, dz, dy, h, way):
        ez, ey = {"z+": (1, 0), "z-": (-1, 0), "y+": (0, 1), "y-": (0, -1)}[way]
        r0, n = ROW[kind][h]
        slot = s_h.at[used[0]]
        used[0] += 1
        src = hid.at[pl.ds(r0, n), :] if (dz, dy) == (0, 0) else hpiece(kind, dz, dy, h)

        def go():
            w.send(src, hpiece(kind, dz, dy, h), slot, hsem(kind, dz, dy, h),
                   s, d.fid((z + ez) % Z, (yh + ey) % YH, c))
        return (way, n / 4, (kind, (dz - ez) % Z, (dy - ey) % YH, h), go)

    def hidden_tasks():
        for kind in KINDS:
            for dz in range(Z):
                for dy in range(YH):
                    two = dy == 2 and (kind == "Z" or dz == 0) or dz == 4 and (kind == "Y" or dy == 0)
                    needs = [(kind, dz, dy, h) for h in ("AB" if two else "F")] if dz or dy else []
                    for key in needs:
                        flow.arrival(key, hpiece(*key), hsem(*key))
                    sends = []
                    if kind == "Y":
                        if dz == 0:
                            if dy == 0:
                                sends += [("y+", "F"), ("y-", "F")]
                            if dy == 3:
                                sends.append(("y+", "A"))
                            if dy == 1:
                                sends.append(("y-", "B"))
                            sends += [("z+", "F"), ("z-", "F")]
                        elif dz > 4:
                            sends.append(("z+", "A" if dz == 5 else "F"))
                        elif dz < 4:
                            sends.append(("z-", "B" if dz == 3 else "F"))
                    elif dy == 0:
                        if dz == 0:
                            sends += [("z+", "F"), ("z-", "F")]
                        elif dz > 4:
                            sends.append(("z+", "A" if dz == 5 else "F"))
                        elif dz < 4:
                            sends.append(("z-", "B" if dz == 3 else "F"))
                        if dz == 0:
                            sends += [("y+", "F"), ("y-", "F")]
                        else:
                            flow.task(("Zy", dz), after=[("Z", dz, 0), ("Y", 0, 1), ("Y", 0, 3)], rank=1,
                                      sends=[hsend(kind, dz, dy, "F", way) for way in ("y+", "y-")])
                    elif dy == 3:
                        sends.append(("y+", "A"))
                    elif dy == 1:
                        sends.append(("y-", "B"))
                    flow.task((kind, dz, dy), needs=needs,
                              sends=[hsend(kind, dz, dy, h, way) for way, h in sends],
                              rank=0 if dz or dy else (-2 if kind == "Z" else -1))
    hidden_tasks()

    T = {}

    def setup():
        def wload(k, _):
            pltpu.make_async_copy(qw.at[:, pl.ds(pl.multiple_of(k * 256 + c * 128, 128), 128)],
                                  W2.at[pl.ds(c * 128, 128), lanes(k)], l_w).start()
            w.make(qw.at[:, pl.ds(pl.multiple_of(k * 256 + o * 128, 128), 128)],
                   W2.at[pl.ds(c * 128, 128), lanes(k)], s_w, r_w, s, mate).start()
            return 0
        lax.fori_loop(0, Z * YH, wload, 0)
        kvload = pltpu.make_async_copy(kvflat, KVL, l_v)
        kvload.start()
        for load in loads:
            load.wait()

        tok = s * ROWS + lax.broadcasted_iota(jnp.int32, (1, ROWS), 1)
        place = (tok - openings(tok, doc)).astype(F32)
        freq = jnp.exp(lax.broadcasted_iota(jnp.int32, (HD // 2, 1), 0).astype(F32) * STEP)
        angle = freq * place
        COS[...] = jnp.cos(angle)
        SIN[...] = jnp.sin(angle)
        prompts = prow[...]
        for i in range(8):
            at = i * 256 + lax.broadcasted_iota(jnp.int32, (256, NP), 0)
            CM[pl.ds(i * 256, 256), :] = jnp.where(at == prompts, 1.0, 0.0).astype(BF16)
        near = lax.broadcasted_iota(jnp.int32, (PL, NP), 1) == (
            s * PL + lax.broadcasted_iota(jnp.int32, (PL, NP), 0))
        own_p = jnp.sum(jnp.where(near, prompts.astype(F32), 0.0), axis=1, keepdims=True).astype(jnp.int32)
        pick = jnp.where(lax.broadcasted_iota(jnp.int32, (PL, ROWS), 1) == own_p - s * ROWS,
                         1.0, 0.0).astype(BF16)
        lane = lax.broadcasted_iota(jnp.int32, (1, HD), 1)
        freq_l = jnp.exp(jnp.where(lane < 64, lane, lane - 64).astype(F32) * STEP)
        angle_p = (own_p - openings(own_p, doc)).astype(F32) * freq_l
        cos_p = jnp.cos(angle_p)
        sin_p = jnp.where(lane < 64, 1.0, -1.0) * jnp.sin(angle_p)
        T.update(kvload=kvload, pick=pick, cos_p=cos_p, sin_p=sin_p)

    def back(u):
        return u * T["cos_p"] + pltpu.roll(u, 64, 1) * T["sin_p"]

    flow.task("setup", after=[("Y", 0, 0)], work=setup, cost=1.0, rank=-1)

    def gain(zz):
        cols = pl.ds(pl.multiple_of(zz * 512, 512), 512)
        part = nt(W2[:, cols], H[:, cols])
        QP[0] = QP[0] + part[:128]
        QP[1] = QP[1] + part[128:]

    def gain_kv(zz):
        cols = pl.ds(pl.multiple_of(zz * 512, 512), 512)
        part = nt(KWF[:, cols], H[:, cols]).reshape(2, 2, 16, ROWS)
        KP[0] = KP[0] + part[:, 0]
        KP[1] = KP[1] + part[:, 1]

    kz_keys = [("kz", i) for i in range(Z - 1)]
    for key, zz in zip(kz_keys, zpeers):
        flow.arrival(key, KZ.at[zz], r_kz.at[zz])
    ysides = [(yh + e) % YH for e in range(1, YH)]

    def ky_go(e, yy):
        return lambda: w.send(KZ.at[:, yy // 2, yy % 2], KY.at[yh], s_ky.at[e], r_ky.at[yh], s, d.fid(z, yy, c))

    def kz_work():
        kzown.wait()
        KY[yh] = KZ[:, yh // 2, yh % 2]
    flow.task("kz0", sends=[("n", 8, key, lambda: None) for key in kz_keys], rank=-3)
    flow.task("kz", needs=kz_keys, work=kz_work,
              sends=[(("y+", "y-", "y+")[e], 16, ("ky", e), ky_go(e, yy)) for e, yy in enumerate(ysides)])
    for e, yy in enumerate(ysides):
        flow.arrival(("ky", e), KY.at[yy], r_ky.at[yy])
    sx = (1 - yl) * X + x
    kx_row = lambda dx, ep: (yl + ep) % YL * X + (x + dx) % X

    def ky_work():
        for zz in range(Z):
            for yy in range(YH):
                KW[s, :, pl.ds((zz * YH + yy) * 128, 128)] = KY[yy, zz]

    def kx_send(dx, ep, way):
        ex = 1 if way == "x+" else -1
        row = kx_row(dx, ep)
        slot = s_kx.at[used[1]]
        used[1] += 1
        return (way, 64, ("kx", (dx - ex) % X, ep), lambda: w.send(
            KW.at[row], KW.at[row], slot, r_kx.at[row], yl * X + (x + ex) % X, f))
    used.append(0)
    flow.task("ky", needs=[("ky", e) for e in range(YH - 1)], work=ky_work, cost=0.2,
              sends=[("y+", 64, ("kl",), lambda: w.send(KW.at[s], KW.at[s], s_kl, r_kl, sx, f)),
                     kx_send(0, 0, "x+"), kx_send(0, 0, "x-")])
    flow.arrival(("kl",), KW.at[sx], r_kl)
    flow.task("kl", needs=[("kl",)], sends=[kx_send(0, 1, "x+"), kx_send(0, 1, "x-")])
    for ep in range(YL):
        for dx in range(1, X):
            flow.arrival(("kx", dx, ep), KW.at[kx_row(dx, ep)], r_kx.at[kx_row(dx, ep)])
            sends = []
            if dx == 3 and ep == 0:
                sends = [kx_send(dx, ep, "x+")]
            if dx == 1 and ep == 1:
                sends = [kx_send(dx, ep, "x-")]
            flow.task(("kx", dx, ep), needs=[("kx", dx, ep)], sends=sends)

    def kwf_work():
        for i in range(X * YL):
            KWF[pl.ds(i * 8, 8), :] = KW[i]
    flow.task("kwf", after=["ky", "kl"] + [("kx", dx, ep) for dx in range(1, X) for ep in range(YL)],
              work=kwf_work, cost=0.2, rank=1)

    def wq_work():
        mine_w, other_w = W2.at[pl.ds(c * 128, 128)], W2.at[pl.ds(o * 128, 128)]
        pltpu.make_async_copy(mine_w, mine_w, l_w).wait()
        recv(other_w, r_w)
        w.make(other_w, other_w, s_w, r_w, s, mate).wait_send()
        hown.wait()
        QP[...] = jnp.zeros_like(QP)
        KP[...] = jnp.zeros_like(KP)
    flow.task("wq0", sends=[("n", 8, ("wq",), lambda: None)], rank=-3)
    flow.task("wq", after=["wq0", ("Y", 0, 2)], work=wq_work, cost=0.3, rank=1)
    for dz in range(Z):
        chunk_of = [(kind, dz, dy) for kind in KINDS for dy in range(YH)]
        flow.task(("gkv", dz), after=chunk_of + ["wq", "kwf"], cost=0.15, rank=1,
                  work=functools.partial(lambda i: gain_kv((z + i) % Z), dz))
        flow.task(("gq", dz), after=chunk_of + ["wq"], cost=0.32, rank=2,
                  work=functools.partial(lambda i: gain((z + i) % Z), dz))
    flow.task("kvx", after=[("gkv", dz) for dz in range(Z)], rank=1,
              sends=[("m", 32, ("kr",), lambda: w.send(KP.at[o], KR, s_p, r_p, s, mate))])
    flow.task("qx", after=[("gq", dz) for dz in range(Z)], rank=1,
              sends=[("m", 128, ("qr",), lambda: w.send(QP.at[o], QR, s_q, r_q, s, mate))])

    def kblock(yy, ll, xx):
        return KVT.at[yy // 2, :, yy % 2, c, :, lanes(ll * X + xx, ROWS)]

    def kr_work():
        total = KP[c] + KR[...]
        kvb = total.astype(BF16)
        kf = kvb.astype(F32)
        b16 = pl.ds(pl.multiple_of((yh % 2) * 32 + c * 16, 16), 16)
        ck, sk = COS[b16, :], SIN[b16, :]
        iskey = yh < 2
        KB[0] = jnp.where(iskey, kf[0] * ck - kf[1] * sk, kf[0]).astype(BF16)
        KB[1] = jnp.where(iskey, kf[1] * ck + kf[0] * sk, kf[1]).astype(BF16)
        KVT[yh // 2, :, yh % 2, c, :, lanes(s, ROWS)] = KB[...]

    yrel = [(yh, yl)] + ypeers
    used.append(0)

    def x_send(dx, e, way):
        ex = 1 if way == "x+" else -1
        yy, ll = yrel[e]
        block = kblock(yy, ll, (x + dx) % X)
        src = KB if (dx, e) == (0, 0) else block
        slot = s_x.at[used[2]]
        used[2] += 1
        return (way, 16, ("x", (dx - ex) % X, e), lambda: w.send(
            src, block, slot, r_x.at[(x + dx) % X, yy, ll], yl * X + (x + ex) % X, f))

    def b_send(e):
        yy, ll = ypeers[e]
        return ("y+" if e < 4 else "y-", 16 * min(e + 1, 7 - e) / 4, ("b", 7 - e), lambda: w.send(
            KB, kblock(yh, yl, x), s_b.at[e], r_b.at[yh, yl], ll * X + x, d.fid(z, yy, c)))

    flow.arrival(("kr",), KR, r_p)
    flow.task("kr", needs=[("kr",)], work=kr_work, cost=0.2,
              sends=[b_send(e) for e in (3, 2, 4, 1, 5, 0, 6)] + [x_send(0, 0, "x+"), x_send(0, 0, "x-")])
    for e in range(1, YH * YL):
        yy, ll = yrel[e]
        flow.arrival(("b", e), kblock(yy, ll, x), r_b.at[yy, ll])
        flow.task(("b", e), needs=[("b", e)], sends=[x_send(0, e, "x+"), x_send(0, e, "x-")])
    for e in range(YH * YL):
        yy, ll = yrel[e]
        for dx in range(1, X):
            xx = (x + dx) % X
            flow.arrival(("x", dx, e), kblock(yy, ll, xx), r_x.at[xx, yy, ll])
            sends = []
            if dx == 3 and e % 2 == 0:
                sends = [x_send(dx, e, "x+")]
            if dx == 1 and e % 2 == 1:
                sends = [x_send(dx, e, "x-")]
            flow.task(("x", dx, e), needs=[("x", dx, e)], sends=sends)

    def c_send(dx, ep):
        col = (yl + ep) % YL * X + (x + dx) % X
        part = KVT.at[:, :, :, c, :, lanes(col, ROWS)]
        other = KVT.at[:, :, :, o, :, lanes(col, ROWS)]
        flow.arrival(("c", dx, ep), other, r_c.at[col])
        return ("m", 64, ("c", dx, ep), lambda: w.send(part, part, s_c.at[dx, ep], r_c.at[col], s, mate))
    for dx in range(X):
        for ep in range(YL):
            if dx:
                after = [("x", dx, e) for e in range(ep, 8, 2)]
            else:
                after = [("b", e) if e else "kr" for e in range(ep, 8, 2)]
            flow.task(("cs", dx, ep), after=after, sends=[c_send(dx, ep)])
            flow.task(("c", dx, ep), needs=[("c", dx, ep)])

    def q_work():
        q = QP[c] + QR[...]
        q1, q2 = q[:64], q[64:]
        co, si = COS[...], SIN[...]
        qt = jnp.concatenate([q1 * co - q2 * si, q2 * co + q1 * si], axis=0)
        QB[...] = jnp.transpose(qt).astype(BF16)
    flow.arrival(("qr",), QR, r_q)
    flow.task("q", needs=[("qr",)], work=q_work, cost=0.3, rank=1)
    flow.emit(recv)

    pick = T["pick"]
    kt = KVT[0].reshape(HD, SEQ)
    vt = KVT[1].reshape(HD, SEQ)
    CH = 64

    def chunk(i, _):
        rows = pl.ds(pl.multiple_of(i * CH, CH), CH)
        raw = nn(QB[rows, :], KVT[0].reshape(HD, SEQ)) * SCALE
        t = s * ROWS + i * CH + lax.broadcasted_iota(jnp.int32, (CH, 1), 0)
        start = openings(t, doc)
        j = lax.broadcasted_iota(jnp.int32, (CH, SEQ), 1)
        raw = jnp.where((j >= start) & (j <= t), raw, -jnp.inf)
        top = jnp.max(raw, axis=1, keepdims=True)
        e = jnp.exp(raw - top)
        probs = (e * (1.0 / jnp.sum(e, axis=1, keepdims=True))).astype(BF16)
        PB[rows, :] = probs
        att_out[rows, :] = nt(probs, KVT[1].reshape(HD, SEQ)).astype(BF16)
        return 0
    lax.fori_loop(0, ROWS // CH, chunk, 0)

    att = att_out[...]
    da = dat[...]
    rowdot = jnp.sum(da.astype(F32) * att.astype(F32), axis=1, keepdims=True)
    colp = nn(PB[...], CM[...])
    cv = nn(vt, CM[...]).astype(BF16)
    cds = (colp * (nn(da, cv) - rowdot)).astype(BF16)
    GP[0] = tn(cds, QB[...]).reshape(YL, X, PL, HD)
    GP[1] = tn(colp.astype(BF16), da).reshape(YL, X, PL, HD)
    for e in range(X):
        xx = (x + e) % X
        for i, (pp, ff) in enumerate(((c, f), (o, mate))):
            if e or i:
                w.send(GP.at[pp, :, xx], GX.at[x, c], s_d2.at[e, i], r_d2.at[x, c], yl * X + xx, ff)
    row_up = nn(pick, da)
    row_dot = jnp.sum(row_up * nn(pick, att), axis=1, keepdims=True)
    row_dp = nn(row_up.astype(BF16), vt)
    row_ds = (nn(pick, PB[...]) * (row_dp - row_dot)).astype(BF16)
    QG[c] = back(nt(row_ds, kt) * SCALE).astype(BF16)
    w.send(QG.at[c], QG.at[c], s_g, r_g, s, mate)
    recv(QG.at[o], r_g)
    both = jnp.concatenate([QG[0], QG[1]], axis=1)

    for e in (4, 3, 5, 2, 6, 1, 7, 0):
        zz = (z + e) % Z
        part = nn(both, W2[:, pl.ds(pl.multiple_of(zz * 512, 512), 512)])
        for yy in range(YH):
            piece = part[:, yy * 128:(yy + 1) * 128]
            if e:
                QF[zz, yy] = piece.astype(BF16)
            else:
                QS[yy] = piece
        if e:
            w.send(QF.at[zz], QY.at[z], s_e2.at[e - 1], r_e2.at[z], s, d.fid(zz, yh, c))

    recv(GX.at[x, o], r_d2.at[x, o])
    acc = GP[c, :, x] + GX[x, o]
    for xx in xpeers:
        for cc in range(C):
            recv(GX.at[xx, cc], r_d2.at[xx, cc])
            acc = acc + GX[xx, cc]
    G2[...] = acc
    for e, (yy, ll) in enumerate(ypeers):
        w.send(G2.at[ll], GY.at[yh, yl], s_d3.at[e], r_d3.at[yh, yl], ll * X + x, d.fid(z, yy, c))
    acc = G2[yl]
    for yy, ll in ypeers:
        recv(GY.at[yy, ll], r_d3.at[yy, ll])
        acc = acc + GY[yy, ll]
    dkv = jnp.where(c == 0, back(acc * SCALE), acc).astype(BF16)
    DK[...] = dkv
    DKV[z, c] = dkv
    w.send(DK, DKV.at[z, c], s_d4.at[Z - 1, 0], r_d4.at[z, c], s, mate)
    for e, zz in enumerate(zpeers):
        for i, cc in enumerate((c, o)):
            w.send(DK, DKV.at[z, c], s_d4.at[e, i], r_d4.at[z, c], s, d.fid(zz, yh, cc))
    for zz in zpeers:
        recv(QY.at[zz], r_e2.at[zz])
        QS[...] = QS[...] + QY[zz].astype(F32)
    for e, yy in enumerate(ysides):
        w.send(QS.at[yy], QZ.at[yh], s_e3.at[e], r_e3.at[yh], s, d.fid(z, yy, c))
    T["kvload"].wait()
    recv(DKV.at[z, o], r_d4.at[z, o])
    for zz in zpeers:
        recv(DKV.at[zz, 0], r_d4.at[zz, 0])
        recv(DKV.at[zz, 1], r_d4.at[zz, 1])
    wide = jnp.concatenate([DKV[g, p] for g in range(Z) for p in range(2)], axis=1)
    out = QS[yh] + nn(wide, KVL[...])
    for yy in ysides:
        recv(QZ.at[yy], r_e3.at[yy])
        out = out + QZ[yy]
    pg_out[...] = out
    w.finish()


def per_device(hidden, q_weight, kv_weight, d_attended, doc_lengths, prompt_pos):
    vm = pl.BlockSpec(memory_space=pltpu.VMEM)
    hbm = pl.BlockSpec(memory_space=pltpu.HBM)
    return pl.pallas_call(
        whole,
        out_shape=(jax.ShapeDtypeStruct((ROWS, HD), BF16),
                   jax.ShapeDtypeStruct((PL, HD), F32)),
        in_specs=[hbm] * 7,
        out_specs=(vm, vm),
        scratch_shapes=[
            VMEM((ROWS, 4096), BF16),
            VMEM((256, 4096), BF16),
            VMEM((Z, 2, 2, 8, FB), BF16),
            VMEM((YH, Z, 8, FB), BF16),
            VMEM((X * YL, 8, 4096), BF16),
            VMEM((64, 4096), BF16),
            VMEM((2, 2, 16, ROWS), F32),
            VMEM((2, 16, ROWS), F32),
            VMEM((2, 16, ROWS), BF16),
            VMEM((2, HD, ROWS), F32),
            VMEM((HD, ROWS), F32),
            VMEM((2, 2, 2, 2, 16, SEQ), BF16),
            VMEM((HD // 2, ROWS), F32),
            VMEM((HD // 2, ROWS), F32),
            VMEM((ROWS, HD), BF16),
            VMEM((ROWS, SEQ), BF16),
            VMEM((SEQ, NP), BF16),
            VMEM((SEQ, FB), BF16),
            VMEM((2, PL, HD), BF16),
            VMEM((2, YL, X, PL, HD), F32),
            VMEM((X, C, YL, PL, HD), F32),
            VMEM((YL, PL, HD), F32),
            VMEM((YH, YL, PL, HD), F32),
            VMEM((PL, HD), BF16),
            VMEM((Z, 2, PL, HD), BF16),
            VMEM((Z, YH, PL, HD), BF16),
            VMEM((Z, YH, PL, HD), BF16),
            VMEM((YH, PL, HD), F32),
            VMEM((YH, PL, HD), F32),
            VMEM((ROWS, FB), BF16),
            pltpu.SMEM((4,), jnp.int32),
            VMEM((1, NP), jnp.int32),
            DMA((76,)), DMA((2, 2, Z * YH)),
            DMA(()), DMA(()), DMA(()),
            DMA((Z - 1,)), DMA((Z,)), DMA((YH - 1,)), DMA((YH,)),
            DMA(()), DMA(()), DMA((6,)), DMA((X * YL,)),
            DMA(()), DMA(()),
            DMA((YH * YL - 1,)), DMA((YH, YL)),
            DMA((24,)), DMA((X, YH, YL)),
            DMA((X, YL)), DMA((X * YL,)),
            DMA(()), DMA(()), DMA(()), DMA((5,)),
            DMA(()), DMA(()),
            DMA((X, C)), DMA((X, C)),
            DMA((YH * YL - 1,)), DMA((YH, YL)),
            DMA((Z, 2)), DMA((Z, 2)),
            DMA((Z - 1,)), DMA((Z,)),
            DMA((YH - 1,)), DMA((YH,)),
        ],
        compiler_params=pltpu.CompilerParams(
            collective_id=0, has_side_effects=True, vmem_limit_bytes=67043328),
        name="whole",
    )(hidden, q_weight, kv_weight.reshape(Z, 2, 2, 2, 32, FB), kv_weight, d_attended,
      doc_lengths, prompt_pos.reshape(1, NP))


def solution(mesh):
    placed = (P("seq", "fsdp"), P("fsdp", None), P(None, "fsdp"), P("seq", "fsdp"), P(), P())
    return jax.shard_map(
        per_device,
        mesh=mesh,
        in_specs=placed,
        out_specs=(P("seq", "fsdp"), P("seq", "fsdp")),
        check_vma=False,
    )
```

```python
import functools
import math

import jax
import jax.numpy as jnp
from jax import lax
from jax.experimental import pallas as pl
from jax.experimental.pallas import tpu as pltpu
from jax.sharding import PartitionSpec as P

ROPE_THETA = 1000000.0
MESH = pl.DeviceIdType.MESH
F32 = jnp.float32
BF16 = jnp.bfloat16
VMEM = pltpu.VMEM
DMA = pltpu.SemaphoreType.DMA

X, YL, YH, Z, C = 4, 2, 4, 8, 2
ZROWS = 32
KINDS = "YZ" if ZROWS else "Y"
ROWS, HD, FB = 256, 128, 128


def nt(a, b):
    return lax.dot_general(a, b, (((1,), (1,)), ((), ())), preferred_element_type=F32)


class Place:
    def __init__(self):
        self.s = lax.axis_index("seq")
        self.f = lax.axis_index("fsdp")
        self.x = self.s % X
        self.yl = self.s // X
        self.z = self.f // (YH * C)
        self.yh = (self.f // C) % YH
        self.c = self.f % C
        self.o = 1 - self.c

    def hop(self, z, yh):
        return (self.c + z + self.z + yh + self.yh) % 2

    def far(self, z, yh):
        return self.fid(z, yh, self.hop(z, yh))

    def fid(self, z, yh, c):
        return (z * YH + yh) * C + c


class Wires:
    def __init__(self):
        self.open = []

    def make(self, src, dst, ss, rs, seq, fs):
        return pltpu.make_async_remote_copy(
            src_ref=src, dst_ref=dst, send_sem=ss, recv_sem=rs,
            device_id={"seq": seq, "fsdp": fs}, device_id_type=MESH)

    def send(self, *args):
        copy = self.make(*args)
        copy.start()
        self.open.append(copy)

    def finish(self):
        for copy in self.open:
            copy.wait_send()


def nn(a, b):
    return lax.dot_general(a, b, (((1,), (0,)), ((), ())), preferred_element_type=F32)


def tn(a, b):
    return lax.dot_general(a, b, (((0,), (0,)), ((), ())), preferred_element_type=F32)


class Flow:
    RATE = {"z+": 45.0, "z-": 45.0, "y+": 22.0, "y-": 22.0, "x+": 45.0, "x-": 45.0, "x2": 22.0, "m": 300.0, "n": 1e9}
    LAG = {"z+": 2.1, "z-": 2.1, "y+": 2.9, "y-": 2.9, "x+": 2.1, "x-": 2.1, "x2": 2.8, "m": 1.0, "n": 4.0}

    def __init__(self):
        self.tasks = {}
        self.recvs = {}

    def arrival(self, key, ref, sem):
        self.recvs[key] = (ref, sem)

    def task(self, name, needs=(), after=(), sends=(), work=None, cost=0.05, rank=0):
        self.tasks[name] = (set(needs), set(after), list(sends), work, cost, rank)

    def order(self):
        at, done, free, now, out = {}, {}, {}, 0.0, []
        todo = list(self.tasks)
        while todo:
            best = None
            for i, name in enumerate(todo):
                needs, after, _, _, _, rank = self.tasks[name]
                if all(n in at for n in needs) and all(a in done for a in after):
                    ready = max([at[n] for n in needs] + [done[a] for a in after] + [0.0])
                    cand = (max(ready, now), rank, i)
                    if best is None or cand < best:
                        best = cand
            assert best is not None, todo
            name = todo.pop(best[2])
            _, _, sends, _, cost, _ = self.tasks[name]
            now = best[0] + cost
            done[name] = now
            for link, size, key, _ in sends:
                start = max(free.get(link, 0.0), now)
                free[link] = start + size / self.RATE[link]
                if key is not None:
                    at[key] = max(at.get(key, 0.0), free[link] + self.LAG[link])
            out.append(name)
        self.model = done
        return out

    def emit(self, recv):
        for name in self.order():
            needs, _, sends, work, _, _ = self.tasks[name]
            for key in sorted(needs, key=repr):
                recv(*self.recvs[key])
            if work is not None:
                work()
            for _, _, _, go in sends:
                go()


def lanes(k, n=128):
    return pl.ds(pl.multiple_of(k * n, n), n)


STEP = -2.0 * math.log(ROPE_THETA) / HD
SCALE = 1.0 / math.sqrt(HD)
SEQ, NP, PL = 2048, 128, 16


def openings(tokens, doc):
    end = jnp.int32(0)
    start = jnp.zeros_like(tokens)
    for i in range(4):
        end = end + doc[i]
        start = start + jnp.where(tokens >= end, doc[i], 0)
    return start


def whole(hid, qw, kvw, kvflat, dhbm, dochbm, phbm, att_out, pg_out,
          H, W2, KZ, KY, KW, KWF, KP, KR, KB, QP, QR, KVT, COS, SIN, QB, PB, CM, KVL,
          QG, GP, GX, G2, GY, DK, DKV, QF, QY, QS, QZ, dat, doc, prow,
          s_h, r_h, s_w, r_w, l_w, s_kz, r_kz, s_ky, r_ky, s_kl, r_kl, s_kx, r_kx,
          s_p, r_p, s_b, r_b, s_x, r_x, s_c, r_c, s_q, r_q, l_v, l_in,
          s_g, r_g, s_d2, r_d2, s_d3, r_d3, s_d4, r_d4, s_e2, r_e2, s_e3, r_e3):
    d = Place()
    s, f, x, yl, z, yh, c, o = d.s, d.f, d.x, d.yl, d.z, d.yh, d.c, d.o
    mate = d.fid(z, yh, o)
    zup, zdn = (z + 1) % Z, (z + Z - 1) % Z
    w = Wires()

    loads = [pltpu.make_async_copy(a, b, l_in.at[i]) for i, (a, b) in enumerate(
        ((dochbm, doc), (phbm, prow), (dhbm, dat)))]
    for load in loads:
        load.start()
    bar = pltpu.get_barrier_semaphore()
    peers = [(s, mate)]
    ypeers = []
    for e in range(1, YH * YL):
        y = (yh * YL + yl + e) % (YH * YL)
        ypeers.append((y // YL, y % YL))
        peers.append(((y % YL) * X + x, d.fid(z, y // YL, c)))
    for e in (1, 3):
        peers.append((s, d.fid(z, (yh + e) % YH, o)))
    xpeers = [(x + e) % X for e in range(1, X)]
    for xx in xpeers:
        peers.append((yl * X + xx, f))
        peers.append((yl * X + xx, mate))
    zpeers = [(z + e) % Z for e in range(1, Z)]
    for zz in zpeers:
        peers.append((s, d.fid(zz, yh, c)))
        peers.append((s, d.fid(zz, yh, o)))
    for ps, pf in peers:
        pl.semaphore_signal(bar, inc=1, device_id={"seq": ps, "fsdp": pf}, device_id_type=MESH)
    pl.semaphore_wait(bar, len(peers))

    def hblock(zz, yy):
        return H.at[:, lanes(zz * YH + yy)]

    def recv(ref, sem):
        w.make(ref, ref, s_q, sem, s, mate).wait_recv()

    def eighth(g):
        return kvw.at[g, :, s // 4, :, pl.ds(pl.multiple_of((s % 4) * 8, 8), 8), :]
    for e, zz in enumerate(zpeers):
        w.send(eighth(zz), KZ.at[z], s_kz.at[e], r_kz.at[z], s, d.far(zz, yh))
    kzown = pltpu.make_async_copy(eighth(z), KZ.at[z], l_in.at[3])
    kzown.start()
    hown = pltpu.make_async_copy(hid, hblock(z, yh), l_in.at[4])
    hown.start()
    flow = Flow()
    used = [0]
    ny = ROWS - ZROWS
    ROW = {"Y": {"A": (0, ny // 2), "B": (ny // 2, ny // 2)}, "Z": {"A": (ny, ZROWS // 2), "B": (ny + ZROWS // 2, ZROWS // 2)}}
    REACH = {"A": {"z+": 4, "z-": 3, "y+": 2, "y-": 1}, "B": {"z+": 3, "z-": 4, "y+": 1, "y-": 2}}
    STEPS = {"z+": (1, 0), "z-": (-1, 0), "y+": (0, 1), "y-": (0, -1)}

    def hpiece(kind, dz, dy, h):
        r0, n = ROW[kind][h]
        return H.at[pl.ds(r0, n), lanes((z + dz) % Z * YH + (yh + dy) % YH)]

    def hsem(kind, dz, dy, h):
        return r_h.at["YZ".index(kind), "AB".index(h), (z + dz) % Z * YH + (yh + dy) % YH]

    def hsend(kind, dz, dy, h, way):
        ez, ey = STEPS[way]
        r0, n = ROW[kind][h]
        slot = s_h.at[used[0]]
        used[0] += 1
        src = hid.at[pl.ds(r0, n), :] if (dz, dy) == (0, 0) else hpiece(kind, dz, dy, h)

        def go():
            w.send(src, hpiece(kind, dz, dy, h), slot, hsem(kind, dz, dy, h),
                   s, d.fid((z + ez) % Z, (yh + ey) % YH, o))
        return (way, n / 4, (kind, (dz - ez) % Z, (dy - ey) % YH, h), go)

    def onward(dist, size, h, up, down, first):
        if dist == 0:
            return [up, down] if first == up else [down, up]
        out = []
        back = size - dist
        if back < REACH[h][up] and dist > size // 2:
            out.append(up)
        if dist < REACH[h][down] and dist < size // 2:
            out.append(down)
        return out

    def hidden_tasks():
        for kind in KINDS:
            start = []
            for dz in range(Z):
                for dy in range(YH):
                    for h in "AB":
                        name = (kind, dz, dy, h)
                        needs = [name] if dz or dy else []
                        if needs:
                            flow.arrival(name, hpiece(*name), hsem(*name))
                        alongz = onward(dz, Z, h, "z+", "z-", "z+" if h == "A" else "z-")
                        alongy = onward(dy, YH, h, "y+", "y-", "y+" if h == "A" else "y-")
                        if kind == "Y":
                            ways = (alongy if dz == 0 else []) + alongz
                            if dz == 0 and dy == 0:
                                ways = [alongy[0], alongz[0], alongz[1], alongy[1]]
                        else:
                            ways = alongz if dy == 0 else alongy
                        if kind == "Z" and dy == 0:
                            after = [name] + ([("Y", 0, 1, "B"), ("Y", 0, 3, "A")] if dz else [])
                            flow.task(("Zy", dz, h), after=after, rank=1,
                                      sends=[hsend(kind, dz, dy, h, way) for way in alongy])
                        if dz or dy:
                            flow.task(name, needs=needs, sends=[hsend(kind, dz, dy, h, way) for way in ways])
                        else:
                            start += [(i, hsend(kind, dz, dy, h, way)) for i, way in enumerate(ways)]
            start.sort(key=lambda pair: (pair[0] + 1) // 2)
            flow.task((kind, 0, 0, "A"), sends=[send for _, send in start], rank=-1 if kind == "Z" else -2)
            flow.task((kind, 0, 0, "B"), after=[(kind, 0, 0, "A")], rank=-2)
    hidden_tasks()

    T = {}

    def setup():
        def wload(k, _):
            keep = d.hop(k // YH, k % YH)
            pltpu.make_async_copy(qw.at[:, lanes(k * 2 + keep)], W2.at[pl.ds(c * 128, 128), lanes(k)], l_w).start()
            w.make(qw.at[:, lanes(k * 2 + 1 - keep)], W2.at[pl.ds(c * 128, 128), lanes(k)], s_w, r_w, s, mate).start()
            return 0
        lax.fori_loop(0, Z * YH, wload, 0)
        kvload = pltpu.make_async_copy(kvflat, KVL, l_v)
        kvload.start()
        for load in loads:
            load.wait()

        tok = s * ROWS + lax.broadcasted_iota(jnp.int32, (1, ROWS), 1)
        place = (tok - openings(tok, doc)).astype(F32)
        freq = jnp.exp(lax.broadcasted_iota(jnp.int32, (HD // 2, 1), 0).astype(F32) * STEP)
        angle = freq * place
        COS[...] = jnp.cos(angle)
        SIN[...] = jnp.sin(angle)
        prompts = prow[...]
        for i in range(8):
            at = i * 256 + lax.broadcasted_iota(jnp.int32, (256, NP), 0)
            CM[pl.ds(i * 256, 256), :] = jnp.where(at == prompts, 1.0, 0.0).astype(BF16)
        near = lax.broadcasted_iota(jnp.int32, (PL, NP), 1) == (
            s * PL + lax.broadcasted_iota(jnp.int32, (PL, NP), 0))
        own_p = jnp.sum(jnp.where(near, prompts.astype(F32), 0.0), axis=1, keepdims=True).astype(jnp.int32)
        pick = jnp.where(lax.broadcasted_iota(jnp.int32, (PL, ROWS), 1) == own_p - s * ROWS,
                         1.0, 0.0).astype(BF16)
        lane = lax.broadcasted_iota(jnp.int32, (1, HD), 1)
        freq_l = jnp.exp(jnp.where(lane < 64, lane, lane - 64).astype(F32) * STEP)
        angle_p = (own_p - openings(own_p, doc)).astype(F32) * freq_l
        cos_p = jnp.cos(angle_p)
        sin_p = jnp.where(lane < 64, 1.0, -1.0) * jnp.sin(angle_p)
        T.update(kvload=kvload, pick=pick, cos_p=cos_p, sin_p=sin_p)

    def back(u):
        return u * T["cos_p"] + pltpu.roll(u, 64, 1) * T["sin_p"]

    flow.task("setup", after=[("Y", 0, 0, "A"), ("Y", 0, 0, "B")], work=setup, cost=1.0, rank=-1)

    def gain(zz):
        cols = pl.ds(pl.multiple_of(zz * 512, 512), 512)
        part = nt(W2[:, cols], H[:, cols])
        QP[0] = QP[0] + part[:128]
        QP[1] = QP[1] + part[128:]

    def gain_kv(zz):
        cols = pl.ds(pl.multiple_of(zz * 512, 512), 512)
        part = nt(KWF[:, cols], H[:, cols]).reshape(2, 2, 16, ROWS)
        KP[0] = KP[0] + part[:, 0]
        KP[1] = KP[1] + part[:, 1]

    kz_keys = [("kz", i) for i in range(Z - 1)]
    for key, zz in zip(kz_keys, zpeers):
        flow.arrival(key, KZ.at[zz], r_kz.at[zz])
    ysides = [(yh + e) % YH for e in range(1, YH)]

    def ky_go(e, yy):
        return lambda: w.send(KZ.at[:, yy // 2, yy % 2], KY.at[yh], s_ky.at[e], r_ky.at[yh], s, d.far(z, yy))

    def kz_work():
        kzown.wait()
        KY[yh] = KZ[:, yh // 2, yh % 2]
    flow.task("kz0", sends=[("n", 8, key, lambda: None) for key in kz_keys], rank=-3)
    flow.task("kz", needs=kz_keys, work=kz_work,
              sends=[(("y+", "y-", "y+")[e], 16, ("ky", e), ky_go(e, yy)) for e, yy in enumerate(ysides)])
    for e, yy in enumerate(ysides):
        flow.arrival(("ky", e), KY.at[yy], r_ky.at[yy])
    sx = (1 - yl) * X + x
    kx_row = lambda dx, ep: (yl + ep) % YL * X + (x + dx) % X

    def ky_work():
        for zz in range(Z):
            for yy in range(YH):
                KW[s, :, pl.ds((zz * YH + yy) * 128, 128)] = KY[yy, zz]

    def kx_send(dx, ep, way):
        ex = 1 if way == "x+" else -1
        row = kx_row(dx, ep)
        slot = s_kx.at[used[1]]
        used[1] += 1
        return (way, 64, ("kx", (dx - ex) % X, ep), lambda: w.send(
            KW.at[row], KW.at[row], slot, r_kx.at[row], yl * X + (x + ex) % X, f))
    used.append(0)
    flow.task("ky", needs=[("ky", e) for e in range(YH - 1)], work=ky_work, cost=0.2,
              sends=[("y+", 64, ("kl",), lambda: w.send(KW.at[s], KW.at[s], s_kl, r_kl, sx, f)),
                     kx_send(0, 0, "x+"), kx_send(0, 0, "x-")])
    flow.arrival(("kl",), KW.at[sx], r_kl)
    flow.task("kl", needs=[("kl",)], sends=[kx_send(0, 1, "x+"), kx_send(0, 1, "x-")])
    for ep in range(YL):
        for dx in range(1, X):
            flow.arrival(("kx", dx, ep), KW.at[kx_row(dx, ep)], r_kx.at[kx_row(dx, ep)])
            sends = []
            if dx == 3 and ep == 0:
                sends = [kx_send(dx, ep, "x+")]
            if dx == 1 and ep == 1:
                sends = [kx_send(dx, ep, "x-")]
            flow.task(("kx", dx, ep), needs=[("kx", dx, ep)], sends=sends)

    def kwf_work():
        for i in range(X * YL):
            KWF[pl.ds(i * 8, 8), :] = KW[i]
    flow.task("kwf", after=["ky", "kl"] + [("kx", dx, ep) for dx in range(1, X) for ep in range(YL)],
              work=kwf_work, cost=0.2, rank=1)

    def wq_work():
        mine_w, other_w = W2.at[pl.ds(c * 128, 128)], W2.at[pl.ds(o * 128, 128)]
        pltpu.make_async_copy(mine_w, mine_w, l_w).wait()
        recv(other_w, r_w)
        w.make(other_w, other_w, s_w, r_w, s, mate).wait_send()
        hown.wait()
        QP[...] = jnp.zeros_like(QP)
        KP[...] = jnp.zeros_like(KP)
    flow.task("wq0", sends=[("n", 8, ("wq",), lambda: None)], rank=-3)
    flow.task("wq", after=["wq0", ("Y", 0, 2, "A")], work=wq_work, cost=0.3, rank=1)
    for dz in range(Z):
        chunk_of = [(kind, dz, dy, h) for kind in KINDS for dy in range(YH) for h in "AB"]
        flow.task(("gkv", dz), after=chunk_of + ["wq", "kwf"], cost=0.15, rank=1,
                  work=functools.partial(lambda i: gain_kv((z + i) % Z), dz))
        flow.task(("gq", dz), after=chunk_of + ["wq"], cost=0.32, rank=2,
                  work=functools.partial(lambda i: gain((z + i) % Z), dz))
    flow.task("kvx", after=[("gkv", dz) for dz in range(Z)], rank=1,
              sends=[("m", 32, ("kr",), lambda: w.send(KP.at[o], KR, s_p, r_p, s, mate))])
    flow.task("qx", after=[("gq", dz) for dz in range(Z)], rank=1,
              sends=[("m", 128, ("qr",), lambda: w.send(QP.at[o], QR, s_q, r_q, s, mate))])

    def kblock(yy, ll, xx):
        return KVT.at[yy // 2, :, yy % 2, c, :, lanes(ll * X + xx, ROWS)]

    def kr_work():
        total = KP[c] + KR[...]
        kvb = total.astype(BF16)
        kf = kvb.astype(F32)
        b16 = pl.ds(pl.multiple_of((yh % 2) * 32 + c * 16, 16), 16)
        ck, sk = COS[b16, :], SIN[b16, :]
        iskey = yh < 2
        KB[0] = jnp.where(iskey, kf[0] * ck - kf[1] * sk, kf[0]).astype(BF16)
        KB[1] = jnp.where(iskey, kf[1] * ck + kf[0] * sk, kf[1]).astype(BF16)
        KVT[yh // 2, :, yh % 2, c, :, lanes(s, ROWS)] = KB[...]

    yrel = [(yh, yl)] + ypeers
    LATE = (3, 4)
    used.append(0)

    def x_send(dx, e, way):
        ex = {"x+": 1, "x-": -1, "x2": 2}[way]
        yy, ll = yrel[e]
        block = kblock(yy, ll, (x + dx) % X)
        src = KB if (dx, e) == (0, 0) else block
        slot = s_x.at[used[2]]
        used[2] += 1
        return (way, 16, ("x", (dx - ex) % X, e), lambda: w.send(
            src, block, slot, r_x.at[(x + dx) % X, yy, ll], yl * X + (x + ex) % X, f))

    def b_send(e):
        yy, ll = ypeers[e]
        return ("y+" if e < 4 else "y-", 16 * min(e + 1, 7 - e) / 4, ("b", 7 - e), lambda: w.send(
            KB, kblock(yh, yl, x), s_b.at[e], r_b.at[yh, yl], ll * X + x, d.fid(z, yy, c)))

    flow.arrival(("kr",), KR, r_p)
    flow.task("kr", needs=[("kr",)], work=kr_work, cost=0.2,
              sends=[b_send(e) for e in (3, 2, 4, 1, 5, 0, 6)] + [x_send(0, 0, "x+"), x_send(0, 0, "x-")])
    for e in range(1, YH * YL):
        yy, ll = yrel[e]
        flow.arrival(("b", e), kblock(yy, ll, x), r_b.at[yy, ll])
        flow.task(("b", e), needs=[("b", e)], sends=([x_send(0, e, "x2")] if e in LATE else []) + [
            x_send(0, e, "x+"), x_send(0, e, "x-")])
    for e in range(YH * YL):
        yy, ll = yrel[e]
        for dx in range(1, X):
            xx = (x + dx) % X
            flow.arrival(("x", dx, e), kblock(yy, ll, xx), r_x.at[xx, yy, ll])
            sends = []
            if dx == 3 and e % 2 == 0 and e not in LATE:
                sends = [x_send(dx, e, "x+")]
            if dx == 1 and e % 2 == 1 and e not in LATE:
                sends = [x_send(dx, e, "x-")]
            flow.task(("x", dx, e), needs=[("x", dx, e)], sends=sends)

    def c_send(dx, ep):
        col = (yl + ep) % YL * X + (x + dx) % X
        part = KVT.at[:, :, :, c, :, lanes(col, ROWS)]
        other = KVT.at[:, :, :, o, :, lanes(col, ROWS)]
        flow.arrival(("c", dx, ep), other, r_c.at[col])
        return ("m", 64, ("c", dx, ep), lambda: w.send(part, part, s_c.at[dx, ep], r_c.at[col], s, mate))
    for dx in range(X):
        for ep in range(YL):
            if dx:
                after = [("x", dx, e) for e in range(ep, 8, 2)]
            else:
                after = [("b", e) if e else "kr" for e in range(ep, 8, 2)]
            flow.task(("cs", dx, ep), after=after, sends=[c_send(dx, ep)])
            flow.task(("c", dx, ep), needs=[("c", dx, ep)])

    def q_work():
        q = QP[c] + QR[...]
        q1, q2 = q[:64], q[64:]
        co, si = COS[...], SIN[...]
        qt = jnp.concatenate([q1 * co - q2 * si, q2 * co + q1 * si], axis=0)
        QB[...] = jnp.transpose(qt).astype(BF16)
    flow.arrival(("qr",), QR, r_q)
    flow.task("q", needs=[("qr",)], work=q_work, cost=0.3, rank=1)
    flow.emit(recv)

    pick = T["pick"]
    kt = KVT[0].reshape(HD, SEQ)
    vt = KVT[1].reshape(HD, SEQ)
    CH = 64

    def chunk(i, _):
        rows = pl.ds(pl.multiple_of(i * CH, CH), CH)
        raw = nn(QB[rows, :], KVT[0].reshape(HD, SEQ)) * SCALE
        t = s * ROWS + i * CH + lax.broadcasted_iota(jnp.int32, (CH, 1), 0)
        start = openings(t, doc)
        j = lax.broadcasted_iota(jnp.int32, (CH, SEQ), 1)
        raw = jnp.where((j >= start) & (j <= t), raw, -jnp.inf)
        top = jnp.max(raw, axis=1, keepdims=True)
        e = jnp.exp(raw - top)
        probs = (e * (1.0 / jnp.sum(e, axis=1, keepdims=True))).astype(BF16)
        PB[rows, :] = probs
        att_out[rows, :] = nt(probs, KVT[1].reshape(HD, SEQ)).astype(BF16)
        return 0
    lax.fori_loop(0, ROWS // CH, chunk, 0)

    att = att_out[...]
    da = dat[...]
    rowdot = jnp.sum(da.astype(F32) * att.astype(F32), axis=1, keepdims=True)
    colp = nn(PB[...], CM[...])
    cv = nn(vt, CM[...]).astype(BF16)
    cds = (colp * (nn(da, cv) - rowdot)).astype(BF16)
    GP[0] = tn(cds, QB[...]).reshape(YL, X, PL, HD)
    GP[1] = tn(colp.astype(BF16), da).reshape(YL, X, PL, HD)
    for e in range(X):
        xx = (x + e) % X
        for i, (pp, ff) in enumerate(((c, f), (o, mate))):
            if e or i:
                w.send(GP.at[pp, :, xx], GX.at[x, c], s_d2.at[e, i], r_d2.at[x, c], yl * X + xx, ff)
    row_up = nn(pick, da)
    row_dot = jnp.sum(row_up * nn(pick, att), axis=1, keepdims=True)
    row_dp = nn(row_up.astype(BF16), vt)
    row_ds = (nn(pick, PB[...]) * (row_dp - row_dot)).astype(BF16)
    QG[c] = back(nt(row_ds, kt) * SCALE).astype(BF16)
    w.send(QG.at[c], QG.at[c], s_g, r_g, s, mate)
    recv(QG.at[o], r_g)
    both = jnp.concatenate([QG[0], QG[1]], axis=1)

    for e in (4, 3, 5, 2, 6, 1, 7, 0):
        zz = (z + e) % Z
        part = nn(both, W2[:, pl.ds(pl.multiple_of(zz * 512, 512), 512)])
        for yy in range(YH):
            piece = part[:, yy * 128:(yy + 1) * 128]
            if e:
                QF[zz, yy] = piece.astype(BF16)
            else:
                QS[yy] = piece
        if e:
            w.send(QF.at[zz], QY.at[z], s_e2.at[e - 1], r_e2.at[z], s, d.far(zz, yh))

    recv(GX.at[x, o], r_d2.at[x, o])
    acc = GP[c, :, x] + GX[x, o]
    for xx in xpeers:
        for cc in range(C):
            recv(GX.at[xx, cc], r_d2.at[xx, cc])
            acc = acc + GX[xx, cc]
    G2[...] = acc
    for e, (yy, ll) in enumerate(ypeers):
        w.send(G2.at[ll], GY.at[yh, yl], s_d3.at[e], r_d3.at[yh, yl], ll * X + x, d.fid(z, yy, c))
    acc = G2[yl]
    for yy, ll in ypeers:
        recv(GY.at[yy, ll], r_d3.at[yy, ll])
        acc = acc + GY[yy, ll]
    dkv = jnp.where(c == 0, back(acc * SCALE), acc).astype(BF16)
    DK[...] = dkv
    DKV[z, c] = dkv
    w.send(DK, DKV.at[z, c], s_d4.at[Z - 1, 0], r_d4.at[z, c], s, mate)
    for e, zz in enumerate(zpeers):
        for i, cc in enumerate((c, o)):
            w.send(DK, DKV.at[z, c], s_d4.at[e, i], r_d4.at[z, c], s, d.fid(zz, yh, cc))
    for zz in zpeers:
        recv(QY.at[zz], r_e2.at[zz])
        QS[...] = QS[...] + QY[zz].astype(F32)
    for e, yy in enumerate(ysides):
        w.send(QS.at[yy], QZ.at[yh], s_e3.at[e], r_e3.at[yh], s, d.far(z, yy))
    T["kvload"].wait()
    recv(DKV.at[z, o], r_d4.at[z, o])
    for zz in zpeers:
        recv(DKV.at[zz, 0], r_d4.at[zz, 0])
        recv(DKV.at[zz, 1], r_d4.at[zz, 1])
    wide = jnp.concatenate([DKV[g, p] for g in range(Z) for p in range(2)], axis=1)
    out = QS[yh] + nn(wide, KVL[...])
    for yy in ysides:
        recv(QZ.at[yy], r_e3.at[yy])
        out = out + QZ[yy]
    pg_out[...] = out
    w.finish()


def per_device(hidden, q_weight, kv_weight, d_attended, doc_lengths, prompt_pos):
    vm = pl.BlockSpec(memory_space=pltpu.VMEM)
    hbm = pl.BlockSpec(memory_space=pltpu.HBM)
    return pl.pallas_call(
        whole,
        out_shape=(jax.ShapeDtypeStruct((ROWS, HD), BF16),
                   jax.ShapeDtypeStruct((PL, HD), F32)),
        in_specs=[hbm] * 7,
        out_specs=(vm, vm),
        scratch_shapes=[
            VMEM((ROWS, 4096), BF16),
            VMEM((256, 4096), BF16),
            VMEM((Z, 2, 2, 8, FB), BF16),
            VMEM((YH, Z, 8, FB), BF16),
            VMEM((X * YL, 8, 4096), BF16),
            VMEM((64, 4096), BF16),
            VMEM((2, 2, 16, ROWS), F32),
            VMEM((2, 16, ROWS), F32),
            VMEM((2, 16, ROWS), BF16),
            VMEM((2, HD, ROWS), F32),
            VMEM((HD, ROWS), F32),
            VMEM((2, 2, 2, 2, 16, SEQ), BF16),
            VMEM((HD // 2, ROWS), F32),
            VMEM((HD // 2, ROWS), F32),
            VMEM((ROWS, HD), BF16),
            VMEM((ROWS, SEQ), BF16),
            VMEM((SEQ, NP), BF16),
            VMEM((SEQ, FB), BF16),
            VMEM((2, PL, HD), BF16),
            VMEM((2, YL, X, PL, HD), F32),
            VMEM((X, C, YL, PL, HD), F32),
            VMEM((YL, PL, HD), F32),
            VMEM((YH, YL, PL, HD), F32),
            VMEM((PL, HD), BF16),
            VMEM((Z, 2, PL, HD), BF16),
            VMEM((Z, YH, PL, HD), BF16),
            VMEM((Z, YH, PL, HD), BF16),
            VMEM((YH, PL, HD), F32),
            VMEM((YH, PL, HD), F32),
            VMEM((ROWS, FB), BF16),
            pltpu.SMEM((4,), jnp.int32),
            VMEM((1, NP), jnp.int32),
            DMA((124,)), DMA((2, 2, Z * YH)),
            DMA(()), DMA(()), DMA(()),
            DMA((Z - 1,)), DMA((Z,)), DMA((YH - 1,)), DMA((YH,)),
            DMA(()), DMA(()), DMA((6,)), DMA((X * YL,)),
            DMA(()), DMA(()),
            DMA((YH * YL - 1,)), DMA((YH, YL)),
            DMA((24,)), DMA((X, YH, YL)),
            DMA((X, YL)), DMA((X * YL,)),
            DMA(()), DMA(()), DMA(()), DMA((5,)),
            DMA(()), DMA(()),
            DMA((X, C)), DMA((X, C)),
            DMA((YH * YL - 1,)), DMA((YH, YL)),
            DMA((Z, 2)), DMA((Z, 2)),
            DMA((Z - 1,)), DMA((Z,)),
            DMA((YH - 1,)), DMA((YH,)),
        ],
        compiler_params=pltpu.CompilerParams(
            collective_id=0, has_side_effects=True, vmem_limit_bytes=67043328),
        name="whole",
    )(hidden, q_weight, kv_weight.reshape(Z, 2, 2, 2, 32, FB), kv_weight, d_attended,
      doc_lengths, prompt_pos.reshape(1, NP))


def solution(mesh):
    placed = (P("seq", "fsdp"), P("fsdp", None), P(None, "fsdp"), P("seq", "fsdp"), P(), P())
    return jax.shard_map(
        per_device,
        mesh=mesh,
        in_specs=placed,
        out_specs=(P("seq", "fsdp"), P("seq", "fsdp")),
        check_vma=False,
    )
```

```python
import functools
import math

import jax
import jax.numpy as jnp
from jax import lax
from jax.experimental import pallas as pl
from jax.experimental.pallas import tpu as pltpu
from jax.sharding import PartitionSpec as P

ROPE_THETA = 1000000.0
MESH = pl.DeviceIdType.MESH
F32 = jnp.float32
BF16 = jnp.bfloat16
VMEM = pltpu.VMEM
DMA = pltpu.SemaphoreType.DMA

X, YL, YH, Z, C = 4, 2, 4, 8, 2
ZROWS = 32
KINDS = "YZ" if ZROWS else "Y"
ROWS, HD, FB = 256, 128, 128


def nt(a, b):
    return lax.dot_general(a, b, (((1,), (1,)), ((), ())), preferred_element_type=F32)


class Place:
    def __init__(self):
        self.s = lax.axis_index("seq")
        self.f = lax.axis_index("fsdp")
        self.x = self.s % X
        self.yl = self.s // X
        self.z = self.f // (YH * C)
        self.yh = (self.f // C) % YH
        self.c = self.f % C
        self.o = 1 - self.c

    def hop(self, z, yh):
        return (self.c + z + self.z + yh + self.yh) % 2

    def far(self, z, yh):
        return self.fid(z, yh, self.hop(z, yh))

    def fid(self, z, yh, c):
        return (z * YH + yh) * C + c


class Wires:
    def __init__(self):
        self.open = []

    def make(self, src, dst, ss, rs, seq, fs):
        return pltpu.make_async_remote_copy(
            src_ref=src, dst_ref=dst, send_sem=ss, recv_sem=rs,
            device_id={"seq": seq, "fsdp": fs}, device_id_type=MESH)

    def send(self, *args):
        copy = self.make(*args)
        copy.start()
        self.open.append(copy)

    def finish(self):
        for copy in self.open:
            copy.wait_send()


def nn(a, b):
    return lax.dot_general(a, b, (((1,), (0,)), ((), ())), preferred_element_type=F32)


def tn(a, b):
    return lax.dot_general(a, b, (((0,), (0,)), ((), ())), preferred_element_type=F32)


LAZY = 1.5


class Flow:
    RATE = {"z+": 45.0, "z-": 45.0, "y+": 22.0, "y-": 22.0, "x+": 45.0, "x-": 45.0, "x2": 22.0, "m": 300.0, "n": 1e9}
    LAG = {"z+": 2.1, "z-": 2.1, "y+": 2.9, "y-": 2.9, "x+": 2.1, "x-": 2.1, "x2": 2.8, "m": 1.0, "n": 4.0}

    def __init__(self):
        self.tasks = {}
        self.recvs = {}

    def arrival(self, key, ref, sem):
        self.recvs[key] = (ref, sem)

    def task(self, name, needs=(), after=(), sends=(), work=None, cost=0.05, rank=0):
        self.tasks[name] = (set(needs), set(after), list(sends), work, cost, rank)

    def order(self):
        at, done, free, now, out = {}, {}, {}, 0.0, []
        todo = list(self.tasks)
        while todo:
            best = None
            for i, name in enumerate(todo):
                needs, after, sends, work, _, rank = self.tasks[name]
                if all(n in at for n in needs) and all(a in done for a in after):
                    ready = max([at[n] for n in needs] + [done[a] for a in after] + [0.0])
                    if needs and not sends and work is None:
                        ready += LAZY
                    cand = (max(ready, now), rank, i)
                    if best is None or cand < best:
                        best = cand
            assert best is not None, todo
            name = todo.pop(best[2])
            _, _, sends, _, cost, _ = self.tasks[name]
            now = best[0] + cost
            done[name] = now
            for link, size, key, _ in sends:
                start = max(free.get(link, 0.0), now)
                free[link] = start + size / self.RATE[link]
                if key is not None:
                    at[key] = max(at.get(key, 0.0), free[link] + self.LAG[link])
            out.append(name)
        self.model = done
        return out

    def emit(self, recv):
        for name in self.order():
            needs, _, sends, work, _, _ = self.tasks[name]
            for key in sorted(needs, key=repr):
                recv(*self.recvs[key])
            if work is not None:
                work()
            for _, _, _, go in sends:
                go()


def lanes(k, n=128):
    return pl.ds(pl.multiple_of(k * n, n), n)


STEP = -2.0 * math.log(ROPE_THETA) / HD
SCALE = 1.0 / math.sqrt(HD)
SEQ, NP, PL = 2048, 128, 16


def openings(tokens, doc):
    end = jnp.int32(0)
    start = jnp.zeros_like(tokens)
    for i in range(4):
        end = end + doc[i]
        start = start + jnp.where(tokens >= end, doc[i], 0)
    return start


def whole(hid, qw, kvw, kvflat, dhbm, dochbm, phbm, att_out, pg_out,
          H, W2, KZ, KY, KW, KWF, KP, KR, KB, QP, QR, KVT, COS, SIN, QB, PB, CM, KVL,
          QG, GP, GX, G2, GY, DK, DKV, QF, QY, QS, QZ, dat, doc, prow, BIAS,
          s_h, r_h, s_w, r_w, l_w, s_kz, r_kz, s_ky, r_ky, s_kl, r_kl, s_kx, r_kx,
          s_p, r_p, s_b, r_b, s_x, r_x, s_c, r_c, s_q, r_q, l_v, l_in,
          s_g, r_g, s_d2, r_d2, s_d3, r_d3, s_d4, r_d4, s_e2, r_e2, s_e3, r_e3):
    d = Place()
    s, f, x, yl, z, yh, c, o = d.s, d.f, d.x, d.yl, d.z, d.yh, d.c, d.o
    mate = d.fid(z, yh, o)
    zup, zdn = (z + 1) % Z, (z + Z - 1) % Z
    w = Wires()

    loads = [pltpu.make_async_copy(a, b, l_in.at[i]) for i, (a, b) in enumerate(
        ((dochbm, doc), (phbm, prow), (dhbm, dat)))]
    for load in loads:
        load.start()
    bar = pltpu.get_barrier_semaphore()
    peers = []
    ypeers = []
    for e in range(1, YH * YL):
        y = (yh * YL + yl + e) % (YH * YL)
        ypeers.append((y // YL, y % YL))
    xpeers = [(x + e) % X for e in range(1, X)]
    zpeers = [(z + e) % Z for e in range(1, Z)]
    for e in (4, 3, 5, 2, 6, 1, 7):
        for cc in (c, o):
            peers.append((s, d.fid((z + e) % Z, yh, cc)))
    for e in (4, 3, 5, 2, 6, 1, 7):
        y = (yh * YL + yl + e) % (YH * YL)
        peers.append(((y % YL) * X + x, d.fid(z, y // YL, c)))
    for e in (2, 1, 3):
        for ff in (f, mate):
            peers.append((yl * X + (x + e) % X, ff))
    for e in (1, 3):
        peers.append((s, d.fid(z, (yh + e) % YH, o)))
    peers.append((s, mate))
    for ps, pf in peers:
        pl.semaphore_signal(bar, inc=1, device_id={"seq": ps, "fsdp": pf}, device_id_type=MESH)
    pl.semaphore_wait(bar, len(peers))

    def hblock(zz, yy):
        return H.at[:, lanes(zz * YH + yy)]

    def recv(ref, sem):
        w.make(ref, ref, s_q, sem, s, mate).wait_recv()

    def eighth(g):
        return kvw.at[g, :, s // 4, :, pl.ds(pl.multiple_of((s % 4) * 8, 8), 8), :]
    for e, zz in enumerate(zpeers):
        w.send(eighth(zz), KZ.at[z], s_kz.at[e], r_kz.at[z], s, d.far(zz, yh))
    kzown = pltpu.make_async_copy(eighth(z), KZ.at[z], l_in.at[3])
    kzown.start()
    hown = pltpu.make_async_copy(hid, hblock(z, yh), l_in.at[4])
    hown.start()
    flow = Flow()
    used = [0]
    ny = ROWS - ZROWS
    ROW = {"Y": {"A": (0, ny // 2), "B": (ny // 2, ny // 2)}, "Z": {"A": (ny, ZROWS // 2), "B": (ny + ZROWS // 2, ZROWS // 2)}}
    REACH = {"A": {"z+": 4, "z-": 3, "y+": 2, "y-": 1}, "B": {"z+": 3, "z-": 4, "y+": 1, "y-": 2}}
    STEPS = {"z+": (1, 0), "z-": (-1, 0), "y+": (0, 1), "y-": (0, -1)}

    def hpiece(kind, dz, dy, h):
        r0, n = ROW[kind][h]
        return H.at[pl.ds(r0, n), lanes((z + dz) % Z * YH + (yh + dy) % YH)]

    def hsem(kind, dz, dy, h):
        return r_h.at["YZ".index(kind), "AB".index(h), (z + dz) % Z * YH + (yh + dy) % YH]

    def hsend(kind, dz, dy, h, way):
        ez, ey = STEPS[way]
        r0, n = ROW[kind][h]
        slot = s_h.at[used[0]]
        used[0] += 1
        src = hid.at[pl.ds(r0, n), :] if (dz, dy) == (0, 0) else hpiece(kind, dz, dy, h)

        def go():
            w.send(src, hpiece(kind, dz, dy, h), slot, hsem(kind, dz, dy, h),
                   s, d.fid((z + ez) % Z, (yh + ey) % YH, o))
        return (way, n / 4, (kind, (dz - ez) % Z, (dy - ey) % YH, h), go)

    def onward(dist, size, h, up, down, first):
        if dist == 0:
            return [up, down] if first == up else [down, up]
        out = []
        back = size - dist
        if back < REACH[h][up] and dist > size // 2:
            out.append(up)
        if dist < REACH[h][down] and dist < size // 2:
            out.append(down)
        return out

    def hidden_tasks():
        for kind in KINDS:
            start = []
            for dz in range(Z):
                for dy in range(YH):
                    for h in "AB":
                        name = (kind, dz, dy, h)
                        needs = [name] if dz or dy else []
                        if needs:
                            flow.arrival(name, hpiece(*name), hsem(*name))
                        alongz = onward(dz, Z, h, "z+", "z-", "z+" if h == "A" else "z-")
                        alongy = onward(dy, YH, h, "y+", "y-", "y+" if h == "A" else "y-")
                        if kind == "Y":
                            ways = (alongy if dz == 0 else []) + alongz
                            if dz == 0 and dy == 0:
                                ways = [alongy[0], alongz[0], alongz[1], alongy[1]]
                        else:
                            ways = alongz if dy == 0 else alongy
                        if kind == "Z" and dy == 0:
                            after = [name] + ([("Y", 0, 1, "B"), ("Y", 0, 3, "A")] if dz else [])
                            flow.task(("Zy", dz, h), after=after, rank=1,
                                      sends=[hsend(kind, dz, dy, h, way) for way in alongy])
                        if dz or dy:
                            flow.task(name, needs=needs, sends=[hsend(kind, dz, dy, h, way) for way in ways])
                        else:
                            start += [(i, hsend(kind, dz, dy, h, way)) for i, way in enumerate(ways)]
            start.sort(key=lambda pair: (pair[0] + 1) // 2)
            flow.task((kind, 0, 0, "A"), sends=[send for _, send in start], rank=-1 if kind == "Z" else -2)
            flow.task((kind, 0, 0, "B"), after=[(kind, 0, 0, "A")], rank=-2)
    hidden_tasks()

    T = {}

    def setup():
        def wload(k, _):
            keep = d.hop(k // YH, k % YH)
            pltpu.make_async_copy(qw.at[:, lanes(k * 2 + keep)], W2.at[pl.ds(c * 128, 128), lanes(k)], l_w).start()
            w.make(qw.at[:, lanes(k * 2 + 1 - keep)], W2.at[pl.ds(c * 128, 128), lanes(k)], s_w, r_w, s, mate).start()
            return 0
        lax.fori_loop(0, Z * YH, wload, 0)
        kvload = pltpu.make_async_copy(kvflat, KVL, l_v)
        kvload.start()
        for load in loads:
            load.wait()

        tok = s * ROWS + lax.broadcasted_iota(jnp.int32, (1, ROWS), 1)
        place = (tok - openings(tok, doc)).astype(F32)
        freq = jnp.exp(lax.broadcasted_iota(jnp.int32, (HD // 2, 1), 0).astype(F32) * STEP)
        angle = freq * place
        COS[...] = jnp.cos(angle)
        SIN[...] = jnp.sin(angle)
        prompts = prow[...]
        for i in range(8):
            at = i * 256 + lax.broadcasted_iota(jnp.int32, (256, NP), 0)
            CM[pl.ds(i * 256, 256), :] = jnp.where(at == prompts, 1.0, 0.0).astype(BF16)
        def mask(i, _):
            t = s * ROWS + i * 32 + lax.broadcasted_iota(jnp.int32, (32, 1), 0)
            j = lax.broadcasted_iota(jnp.int32, (32, SEQ), 1)
            BIAS[pl.ds(pl.multiple_of(i * 32, 32), 32), :] = jnp.where(
                (j >= openings(t, doc)) & (j <= t), 0.0, -jnp.inf)
            return 0
        lax.fori_loop(0, ROWS // 32, mask, 0)
        near = lax.broadcasted_iota(jnp.int32, (PL, NP), 1) == (
            s * PL + lax.broadcasted_iota(jnp.int32, (PL, NP), 0))
        own_p = jnp.sum(jnp.where(near, prompts.astype(F32), 0.0), axis=1, keepdims=True).astype(jnp.int32)
        pick = jnp.where(lax.broadcasted_iota(jnp.int32, (PL, ROWS), 1) == own_p - s * ROWS,
                         1.0, 0.0).astype(BF16)
        lane = lax.broadcasted_iota(jnp.int32, (1, HD), 1)
        freq_l = jnp.exp(jnp.where(lane < 64, lane, lane - 64).astype(F32) * STEP)
        angle_p = (own_p - openings(own_p, doc)).astype(F32) * freq_l
        cos_p = jnp.cos(angle_p)
        sin_p = jnp.where(lane < 64, 1.0, -1.0) * jnp.sin(angle_p)
        T.update(kvload=kvload, pick=pick, cos_p=cos_p, sin_p=sin_p)

    def back(u):
        return u * T["cos_p"] + pltpu.roll(u, 64, 1) * T["sin_p"]

    flow.task("setup", after=[("Y", 0, 0, "A"), ("Y", 0, 0, "B")], work=setup, cost=1.0, rank=-1)

    def gain(zz):
        cols = pl.ds(pl.multiple_of(zz * 512, 512), 512)
        part = nt(W2[:, cols], H[:, cols])
        QP[0] = QP[0] + part[:128]
        QP[1] = QP[1] + part[128:]

    def gain_kv(zz):
        cols = pl.ds(pl.multiple_of(zz * 512, 512), 512)
        part = nt(KWF[:, cols], H[:, cols]).reshape(2, 2, 16, ROWS)
        KP[0] = KP[0] + part[:, 0]
        KP[1] = KP[1] + part[:, 1]

    kz_keys = [("kz", i) for i in range(Z - 1)]
    for key, zz in zip(kz_keys, zpeers):
        flow.arrival(key, KZ.at[zz], r_kz.at[zz])
    ysides = [(yh + e) % YH for e in range(1, YH)]

    def ky_go(e, yy):
        return lambda: w.send(KZ.at[:, yy // 2, yy % 2], KY.at[yh], s_ky.at[e], r_ky.at[yh], s, d.far(z, yy))

    def kz_work():
        kzown.wait()
        KY[yh] = KZ[:, yh // 2, yh % 2]
    flow.task("kz0", sends=[("n", 8, key, lambda: None) for key in kz_keys], rank=-3)
    flow.task("kz", needs=kz_keys, work=kz_work,
              sends=[(("y+", "y-", "y+")[e], 16, ("ky", e), ky_go(e, yy)) for e, yy in enumerate(ysides)])
    for e, yy in enumerate(ysides):
        flow.arrival(("ky", e), KY.at[yy], r_ky.at[yy])
    sx = (1 - yl) * X + x
    kx_row = lambda dx, ep: (yl + ep) % YL * X + (x + dx) % X

    def ky_work():
        for zz in range(Z):
            for yy in range(YH):
                KW[s, :, pl.ds((zz * YH + yy) * 128, 128)] = KY[yy, zz]

    def kx_send(dx, ep, way):
        ex = 1 if way == "x+" else -1
        row = kx_row(dx, ep)
        slot = s_kx.at[used[1]]
        used[1] += 1
        return (way, 64, ("kx", (dx - ex) % X, ep), lambda: w.send(
            KW.at[row], KW.at[row], slot, r_kx.at[row], yl * X + (x + ex) % X, f))
    used.append(0)
    flow.task("ky", needs=[("ky", e) for e in range(YH - 1)], work=ky_work, cost=0.2,
              sends=[("y+", 64, ("kl",), lambda: w.send(KW.at[s], KW.at[s], s_kl, r_kl, sx, f)),
                     kx_send(0, 0, "x+"), kx_send(0, 0, "x-")])
    flow.arrival(("kl",), KW.at[sx], r_kl)
    flow.task("kl", needs=[("kl",)], sends=[kx_send(0, 1, "x+"), kx_send(0, 1, "x-")])
    for ep in range(YL):
        for dx in range(1, X):
            flow.arrival(("kx", dx, ep), KW.at[kx_row(dx, ep)], r_kx.at[kx_row(dx, ep)])
            sends = []
            if dx == 3 and ep == 0:
                sends = [kx_send(dx, ep, "x+")]
            if dx == 1 and ep == 1:
                sends = [kx_send(dx, ep, "x-")]
            flow.task(("kx", dx, ep), needs=[("kx", dx, ep)], sends=sends)

    def kwf_work():
        for i in range(X * YL):
            KWF[pl.ds(i * 8, 8), :] = KW[i]
    flow.task("kwf", after=["ky", "kl"] + [("kx", dx, ep) for dx in range(1, X) for ep in range(YL)],
              work=kwf_work, cost=0.2, rank=1)

    def wq_work():
        mine_w, other_w = W2.at[pl.ds(c * 128, 128)], W2.at[pl.ds(o * 128, 128)]
        pltpu.make_async_copy(mine_w, mine_w, l_w).wait()
        recv(other_w, r_w)
        w.make(other_w, other_w, s_w, r_w, s, mate).wait_send()
        hown.wait()
        QP[...] = jnp.zeros_like(QP)
        KP[...] = jnp.zeros_like(KP)
    flow.task("wq0", sends=[("n", 8, ("wq",), lambda: None)], rank=-3)
    flow.task("wq", after=["wq0", ("Y", 0, 2, "A")], work=wq_work, cost=0.3, rank=1)
    for dz in range(Z):
        chunk_of = [(kind, dz, dy, h) for kind in KINDS for dy in range(YH) for h in "AB"]
        flow.task(("gkv", dz), after=chunk_of + ["wq", "kwf"], cost=0.15, rank=1,
                  work=functools.partial(lambda i: gain_kv((z + i) % Z), dz))
        flow.task(("gq", dz), after=chunk_of + ["wq"], cost=0.32, rank=2,
                  work=functools.partial(lambda i: gain((z + i) % Z), dz))
    flow.task("kvx", after=[("gkv", dz) for dz in range(Z)], rank=1,
              sends=[("m", 32, ("kr",), lambda: w.send(KP.at[o], KR, s_p, r_p, s, mate))])
    flow.task("qx", after=[("gq", dz) for dz in range(Z)], rank=1,
              sends=[("m", 128, ("qr",), lambda: w.send(QP.at[o], QR, s_q, r_q, s, mate))])

    def kblock(yy, ll, xx):
        return KVT.at[yy // 2, :, yy % 2, c, :, lanes(ll * X + xx, ROWS)]

    def kr_work():
        total = KP[c] + KR[...]
        kvb = total.astype(BF16)
        kf = kvb.astype(F32)
        b16 = pl.ds(pl.multiple_of((yh % 2) * 32 + c * 16, 16), 16)
        ck, sk = COS[b16, :], SIN[b16, :]
        iskey = yh < 2
        KB[0] = jnp.where(iskey, kf[0] * ck - kf[1] * sk, kf[0]).astype(BF16)
        KB[1] = jnp.where(iskey, kf[1] * ck + kf[0] * sk, kf[1]).astype(BF16)
        KVT[yh // 2, :, yh % 2, c, :, lanes(s, ROWS)] = KB[...]

    yrel = [(yh, yl)] + ypeers
    LATE = (3, 4)
    used.append(0)

    def x_send(dx, e, way):
        ex = {"x+": 1, "x-": -1, "x2": 2}[way]
        yy, ll = yrel[e]
        block = kblock(yy, ll, (x + dx) % X)
        src = KB if (dx, e) == (0, 0) else block
        slot = s_x.at[used[2]]
        used[2] += 1
        return (way, 16, ("x", (dx - ex) % X, e), lambda: w.send(
            src, block, slot, r_x.at[(x + dx) % X, yy, ll], yl * X + (x + ex) % X, f))

    def b_send(e):
        yy, ll = ypeers[e]
        return ("y+" if e < 4 else "y-", 16 * min(e + 1, 7 - e) / 4, ("b", 7 - e), lambda: w.send(
            KB, kblock(yh, yl, x), s_b.at[e], r_b.at[yh, yl], ll * X + x, d.fid(z, yy, c)))

    flow.arrival(("kr",), KR, r_p)
    flow.task("kr", needs=[("kr",)], work=kr_work, cost=0.2,
              sends=[b_send(e) for e in (3, 2, 4, 1, 5, 0, 6)] + [x_send(0, 0, "x+"), x_send(0, 0, "x-")])
    for e in range(1, YH * YL):
        yy, ll = yrel[e]
        flow.arrival(("b", e), kblock(yy, ll, x), r_b.at[yy, ll])
        flow.task(("b", e), needs=[("b", e)], sends=([x_send(0, e, "x2")] if e in LATE else []) + [
            x_send(0, e, "x+"), x_send(0, e, "x-")])
    for e in range(YH * YL):
        yy, ll = yrel[e]
        for dx in range(1, X):
            xx = (x + dx) % X
            flow.arrival(("x", dx, e), kblock(yy, ll, xx), r_x.at[xx, yy, ll])
            sends = []
            if dx == 3 and e % 2 == 0 and e not in LATE:
                sends = [x_send(dx, e, "x+")]
            if dx == 1 and e % 2 == 1 and e not in LATE:
                sends = [x_send(dx, e, "x-")]
            flow.task(("x", dx, e), needs=[("x", dx, e)], sends=sends)

    def c_send(dx, ep):
        col = (yl + ep) % YL * X + (x + dx) % X
        part = KVT.at[:, :, :, c, :, lanes(col, ROWS)]
        other = KVT.at[:, :, :, o, :, lanes(col, ROWS)]
        flow.arrival(("c", dx, ep), other, r_c.at[col])
        return ("m", 64, ("c", dx, ep), lambda: w.send(part, part, s_c.at[dx, ep], r_c.at[col], s, mate))
    for dx in range(X):
        for ep in range(YL):
            if dx:
                after = [("x", dx, e) for e in range(ep, 8, 2)]
            else:
                after = [("b", e) if e else "kr" for e in range(ep, 8, 2)]
            flow.task(("cs", dx, ep), after=after, sends=[c_send(dx, ep)])
            flow.task(("c", dx, ep), needs=[("c", dx, ep)], after=[("cs", i, j) for i in range(X) for j in range(YL)])

    def q_work():
        q = QP[c] + QR[...]
        q1, q2 = q[:64], q[64:]
        co, si = COS[...], SIN[...]
        qt = jnp.concatenate([q1 * co - q2 * si, q2 * co + q1 * si], axis=0)
        QB[...] = jnp.transpose(qt).astype(BF16)
    flow.arrival(("qr",), QR, r_q)
    flow.task("q", needs=[("qr",)], work=q_work, cost=0.3, rank=1)
    flow.emit(recv)

    pick = T["pick"]
    kt = KVT[0].reshape(HD, SEQ)
    vt = KVT[1].reshape(HD, SEQ)
    CH = 64

    for i in range(ROWS // CH):
        rows = pl.ds(i * CH, CH)
        raw = nn(QB[rows, :], kt) * (SCALE * math.log2(math.e)) + BIAS[rows, :]
        e = jnp.exp2(raw - jnp.max(raw, axis=1, keepdims=True))
        probs = (e * (1.0 / jnp.sum(e, axis=1, keepdims=True))).astype(BF16)
        PB[rows, :] = probs
        att_out[rows, :] = nt(probs, vt).astype(BF16)

    att = att_out[...]
    da = dat[...]
    rowdot = jnp.sum(da.astype(F32) * att.astype(F32), axis=1, keepdims=True)
    colp = nn(PB[...], CM[...])
    cv = nn(vt, CM[...]).astype(BF16)
    cds = (colp * (nn(da, cv) - rowdot)).astype(BF16)
    GP[0] = tn(cds, QB[...]).reshape(YL, X, PL, HD)
    GP[1] = tn(colp.astype(BF16), da).reshape(YL, X, PL, HD)
    for e in range(X):
        xx = (x + e) % X
        for i, (pp, ff) in enumerate(((c, f), (o, mate))):
            if e or i:
                w.send(GP.at[pp, :, xx], GX.at[x, c], s_d2.at[e, i], r_d2.at[x, c], yl * X + xx, ff)
    row_up = nn(pick, da)
    row_dot = jnp.sum(row_up * nn(pick, att), axis=1, keepdims=True)
    row_dp = nn(row_up.astype(BF16), vt)
    row_ds = (nn(pick, PB[...]) * (row_dp - row_dot)).astype(BF16)
    QG[c] = back(nt(row_ds, kt) * SCALE).astype(BF16)
    w.send(QG.at[c], QG.at[c], s_g, r_g, s, mate)
    recv(QG.at[o], r_g)
    both = jnp.concatenate([QG[0], QG[1]], axis=1)

    for e in (4, 3, 5, 2, 6, 1, 7, 0):
        zz = (z + e) % Z
        part = nn(both, W2[:, pl.ds(pl.multiple_of(zz * 512, 512), 512)])
        for yy in range(YH):
            piece = part[:, yy * 128:(yy + 1) * 128]
            if e:
                QF[zz, yy] = piece.astype(BF16)
            else:
                QS[yy] = piece
        if e:
            w.send(QF.at[zz], QY.at[z], s_e2.at[e - 1], r_e2.at[z], s, d.far(zz, yh))

    recv(GX.at[x, o], r_d2.at[x, o])
    acc = GP[c, :, x] + GX[x, o]
    for xx in xpeers:
        for cc in range(C):
            recv(GX.at[xx, cc], r_d2.at[xx, cc])
            acc = acc + GX[xx, cc]
    G2[...] = acc
    for e, (yy, ll) in enumerate(ypeers):
        w.send(G2.at[ll], GY.at[yh, yl], s_d3.at[e], r_d3.at[yh, yl], ll * X + x, d.fid(z, yy, c))
    acc = G2[yl]
    for yy, ll in ypeers:
        recv(GY.at[yy, ll], r_d3.at[yy, ll])
        acc = acc + GY[yy, ll]
    dkv = jnp.where(c == 0, back(acc * SCALE), acc).astype(BF16)
    DK[...] = dkv
    DKV[z, c] = dkv
    w.send(DK, DKV.at[z, c], s_d4.at[Z - 1, 0], r_d4.at[z, c], s, mate)
    for e, zz in enumerate(zpeers):
        for i, cc in enumerate((c, o)):
            w.send(DK, DKV.at[z, c], s_d4.at[e, i], r_d4.at[z, c], s, d.fid(zz, yh, cc))
    for zz in zpeers:
        recv(QY.at[zz], r_e2.at[zz])
        QS[...] = QS[...] + QY[zz].astype(F32)
    for e, yy in enumerate(ysides):
        w.send(QS.at[yy], QZ.at[yh], s_e3.at[e], r_e3.at[yh], s, d.far(z, yy))
    T["kvload"].wait()
    recv(DKV.at[z, o], r_d4.at[z, o])
    for zz in zpeers:
        recv(DKV.at[zz, 0], r_d4.at[zz, 0])
        recv(DKV.at[zz, 1], r_d4.at[zz, 1])
    wide = jnp.concatenate([DKV[g, p] for g in range(Z) for p in range(2)], axis=1)
    out = QS[yh] + nn(wide, KVL[...])
    for yy in ysides:
        recv(QZ.at[yy], r_e3.at[yy])
        out = out + QZ[yy]
    pg_out[...] = out
    w.finish()


def per_device(hidden, q_weight, kv_weight, d_attended, doc_lengths, prompt_pos):
    vm = pl.BlockSpec(memory_space=pltpu.VMEM)
    hbm = pl.BlockSpec(memory_space=pltpu.HBM)
    return pl.pallas_call(
        whole,
        out_shape=(jax.ShapeDtypeStruct((ROWS, HD), BF16),
                   jax.ShapeDtypeStruct((PL, HD), F32)),
        in_specs=[hbm] * 7,
        out_specs=(vm, vm),
        scratch_shapes=[
            VMEM((ROWS, 4096), BF16),
            VMEM((256, 4096), BF16),
            VMEM((Z, 2, 2, 8, FB), BF16),
            VMEM((YH, Z, 8, FB), BF16),
            VMEM((X * YL, 8, 4096), BF16),
            VMEM((64, 4096), BF16),
            VMEM((2, 2, 16, ROWS), F32),
            VMEM((2, 16, ROWS), F32),
            VMEM((2, 16, ROWS), BF16),
            VMEM((2, HD, ROWS), F32),
            VMEM((HD, ROWS), F32),
            VMEM((2, 2, 2, 2, 16, SEQ), BF16),
            VMEM((HD // 2, ROWS), F32),
            VMEM((HD // 2, ROWS), F32),
            VMEM((ROWS, HD), BF16),
            VMEM((ROWS, SEQ), BF16),
            VMEM((SEQ, NP), BF16),
            VMEM((SEQ, FB), BF16),
            VMEM((2, PL, HD), BF16),
            VMEM((2, YL, X, PL, HD), F32),
            VMEM((X, C, YL, PL, HD), F32),
            VMEM((YL, PL, HD), F32),
            VMEM((YH, YL, PL, HD), F32),
            VMEM((PL, HD), BF16),
            VMEM((Z, 2, PL, HD), BF16),
            VMEM((Z, YH, PL, HD), BF16),
            VMEM((Z, YH, PL, HD), BF16),
            VMEM((YH, PL, HD), F32),
            VMEM((YH, PL, HD), F32),
            VMEM((ROWS, FB), BF16),
            pltpu.SMEM((4,), jnp.int32),
            VMEM((1, NP), jnp.int32),
            VMEM((ROWS, SEQ), F32),
            DMA((124,)), DMA((2, 2, Z * YH)),
            DMA(()), DMA(()), DMA(()),
            DMA((Z - 1,)), DMA((Z,)), DMA((YH - 1,)), DMA((YH,)),
            DMA(()), DMA(()), DMA((6,)), DMA((X * YL,)),
            DMA(()), DMA(()),
            DMA((YH * YL - 1,)), DMA((YH, YL)),
            DMA((24,)), DMA((X, YH, YL)),
            DMA((X, YL)), DMA((X * YL,)),
            DMA(()), DMA(()), DMA(()), DMA((5,)),
            DMA(()), DMA(()),
            DMA((X, C)), DMA((X, C)),
            DMA((YH * YL - 1,)), DMA((YH, YL)),
            DMA((Z, 2)), DMA((Z, 2)),
            DMA((Z - 1,)), DMA((Z,)),
            DMA((YH - 1,)), DMA((YH,)),
        ],
        compiler_params=pltpu.CompilerParams(
            collective_id=0, has_side_effects=True, vmem_limit_bytes=48 << 20),
        name="whole",
    )(*(pltpu.with_memory_space_constraint(a, pltpu.HBM) for a in (
        hidden, q_weight, kv_weight.reshape(Z, 2, 2, 2, 32, FB), kv_weight, d_attended,
        doc_lengths, prompt_pos.reshape(1, NP))))


def solution(mesh):
    placed = (P("seq", "fsdp"), P("fsdp", None), P(None, "fsdp"), P("seq", "fsdp"), P(), P())
    return jax.shard_map(
        per_device,
        mesh=mesh,
        in_specs=placed,
        out_specs=(P("seq", "fsdp"), P("seq", "fsdp")),
        check_vma=False,
    )
```

```python
import functools
import math

import jax
import jax.numpy as jnp
from jax import lax
from jax.experimental import pallas as pl
from jax.experimental.pallas import tpu as pltpu
from jax.sharding import PartitionSpec as P

ROPE_THETA = 1000000.0
MESH = pl.DeviceIdType.MESH
F32 = jnp.float32
BF16 = jnp.bfloat16
VMEM = pltpu.VMEM
DMA = pltpu.SemaphoreType.DMA

X, YL, YH, Z, C = 4, 2, 4, 8, 2
ZROWS = 32
KINDS = "YZ" if ZROWS else "Y"
ROWS, HD, FB = 256, 128, 128


def nt(a, b):
    return lax.dot_general(a, b, (((1,), (1,)), ((), ())), preferred_element_type=F32)


class Place:
    def __init__(self):
        self.s = lax.axis_index("seq")
        self.f = lax.axis_index("fsdp")
        self.x = self.s % X
        self.yl = self.s // X
        self.z = self.f // (YH * C)
        self.yh = (self.f // C) % YH
        self.c = self.f % C
        self.o = 1 - self.c

    def hop(self, z, yh):
        return (self.c + z + self.z + yh + self.yh) % 2

    def far(self, z, yh):
        return self.fid(z, yh, self.hop(z, yh))

    def fid(self, z, yh, c):
        return (z * YH + yh) * C + c


class Wires:
    def __init__(self):
        self.open = []

    def make(self, src, dst, ss, rs, seq, fs):
        return pltpu.make_async_remote_copy(
            src_ref=src, dst_ref=dst, send_sem=ss, recv_sem=rs,
            device_id={"seq": seq, "fsdp": fs}, device_id_type=MESH)

    def send(self, *args):
        copy = self.make(*args)
        copy.start()
        self.open.append(copy)

    def finish(self):
        for copy in self.open:
            copy.wait_send()


def nn(a, b):
    return lax.dot_general(a, b, (((1,), (0,)), ((), ())), preferred_element_type=F32)


def tn(a, b):
    return lax.dot_general(a, b, (((0,), (0,)), ((), ())), preferred_element_type=F32)


LAZY = 1.5


class Flow:
    RATE = {"z+": 45.0, "z-": 45.0, "y+": 22.0, "y-": 22.0, "x+": 45.0, "x-": 45.0, "x2": 22.0, "m": 300.0, "n": 1e9}
    LAG = {"z+": 2.1, "z-": 2.1, "y+": 2.9, "y-": 2.9, "x+": 2.1, "x-": 2.1, "x2": 2.8, "m": 1.0, "n": 4.0}

    def __init__(self):
        self.tasks = {}
        self.recvs = {}

    def arrival(self, key, ref, sem):
        self.recvs[key] = (ref, sem)

    def task(self, name, needs=(), after=(), sends=(), work=None, cost=0.05, rank=0):
        self.tasks[name] = (set(needs), set(after), list(sends), work, cost, rank)

    def order(self):
        at, done, free, now, out = {}, {}, {}, 0.0, []
        todo = list(self.tasks)
        while todo:
            best = None
            for i, name in enumerate(todo):
                needs, after, sends, work, _, rank = self.tasks[name]
                if all(n in at for n in needs) and all(a in done for a in after):
                    ready = max([at[n] for n in needs] + [done[a] for a in after] + [0.0])
                    if needs and not sends and work is None:
                        ready += LAZY
                    cand = (max(ready, now), rank, i)
                    if best is None or cand < best:
                        best = cand
            assert best is not None, todo
            name = todo.pop(best[2])
            _, _, sends, _, cost, _ = self.tasks[name]
            now = best[0] + cost
            done[name] = now
            for link, size, key, _ in sends:
                start = max(free.get(link, 0.0), now)
                free[link] = start + size / self.RATE[link]
                if key is not None:
                    lag = self.LAG[link] if key[0] != "b" else 1.5 + 0.8 * min(key[1], 8 - key[1])
                    at[key] = max(at.get(key, 0.0), free[link] + lag)
            out.append(name)
        self.model = done
        return out

    def emit(self, recv):
        for name in self.order():
            needs, _, sends, work, _, _ = self.tasks[name]
            for key in sorted(needs, key=repr):
                recv(*self.recvs[key])
            if work is not None:
                work()
            for _, _, _, go in sends:
                go()


def lanes(k, n=128):
    return pl.ds(pl.multiple_of(k * n, n), n)


STEP = -2.0 * math.log(ROPE_THETA) / HD
SCALE = 1.0 / math.sqrt(HD)
SEQ, NP, PL = 2048, 128, 16


def openings(tokens, doc):
    end = jnp.int32(0)
    start = jnp.zeros_like(tokens)
    for i in range(4):
        end = end + doc[i]
        start = start + jnp.where(tokens >= end, doc[i], 0)
    return start


def whole(hid, qw, kvw, kvflat, dhbm, dochbm, phbm, att_out, pg_out,
          H, W2, KZ, KY, KW, KWF, KP, KR, KB, QP, QR, KVT, COS, SIN, QB, PB, CM, KVL,
          QG, GP, GX, G2, GY, DK, DKV, QF, QY, QS, QZ, dat, doc, prow, BIAS,
          s_h, r_h, s_w, r_w, l_w, s_kz, r_kz, s_ky, r_ky, s_kl, r_kl, s_kx, r_kx,
          s_p, r_p, s_b, r_b, s_x, r_x, s_c, r_c, s_q, r_q, l_v, l_in,
          s_g, r_g, s_d2, r_d2, s_d3, r_d3, s_d4, r_d4, s_e2, r_e2, s_e3, r_e3):
    d = Place()
    s, f, x, yl, z, yh, c, o = d.s, d.f, d.x, d.yl, d.z, d.yh, d.c, d.o
    mate = d.fid(z, yh, o)
    zup, zdn = (z + 1) % Z, (z + Z - 1) % Z
    w = Wires()

    loads = [pltpu.make_async_copy(a, b, l_in.at[i]) for i, (a, b) in enumerate(
        ((dochbm, doc), (phbm, prow), (dhbm, dat)))]
    for load in loads:
        load.start()
    bar = pltpu.get_barrier_semaphore()
    peers = []
    ypeers = []
    for e in range(1, YH * YL):
        y = (yh * YL + yl + e) % (YH * YL)
        ypeers.append((y // YL, y % YL))
    xpeers = [(x + e) % X for e in range(1, X)]
    zpeers = [(z + e) % Z for e in range(1, Z)]
    for e in (4, 3, 5, 2, 6, 1, 7):
        for cc in (c, o):
            peers.append((s, d.fid((z + e) % Z, yh, cc)))
    for e in (4, 3, 5, 2, 6, 1, 7):
        y = (yh * YL + yl + e) % (YH * YL)
        peers.append(((y % YL) * X + x, d.fid(z, y // YL, c)))
        if e % 2:
            peers.append(((y % YL) * X + x, d.fid(z, y // YL, o)))
    for e in (2, 1, 3):
        for ff in (f, mate):
            peers.append((yl * X + (x + e) % X, ff))
    for e in (1, 3):
        peers.append((s, d.fid(z, (yh + e) % YH, o)))
    peers.append((s, mate))
    for ps, pf in peers:
        pl.semaphore_signal(bar, inc=1, device_id={"seq": ps, "fsdp": pf}, device_id_type=MESH)
    pl.semaphore_wait(bar, len(peers))

    def hblock(zz, yy):
        return H.at[:, lanes(zz * YH + yy)]

    def recv(ref, sem):
        w.make(ref, ref, s_q, sem, s, mate).wait_recv()

    def eighth(g):
        return kvw.at[g, :, s // 4, :, pl.ds(pl.multiple_of((s % 4) * 8, 8), 8), :]
    for e, zz in enumerate(zpeers):
        w.send(eighth(zz), KZ.at[z], s_kz.at[e], r_kz.at[z], s, d.far(zz, yh))
    kzown = pltpu.make_async_copy(eighth(z), KZ.at[z], l_in.at[3])
    kzown.start()
    hown = pltpu.make_async_copy(hid, hblock(z, yh), l_in.at[4])
    hown.start()
    flow = Flow()
    used = [0]
    ny = ROWS - ZROWS
    ROW = {"Y": {"A": (0, ny // 2), "B": (ny // 2, ny // 2)}, "Z": {"A": (ny, ZROWS // 2), "B": (ny + ZROWS // 2, ZROWS // 2)}}
    REACH = {"A": {"z+": 4, "z-": 3, "y+": 2, "y-": 1}, "B": {"z+": 3, "z-": 4, "y+": 1, "y-": 2}}
    STEPS = {"z+": (1, 0), "z-": (-1, 0), "y+": (0, 1), "y-": (0, -1)}

    def hpiece(kind, dz, dy, h):
        r0, n = ROW[kind][h]
        return H.at[pl.ds(r0, n), lanes((z + dz) % Z * YH + (yh + dy) % YH)]

    def hsem(kind, dz, dy, h):
        return r_h.at["YZ".index(kind), "AB".index(h), (z + dz) % Z * YH + (yh + dy) % YH]

    def hsend(kind, dz, dy, h, way):
        ez, ey = STEPS[way]
        r0, n = ROW[kind][h]
        slot = s_h.at[used[0]]
        used[0] += 1
        src = hid.at[pl.ds(r0, n), :] if (dz, dy) == (0, 0) else hpiece(kind, dz, dy, h)

        def go():
            w.send(src, hpiece(kind, dz, dy, h), slot, hsem(kind, dz, dy, h),
                   s, d.fid((z + ez) % Z, (yh + ey) % YH, o))
        return (way, n / 4, (kind, (dz - ez) % Z, (dy - ey) % YH, h), go)

    def onward(dist, size, h, up, down, first):
        if dist == 0:
            return [up, down] if first == up else [down, up]
        out = []
        back = size - dist
        if back < REACH[h][up] and dist > size // 2:
            out.append(up)
        if dist < REACH[h][down] and dist < size // 2:
            out.append(down)
        return out

    def hidden_tasks():
        for kind in KINDS:
            start = []
            for dz in range(Z):
                for dy in range(YH):
                    for h in "AB":
                        name = (kind, dz, dy, h)
                        needs = [name] if dz or dy else []
                        if needs:
                            flow.arrival(name, hpiece(*name), hsem(*name))
                        alongz = onward(dz, Z, h, "z+", "z-", "z+" if h == "A" else "z-")
                        alongy = onward(dy, YH, h, "y+", "y-", "y+" if h == "A" else "y-")
                        if kind == "Y":
                            ways = (alongy if dz == 0 else []) + alongz
                            if dz == 0 and dy == 0:
                                ways = [alongy[0], alongz[0], alongz[1], alongy[1]]
                        else:
                            ways = alongz if dy == 0 else alongy
                        if kind == "Z" and dy == 0:
                            after = [name] + ([("Y", 0, 1, "B"), ("Y", 0, 3, "A")] if dz else [])
                            flow.task(("Zy", dz, h), after=after, rank=1,
                                      sends=[hsend(kind, dz, dy, h, way) for way in alongy])
                        if dz or dy:
                            flow.task(name, needs=needs, sends=[hsend(kind, dz, dy, h, way) for way in ways])
                        else:
                            start += [(i, hsend(kind, dz, dy, h, way)) for i, way in enumerate(ways)]
            start.sort(key=lambda pair: (pair[0] + 1) // 2)
            flow.task((kind, 0, 0, "A"), sends=[send for _, send in start], rank=-1 if kind == "Z" else -2)
            flow.task((kind, 0, 0, "B"), after=[(kind, 0, 0, "A")], rank=-2)
    hidden_tasks()

    T = {}

    def setup():
        def wload(k, _):
            keep = d.hop(k // YH, k % YH)
            pltpu.make_async_copy(qw.at[:, lanes(k * 2 + keep)], W2.at[pl.ds(c * 128, 128), lanes(k)], l_w).start()
            w.make(qw.at[:, lanes(k * 2 + 1 - keep)], W2.at[pl.ds(c * 128, 128), lanes(k)], s_w, r_w, s, mate).start()
            return 0
        lax.fori_loop(0, Z * YH, wload, 0)
        kvload = pltpu.make_async_copy(kvflat, KVL, l_v)
        kvload.start()
        for load in loads:
            load.wait()

        tok = s * ROWS + lax.broadcasted_iota(jnp.int32, (1, ROWS), 1)
        place = (tok - openings(tok, doc)).astype(F32)
        freq = jnp.exp(lax.broadcasted_iota(jnp.int32, (HD // 2, 1), 0).astype(F32) * STEP)
        angle = freq * place
        COS[...] = jnp.cos(angle)
        SIN[...] = jnp.sin(angle)
        prompts = prow[...]
        for i in range(8):
            at = i * 256 + lax.broadcasted_iota(jnp.int32, (256, NP), 0)
            CM[pl.ds(i * 256, 256), :] = jnp.where(at == prompts, 1.0, 0.0).astype(BF16)
        def mask(i, _):
            t = s * ROWS + i * 32 + lax.broadcasted_iota(jnp.int32, (32, 1), 0)
            j = lax.broadcasted_iota(jnp.int32, (32, SEQ), 1)
            BIAS[pl.ds(pl.multiple_of(i * 32, 32), 32), :] = jnp.where(
                (j >= openings(t, doc)) & (j <= t), 0.0, -jnp.inf)
            return 0
        lax.fori_loop(0, ROWS // 32, mask, 0)
        near = lax.broadcasted_iota(jnp.int32, (PL, NP), 1) == (
            s * PL + lax.broadcasted_iota(jnp.int32, (PL, NP), 0))
        own_p = jnp.sum(jnp.where(near, prompts.astype(F32), 0.0), axis=1, keepdims=True).astype(jnp.int32)
        pick = jnp.where(lax.broadcasted_iota(jnp.int32, (PL, ROWS), 1) == own_p - s * ROWS,
                         1.0, 0.0).astype(BF16)
        lane = lax.broadcasted_iota(jnp.int32, (1, HD), 1)
        freq_l = jnp.exp(jnp.where(lane < 64, lane, lane - 64).astype(F32) * STEP)
        angle_p = (own_p - openings(own_p, doc)).astype(F32) * freq_l
        cos_p = jnp.cos(angle_p)
        sin_p = jnp.where(lane < 64, 1.0, -1.0) * jnp.sin(angle_p)
        T.update(kvload=kvload, pick=pick, cos_p=cos_p, sin_p=sin_p)

    def back(u):
        return u * T["cos_p"] + pltpu.roll(u, 64, 1) * T["sin_p"]

    flow.task("setup", after=[("Y", 0, 0, "A"), ("Y", 0, 0, "B")], work=setup, cost=1.0, rank=-1)

    def gain(zz):
        cols = pl.ds(pl.multiple_of(zz * 512, 512), 512)
        part = nt(W2[:, cols], H[:, cols])
        QP[0] = QP[0] + part[:128]
        QP[1] = QP[1] + part[128:]

    def gain_kv(zz):
        cols = pl.ds(pl.multiple_of(zz * 512, 512), 512)
        part = nt(KWF[:, cols], H[:, cols]).reshape(2, 2, 16, ROWS)
        KP[0] = KP[0] + part[:, 0]
        KP[1] = KP[1] + part[:, 1]

    kz_keys = [("kz", i) for i in range(Z - 1)]
    for key, zz in zip(kz_keys, zpeers):
        flow.arrival(key, KZ.at[zz], r_kz.at[zz])
    ysides = [(yh + e) % YH for e in range(1, YH)]

    def ky_go(e, yy):
        return lambda: w.send(KZ.at[:, yy // 2, yy % 2], KY.at[yh], s_ky.at[e], r_ky.at[yh], s, d.far(z, yy))

    def kz_work():
        kzown.wait()
        KY[yh] = KZ[:, yh // 2, yh % 2]
    flow.task("kz0", sends=[("n", 8, key, lambda: None) for key in kz_keys], rank=-3)
    flow.task("kz", needs=kz_keys, work=kz_work,
              sends=[(("y+", "y-", "y+")[e], 16, ("ky", e), ky_go(e, yy)) for e, yy in enumerate(ysides)])
    for e, yy in enumerate(ysides):
        flow.arrival(("ky", e), KY.at[yy], r_ky.at[yy])
    sx = (1 - yl) * X + x
    kx_row = lambda dx, ep: (yl + ep) % YL * X + (x + dx) % X

    def ky_work():
        for zz in range(Z):
            for yy in range(YH):
                KW[s, :, pl.ds((zz * YH + yy) * 128, 128)] = KY[yy, zz]

    def kx_send(dx, ep, way):
        ex = 1 if way == "x+" else -1
        row = kx_row(dx, ep)
        slot = s_kx.at[used[1]]
        used[1] += 1
        return (way, 64, ("kx", (dx - ex) % X, ep), lambda: w.send(
            KW.at[row], KW.at[row], slot, r_kx.at[row], yl * X + (x + ex) % X, f))
    used.append(0)
    flow.task("ky", needs=[("ky", e) for e in range(YH - 1)], work=ky_work, cost=0.2,
              sends=[("y+", 64, ("kl",), lambda: w.send(KW.at[s], KW.at[s], s_kl, r_kl, sx, f)),
                     kx_send(0, 0, "x+"), kx_send(0, 0, "x-")])
    flow.arrival(("kl",), KW.at[sx], r_kl)
    flow.task("kl", needs=[("kl",)], sends=[kx_send(0, 1, "x+"), kx_send(0, 1, "x-")])
    for ep in range(YL):
        for dx in range(1, X):
            flow.arrival(("kx", dx, ep), KW.at[kx_row(dx, ep)], r_kx.at[kx_row(dx, ep)])
            sends = []
            if dx == 3 and ep == 0:
                sends = [kx_send(dx, ep, "x+")]
            if dx == 1 and ep == 1:
                sends = [kx_send(dx, ep, "x-")]
            flow.task(("kx", dx, ep), needs=[("kx", dx, ep)], sends=sends)

    def kwf_work():
        for i in range(X * YL):
            KWF[pl.ds(i * 8, 8), :] = KW[i]
    flow.task("kwf", after=["ky", "kl"] + [("kx", dx, ep) for dx in range(1, X) for ep in range(YL)],
              work=kwf_work, cost=0.2, rank=1)

    def wq_work():
        mine_w, other_w = W2.at[pl.ds(c * 128, 128)], W2.at[pl.ds(o * 128, 128)]
        pltpu.make_async_copy(mine_w, mine_w, l_w).wait()
        recv(other_w, r_w)
        w.make(other_w, other_w, s_w, r_w, s, mate).wait_send()
        hown.wait()
        QP[...] = jnp.zeros_like(QP)
        KP[...] = jnp.zeros_like(KP)
    flow.task("wq0", sends=[("n", 8, ("wq",), lambda: None)], rank=-3)
    flow.task("wq", after=["wq0", ("Y", 0, 2, "A")], work=wq_work, cost=0.3, rank=1)
    for dz in range(Z):
        chunk_of = [(kind, dz, dy, h) for kind in KINDS for dy in range(YH) for h in "AB"]
        flow.task(("gkv", dz), after=chunk_of + ["wq", "kwf"], cost=0.15, rank=1,
                  work=functools.partial(lambda i: gain_kv((z + i) % Z), dz))
        flow.task(("gq", dz), after=chunk_of + ["wq"], cost=0.32, rank=2,
                  work=functools.partial(lambda i: gain((z + i) % Z), dz))
    flow.task("kvx", after=[("gkv", dz) for dz in range(Z)], rank=1,
              sends=[("m", 32, ("kr",), lambda: w.send(KP.at[o], KR, s_p, r_p, s, mate))])
    flow.task("qx", after=[("gq", dz) for dz in range(Z)], rank=1,
              sends=[("m", 128, ("qr",), lambda: w.send(QP.at[o], QR, s_q, r_q, s, mate))])

    def kblock(e, dx):
        yy, ll = yrel[e]
        return KVT.at[yy // 2, :, yy % 2, (c + e + dx) % 2, :, lanes(ll * X + (x + dx) % X, ROWS)]

    def kr_work():
        total = KP[c] + KR[...]
        kvb = total.astype(BF16)
        kf = kvb.astype(F32)
        b16 = pl.ds(pl.multiple_of((yh % 2) * 32 + c * 16, 16), 16)
        ck, sk = COS[b16, :], SIN[b16, :]
        iskey = yh < 2
        KB[0] = jnp.where(iskey, kf[0] * ck - kf[1] * sk, kf[0]).astype(BF16)
        KB[1] = jnp.where(iskey, kf[1] * ck + kf[0] * sk, kf[1]).astype(BF16)
        KVT[yh // 2, :, yh % 2, c, :, lanes(s, ROWS)] = KB[...]

    yrel = [(yh, yl)] + ypeers
    LATE = (4,)
    used.append(0)

    def x_send(dx, e, way):
        ex = {"x+": 1, "x-": -1, "x2": 2}[way]
        yy, ll = yrel[e]
        block = kblock(e, dx)
        src = KB if (dx, e) == (0, 0) else block
        slot = s_x.at[used[2]]
        used[2] += 1
        return (way, 16, ("x", (dx - ex) % X, e), lambda: w.send(
            src, block, slot, r_x.at[(x + dx) % X, yy, ll], yl * X + (x + ex) % X,
            f if ex == 2 else mate))

    def b_send(e):
        yy, ll = ypeers[e]
        return ("y+" if e < 4 else "y-", 16 * min(e + 1, 7 - e) / 4, ("b", 7 - e), lambda: w.send(
            KB, kblock(0, 0), s_b.at[e], r_b.at[yh, yl], ll * X + x, d.fid(z, yy, (c + e + 1) % 2)))

    flow.arrival(("kr",), KR, r_p)
    flow.task("kr", needs=[("kr",)], work=kr_work, cost=0.2,
              sends=[b_send(e) for e in (0, 6, 1, 5, 2, 4, 3)] + [x_send(0, 0, "x+"), x_send(0, 0, "x-")])
    for e in range(1, YH * YL):
        yy, ll = yrel[e]
        flow.arrival(("b", e), kblock(e, 0), r_b.at[yy, ll])
        flow.task(("b", e), needs=[("b", e)], sends=([x_send(0, e, "x2")] if e in LATE else []) + [
            x_send(0, e, "x+"), x_send(0, e, "x-")])
    for e in range(YH * YL):
        yy, ll = yrel[e]
        for dx in range(1, X):
            xx = (x + dx) % X
            flow.arrival(("x", dx, e), kblock(e, dx), r_x.at[xx, yy, ll])
            sends = []
            if dx == 3 and e % 2 == 0 and e not in LATE:
                sends = [x_send(dx, e, "x+")]
            if dx == 1 and e % 2 == 1 and e not in LATE:
                sends = [x_send(dx, e, "x-")]
            flow.task(("x", dx, e), needs=[("x", dx, e)], sends=sends)

    def c_send(dx, ep):
        col = (yl + ep) % YL * X + (x + dx) % X
        part = KVT.at[:, :, :, (c + ep + dx) % 2, :, lanes(col, ROWS)]
        other = KVT.at[:, :, :, (o + ep + dx) % 2, :, lanes(col, ROWS)]
        flow.arrival(("c", dx, ep), other, r_c.at[col])
        return ("m", 64, ("c", dx, ep), lambda: w.send(part, part, s_c.at[dx, ep], r_c.at[col], s, mate))
    for dx in range(X):
        for ep in range(YL):
            if dx:
                after = [("x", dx, e) for e in range(ep, 8, 2)]
            else:
                after = [("b", e) if e else "kr" for e in range(ep, 8, 2)]
            flow.task(("cs", dx, ep), after=after, sends=[c_send(dx, ep)])
            flow.task(("c", dx, ep), needs=[("c", dx, ep)], after=[("cs", i, j) for i in range(X) for j in range(YL)])

    def q_work():
        q = QP[c] + QR[...]
        q1, q2 = q[:64], q[64:]
        co, si = COS[...], SIN[...]
        qt = jnp.concatenate([q1 * co - q2 * si, q2 * co + q1 * si], axis=0)
        QB[...] = jnp.transpose(qt).astype(BF16)
    flow.arrival(("qr",), QR, r_q)
    flow.task("q", needs=[("qr",)], work=q_work, cost=0.3, rank=1)
    flow.emit(recv)

    pick = T["pick"]
    kt = KVT[0].reshape(HD, SEQ)
    vt = KVT[1].reshape(HD, SEQ)
    CH = 64

    for i in range(ROWS // CH):
        rows = pl.ds(i * CH, CH)
        raw = nn(QB[rows, :], kt) * (SCALE * math.log2(math.e)) + BIAS[rows, :]
        e = jnp.exp2(raw - jnp.max(raw, axis=1, keepdims=True))
        probs = (e * (1.0 / jnp.sum(e, axis=1, keepdims=True))).astype(BF16)
        PB[rows, :] = probs
        att_out[rows, :] = nt(probs, vt).astype(BF16)

    att = att_out[...]
    da = dat[...]
    row_up = nn(pick, da)
    row_dot = jnp.sum(row_up * nn(pick, att), axis=1, keepdims=True)
    row_dp = nn(row_up.astype(BF16), vt)
    row_ds = (nn(pick, PB[...]) * (row_dp - row_dot)).astype(BF16)
    QG[c] = back(nt(row_ds, kt) * SCALE).astype(BF16)
    w.send(QG.at[c], QG.at[c], s_g, r_g, s, mate)
    rowdot = jnp.sum(da.astype(F32) * att.astype(F32), axis=1, keepdims=True)
    colp = nn(PB[...], CM[...])
    cv = nn(vt, CM[...]).astype(BF16)
    cds = (colp * (nn(da, cv) - rowdot)).astype(BF16)
    GP[0] = tn(cds, QB[...]).reshape(YL, X, PL, HD)
    GP[1] = tn(colp.astype(BF16), da).reshape(YL, X, PL, HD)
    for e in range(X):
        xx = (x + e) % X
        for i, (pp, ff) in enumerate(((c, f), (o, mate))):
            if e or i:
                w.send(GP.at[pp, :, xx], GX.at[x, c], s_d2.at[e, i], r_d2.at[x, c], yl * X + xx, ff)

    recv(QG.at[o], r_g)
    both = jnp.concatenate([QG[0], QG[1]], axis=1)

    for e in (4, 3, 5, 2, 6, 1, 7, 0):
        zz = (z + e) % Z
        part = nn(both, W2[:, pl.ds(pl.multiple_of(zz * 512, 512), 512)])
        for yy in range(YH):
            piece = part[:, yy * 128:(yy + 1) * 128]
            if e:
                QF[zz, yy] = piece.astype(BF16)
            else:
                QS[yy] = piece
        if e:
            w.send(QF.at[zz], QY.at[z], s_e2.at[e - 1], r_e2.at[z], s, d.far(zz, yh))

    recv(GX.at[x, o], r_d2.at[x, o])
    acc = GP[c, :, x] + GX[x, o]
    for xx in xpeers:
        for cc in range(C):
            recv(GX.at[xx, cc], r_d2.at[xx, cc])
            acc = acc + GX[xx, cc]
    G2[...] = acc
    for e in (3, 2, 4, 1, 5, 0, 6):
        yy, ll = ypeers[e]
        w.send(G2.at[ll], GY.at[yh, yl], s_d3.at[e], r_d3.at[yh, yl], ll * X + x, d.fid(z, yy, c))
    acc = G2[yl]
    for yy, ll in ypeers:
        recv(GY.at[yy, ll], r_d3.at[yy, ll])
        acc = acc + GY[yy, ll]
    dkv = jnp.where(c == 0, back(acc * SCALE), acc).astype(BF16)
    DK[...] = dkv
    DKV[z, c] = dkv
    for e in (3, 2, 4, 1, 5, 0, 6):
        zz = zpeers[e]
        for i, cc in enumerate((c, o)):
            w.send(DK, DKV.at[z, c], s_d4.at[e, i], r_d4.at[z, c], s, d.fid(zz, yh, cc))
    w.send(DK, DKV.at[z, c], s_d4.at[Z - 1, 0], r_d4.at[z, c], s, mate)
    for zz in zpeers:
        recv(QY.at[zz], r_e2.at[zz])
        QS[...] = QS[...] + QY[zz].astype(F32)
    for e, yy in enumerate(ysides):
        w.send(QS.at[yy], QZ.at[yh], s_e3.at[e], r_e3.at[yh], s, d.far(z, yy))
    T["kvload"].wait()
    recv(DKV.at[z, o], r_d4.at[z, o])
    for zz in zpeers:
        recv(DKV.at[zz, 0], r_d4.at[zz, 0])
        recv(DKV.at[zz, 1], r_d4.at[zz, 1])
    wide = jnp.concatenate([DKV[g, p] for g in range(Z) for p in range(2)], axis=1)
    out = QS[yh] + nn(wide, KVL[...])
    for yy in ysides:
        recv(QZ.at[yy], r_e3.at[yy])
        out = out + QZ[yy]
    pg_out[...] = out
    w.finish()


def per_device(hidden, q_weight, kv_weight, d_attended, doc_lengths, prompt_pos):
    vm = pl.BlockSpec(memory_space=pltpu.VMEM)
    hbm = pl.BlockSpec(memory_space=pltpu.HBM)
    return pl.pallas_call(
        whole,
        out_shape=(jax.ShapeDtypeStruct((ROWS, HD), BF16),
                   jax.ShapeDtypeStruct((PL, HD), F32)),
        in_specs=[hbm] * 7,
        out_specs=(vm, vm),
        scratch_shapes=[
            VMEM((ROWS, 4096), BF16),
            VMEM((256, 4096), BF16),
            VMEM((Z, 2, 2, 8, FB), BF16),
            VMEM((YH, Z, 8, FB), BF16),
            VMEM((X * YL, 8, 4096), BF16),
            VMEM((64, 4096), BF16),
            VMEM((2, 2, 16, ROWS), F32),
            VMEM((2, 16, ROWS), F32),
            VMEM((2, 16, ROWS), BF16),
            VMEM((2, HD, ROWS), F32),
            VMEM((HD, ROWS), F32),
            VMEM((2, 2, 2, 2, 16, SEQ), BF16),
            VMEM((HD // 2, ROWS), F32),
            VMEM((HD // 2, ROWS), F32),
            VMEM((ROWS, HD), BF16),
            VMEM((ROWS, SEQ), BF16),
            VMEM((SEQ, NP), BF16),
            VMEM((SEQ, FB), BF16),
            VMEM((2, PL, HD), BF16),
            VMEM((2, YL, X, PL, HD), F32),
            VMEM((X, C, YL, PL, HD), F32),
            VMEM((YL, PL, HD), F32),
            VMEM((YH, YL, PL, HD), F32),
            VMEM((PL, HD), BF16),
            VMEM((Z, 2, PL, HD), BF16),
            VMEM((Z, YH, PL, HD), BF16),
            VMEM((Z, YH, PL, HD), BF16),
            VMEM((YH, PL, HD), F32),
            VMEM((YH, PL, HD), F32),
            VMEM((ROWS, FB), BF16),
            pltpu.SMEM((4,), jnp.int32),
            VMEM((1, NP), jnp.int32),
            VMEM((ROWS, SEQ), F32),
            DMA((124,)), DMA((2, 2, Z * YH)),
            DMA(()), DMA(()), DMA(()),
            DMA((Z - 1,)), DMA((Z,)), DMA((YH - 1,)), DMA((YH,)),
            DMA(()), DMA(()), DMA((6,)), DMA((X * YL,)),
            DMA(()), DMA(()),
            DMA((YH * YL - 1,)), DMA((YH, YL)),
            DMA((24,)), DMA((X, YH, YL)),
            DMA((X, YL)), DMA((X * YL,)),
            DMA(()), DMA(()), DMA(()), DMA((5,)),
            DMA(()), DMA(()),
            DMA((X, C)), DMA((X, C)),
            DMA((YH * YL - 1,)), DMA((YH, YL)),
            DMA((Z, 2)), DMA((Z, 2)),
            DMA((Z - 1,)), DMA((Z,)),
            DMA((YH - 1,)), DMA((YH,)),
        ],
        compiler_params=pltpu.CompilerParams(
            collective_id=0, has_side_effects=True, vmem_limit_bytes=48 << 20),
        name="whole",
    )(*(pltpu.with_memory_space_constraint(a, pltpu.HBM) for a in (
        hidden, q_weight, kv_weight.reshape(Z, 2, 2, 2, 32, FB), kv_weight, d_attended,
        doc_lengths, prompt_pos.reshape(1, NP))))


def solution(mesh):
    placed = (P("seq", "fsdp"), P("fsdp", None), P(None, "fsdp"), P("seq", "fsdp"), P(), P())
    return jax.shard_map(
        per_device,
        mesh=mesh,
        in_specs=placed,
        out_specs=(P("seq", "fsdp"), P("seq", "fsdp")),
        check_vma=False,
    )
```

```python
import functools
import math

import jax
import jax.numpy as jnp
from jax import lax
from jax.experimental import pallas as pl
from jax.experimental.pallas import tpu as pltpu
from jax.sharding import PartitionSpec as P

ROPE_THETA = 1000000.0
MESH = pl.DeviceIdType.MESH
F32 = jnp.float32
BF16 = jnp.bfloat16
VMEM = pltpu.VMEM
DMA = pltpu.SemaphoreType.DMA

X, YL, YH, Z, C = 4, 2, 4, 8, 2
ZROWS = 32
KINDS = "YZ" if ZROWS else "Y"
ROWS, HD, FB = 256, 128, 128


def nt(a, b):
    return lax.dot_general(a, b, (((1,), (1,)), ((), ())), preferred_element_type=F32)


class Place:
    def __init__(self):
        self.s = lax.axis_index("seq")
        self.f = lax.axis_index("fsdp")
        self.x = self.s % X
        self.yl = self.s // X
        self.z = self.f // (YH * C)
        self.yh = (self.f // C) % YH
        self.c = self.f % C
        self.o = 1 - self.c

    def hop(self, z, yh):
        return (self.c + z + self.z + yh + self.yh) % 2

    def far(self, z, yh):
        return self.fid(z, yh, self.hop(z, yh))

    def fid(self, z, yh, c):
        return (z * YH + yh) * C + c


class Wires:
    def __init__(self):
        self.open = []

    def make(self, src, dst, ss, rs, seq, fs):
        return pltpu.make_async_remote_copy(
            src_ref=src, dst_ref=dst, send_sem=ss, recv_sem=rs,
            device_id={"seq": seq, "fsdp": fs}, device_id_type=MESH)

    def send(self, *args):
        copy = self.make(*args)
        copy.start()
        self.open.append(copy)

    def finish(self):
        for copy in self.open:
            copy.wait_send()


def nn(a, b):
    return lax.dot_general(a, b, (((1,), (0,)), ((), ())), preferred_element_type=F32)


def tn(a, b):
    return lax.dot_general(a, b, (((0,), (0,)), ((), ())), preferred_element_type=F32)


LAZY = 1.5


class Flow:
    RATE = {"z+": 45.0, "z-": 45.0, "y+": 22.0, "y-": 22.0, "x+": 45.0, "x-": 45.0, "x2": 22.0, "m": 300.0, "n": 1e9}
    LAG = {"z+": 2.1, "z-": 2.1, "y+": 2.9, "y-": 2.9, "x+": 2.1, "x-": 2.1, "x2": 2.8, "m": 1.0, "n": 4.0}

    def __init__(self):
        self.tasks = {}
        self.recvs = {}

    def arrival(self, key, ref, sem):
        self.recvs[key] = (ref, sem)

    def task(self, name, needs=(), after=(), sends=(), work=None, cost=0.05, rank=0):
        self.tasks[name] = (set(needs), set(after), list(sends), work, cost, rank)

    def order(self):
        at, done, free, now, out = {}, {}, {}, 0.0, []
        todo = list(self.tasks)
        while todo:
            best = None
            for i, name in enumerate(todo):
                needs, after, sends, work, _, rank = self.tasks[name]
                if all(n in at for n in needs) and all(a in done for a in after):
                    ready = max([at[n] for n in needs] + [done[a] for a in after] + [0.0])
                    if needs and not sends and work is None:
                        ready += LAZY
                    cand = (max(ready, now), rank, i)
                    if best is None or cand < best:
                        best = cand
            assert best is not None, todo
            name = todo.pop(best[2])
            _, _, sends, _, cost, _ = self.tasks[name]
            now = best[0] + cost
            done[name] = now
            for link, size, key, _ in sends:
                start = max(free.get(link, 0.0), now)
                free[link] = start + size / self.RATE[link]
                if key is not None:
                    lag = self.LAG[link] if key[0] != "b" else 1.5 + 0.8 * min(key[1], 8 - key[1])
                    at[key] = max(at.get(key, 0.0), free[link] + lag)
            out.append(name)
        self.model = done
        return out

    def emit(self, recv):
        for name in self.order():
            needs, _, sends, work, _, _ = self.tasks[name]
            for key in sorted(needs, key=repr):
                recv(*self.recvs[key])
            if work is not None:
                work()
            for _, _, _, go in sends:
                go()


def lanes(k, n=128):
    return pl.ds(pl.multiple_of(k * n, n), n)


STEP = -2.0 * math.log(ROPE_THETA) / HD
SCALE = 1.0 / math.sqrt(HD)
SEQ, NP, PL = 2048, 128, 16


def openings(tokens, doc):
    end = jnp.int32(0)
    start = jnp.zeros_like(tokens)
    for i in range(4):
        end = end + doc[i]
        start = start + jnp.where(tokens >= end, doc[i], 0)
    return start


def whole(hid, qw, kvw, kvflat, dhbm, dochbm, phbm, att_out, pg_out,
          H, W2, KZ, KY, KW, KWF, KP, KR, KB, QP, QR, KVT, COS, SIN, QB, PB, CM, KVL,
          QG, GP, GB, GX, G2, GY, DK, DKV, QF, QY, QS, QZ, dat, doc, prow, BIAS,
          s_h, r_h, s_w, r_w, l_w, s_kz, r_kz, s_ky, r_ky, s_kl, r_kl, s_kx, r_kx,
          s_p, r_p, s_b, r_b, s_x, r_x, s_c, r_c, s_q, r_q, l_v, l_in,
          s_g, r_g, s_d2, r_d2, s_d3, r_d3, s_d4, r_d4, s_e2, r_e2, s_e3, r_e3):
    d = Place()
    s, f, x, yl, z, yh, c, o = d.s, d.f, d.x, d.yl, d.z, d.yh, d.c, d.o
    mate = d.fid(z, yh, o)
    zup, zdn = (z + 1) % Z, (z + Z - 1) % Z
    w = Wires()

    loads = [pltpu.make_async_copy(a, b, l_in.at[i]) for i, (a, b) in enumerate(
        ((dochbm, doc), (phbm, prow), (dhbm, dat)))]
    for load in loads:
        load.start()
    bar = pltpu.get_barrier_semaphore()
    peers = []
    ypeers = []
    for e in range(1, YH * YL):
        y = (yh * YL + yl + e) % (YH * YL)
        ypeers.append((y // YL, y % YL))
    xpeers = [(x + e) % X for e in range(1, X)]
    zpeers = [(z + e) % Z for e in range(1, Z)]
    for e in (4, 3, 5, 2, 6, 1, 7):
        for cc in (c, o):
            peers.append((s, d.fid((z + e) % Z, yh, cc)))
    for e in (4, 3, 5, 2, 6, 1, 7):
        y = (yh * YL + yl + e) % (YH * YL)
        peers.append(((y % YL) * X + x, d.fid(z, y // YL, c)))
        if e % 2:
            peers.append(((y % YL) * X + x, d.fid(z, y // YL, o)))
    for e in (2, 1, 3):
        for ff in (f, mate):
            peers.append((yl * X + (x + e) % X, ff))
    for e in (1, 3):
        peers.append((s, d.fid(z, (yh + e) % YH, o)))
    peers.append((s, mate))
    for ps, pf in peers:
        pl.semaphore_signal(bar, inc=1, device_id={"seq": ps, "fsdp": pf}, device_id_type=MESH)
    pl.semaphore_wait(bar, len(peers))

    def hblock(zz, yy):
        return H.at[:, lanes(zz * YH + yy)]

    def recv(ref, sem):
        w.make(ref, ref, s_q, sem, s, mate).wait_recv()

    def eighth(g):
        return kvw.at[g, :, s // 4, :, pl.ds(pl.multiple_of((s % 4) * 8, 8), 8), :]
    for e, zz in enumerate(zpeers):
        w.send(eighth(zz), KZ.at[z], s_kz.at[e], r_kz.at[z], s, d.far(zz, yh))
    kzown = pltpu.make_async_copy(eighth(z), KZ.at[z], l_in.at[3])
    kzown.start()
    hown = pltpu.make_async_copy(hid, hblock(z, yh), l_in.at[4])
    hown.start()
    flow = Flow()
    used = [0]
    ny = ROWS - ZROWS
    ROW = {"Y": {"A": (0, ny // 2), "B": (ny // 2, ny // 2)}, "Z": {"A": (ny, ZROWS // 2), "B": (ny + ZROWS // 2, ZROWS // 2)}}
    REACH = {"A": {"z+": 4, "z-": 3, "y+": 2, "y-": 1}, "B": {"z+": 3, "z-": 4, "y+": 1, "y-": 2}}
    STEPS = {"z+": (1, 0), "z-": (-1, 0), "y+": (0, 1), "y-": (0, -1)}

    def hpiece(kind, dz, dy, h):
        r0, n = ROW[kind][h]
        return H.at[pl.ds(r0, n), lanes((z + dz) % Z * YH + (yh + dy) % YH)]

    def hsem(kind, dz, dy, h):
        return r_h.at["YZ".index(kind), "AB".index(h), (z + dz) % Z * YH + (yh + dy) % YH]

    def hsend(kind, dz, dy, h, way):
        ez, ey = STEPS[way]
        r0, n = ROW[kind][h]
        slot = s_h.at[used[0]]
        used[0] += 1
        src = hid.at[pl.ds(r0, n), :] if (dz, dy) == (0, 0) else hpiece(kind, dz, dy, h)

        def go():
            w.send(src, hpiece(kind, dz, dy, h), slot, hsem(kind, dz, dy, h),
                   s, d.fid((z + ez) % Z, (yh + ey) % YH, o))
        return (way, n / 4, (kind, (dz - ez) % Z, (dy - ey) % YH, h), go)

    def onward(dist, size, h, up, down, first):
        if dist == 0:
            return [up, down] if first == up else [down, up]
        out = []
        back = size - dist
        if back < REACH[h][up] and dist > size // 2:
            out.append(up)
        if dist < REACH[h][down] and dist < size // 2:
            out.append(down)
        return out

    def hidden_tasks():
        for kind in KINDS:
            start = []
            for dz in range(Z):
                for dy in range(YH):
                    for h in "AB":
                        name = (kind, dz, dy, h)
                        needs = [name] if dz or dy else []
                        if needs:
                            flow.arrival(name, hpiece(*name), hsem(*name))
                        alongz = onward(dz, Z, h, "z+", "z-", "z+" if h == "A" else "z-")
                        alongy = onward(dy, YH, h, "y+", "y-", "y+" if h == "A" else "y-")
                        if kind == "Y":
                            ways = (alongy if dz == 0 else []) + alongz
                            if dz == 0 and dy == 0:
                                ways = [alongy[0], alongz[0], alongz[1], alongy[1]]
                        else:
                            ways = alongz if dy == 0 else alongy
                        if kind == "Z" and dy == 0:
                            after = [name] + ([("Y", 0, 1, "B"), ("Y", 0, 3, "A")] if dz else [])
                            flow.task(("Zy", dz, h), after=after, rank=1,
                                      sends=[hsend(kind, dz, dy, h, way) for way in alongy])
                        if dz or dy:
                            flow.task(name, needs=needs, sends=[hsend(kind, dz, dy, h, way) for way in ways])
                        else:
                            start += [(i, hsend(kind, dz, dy, h, way)) for i, way in enumerate(ways)]
            start.sort(key=lambda pair: (pair[0] + 1) // 2)
            flow.task((kind, 0, 0, "A"), sends=[send for _, send in start], rank=-1 if kind == "Z" else -2)
            flow.task((kind, 0, 0, "B"), after=[(kind, 0, 0, "A")], rank=-2)
    hidden_tasks()

    T = {}

    def setup():
        def wload(k, _):
            keep = d.hop(k // YH, k % YH)
            pltpu.make_async_copy(qw.at[:, lanes(k * 2 + keep)], W2.at[pl.ds(c * 128, 128), lanes(k)], l_w).start()
            w.make(qw.at[:, lanes(k * 2 + 1 - keep)], W2.at[pl.ds(c * 128, 128), lanes(k)], s_w, r_w, s, mate).start()
            return 0
        lax.fori_loop(0, Z * YH, wload, 0)
        kvload = pltpu.make_async_copy(kvflat, KVL, l_v)
        kvload.start()
        for load in loads:
            load.wait()

        tok = s * ROWS + lax.broadcasted_iota(jnp.int32, (1, ROWS), 1)
        place = (tok - openings(tok, doc)).astype(F32)
        freq = jnp.exp(lax.broadcasted_iota(jnp.int32, (HD // 2, 1), 0).astype(F32) * STEP)
        angle = freq * place
        COS[...] = jnp.cos(angle)
        SIN[...] = jnp.sin(angle)
        prompts = prow[...]
        for i in range(8):
            at = i * 256 + lax.broadcasted_iota(jnp.int32, (256, NP), 0)
            CM[pl.ds(i * 256, 256), :] = jnp.where(at == prompts, 1.0, 0.0).astype(BF16)
        def mask(i, _):
            t = s * ROWS + i * 32 + lax.broadcasted_iota(jnp.int32, (32, 1), 0)
            j = lax.broadcasted_iota(jnp.int32, (32, SEQ), 1)
            BIAS[pl.ds(pl.multiple_of(i * 32, 32), 32), :] = jnp.where(
                (j >= openings(t, doc)) & (j <= t), 0.0, -jnp.inf)
            return 0
        lax.fori_loop(0, ROWS // 32, mask, 0)
        near = lax.broadcasted_iota(jnp.int32, (PL, NP), 1) == (
            s * PL + lax.broadcasted_iota(jnp.int32, (PL, NP), 0))
        own_p = jnp.sum(jnp.where(near, prompts.astype(F32), 0.0), axis=1, keepdims=True).astype(jnp.int32)
        pick = jnp.where(lax.broadcasted_iota(jnp.int32, (PL, ROWS), 1) == own_p - s * ROWS,
                         1.0, 0.0).astype(BF16)
        lane = lax.broadcasted_iota(jnp.int32, (1, HD), 1)
        freq_l = jnp.exp(jnp.where(lane < 64, lane, lane - 64).astype(F32) * STEP)
        angle_p = (own_p - openings(own_p, doc)).astype(F32) * freq_l
        cos_p = jnp.cos(angle_p)
        sin_p = jnp.where(lane < 64, 1.0, -1.0) * jnp.sin(angle_p)
        T.update(kvload=kvload, pick=pick, cos_p=cos_p, sin_p=sin_p)

    def back(u):
        return u * T["cos_p"] + pltpu.roll(u, 64, 1) * T["sin_p"]

    flow.task("setup", after=[("Y", 0, 0, "A"), ("Y", 0, 0, "B")], work=setup, cost=1.0, rank=-1)

    def gain(zz):
        cols = pl.ds(pl.multiple_of(zz * 512, 512), 512)
        part = nt(W2[:, cols], H[:, cols])
        QP[0] = QP[0] + part[:128]
        QP[1] = QP[1] + part[128:]

    def gain_kv(zz):
        cols = pl.ds(pl.multiple_of(zz * 512, 512), 512)
        part = nt(KWF[:, cols], H[:, cols]).reshape(2, 2, 16, ROWS)
        KP[0] = KP[0] + part[:, 0]
        KP[1] = KP[1] + part[:, 1]

    kz_keys = [("kz", i) for i in range(Z - 1)]
    for key, zz in zip(kz_keys, zpeers):
        flow.arrival(key, KZ.at[zz], r_kz.at[zz])
    ysides = [(yh + e) % YH for e in range(1, YH)]

    def ky_go(e, yy):
        return lambda: w.send(KZ.at[:, yy // 2, yy % 2], KY.at[yh], s_ky.at[e], r_ky.at[yh], s, d.far(z, yy))

    def kz_work():
        kzown.wait()
        KY[yh] = KZ[:, yh // 2, yh % 2]
    flow.task("kz0", sends=[("n", 8, key, lambda: None) for key in kz_keys], rank=-3)
    flow.task("kz", needs=kz_keys, work=kz_work,
              sends=[(("y+", "y-", "y+")[e], 16, ("ky", e), ky_go(e, yy)) for e, yy in enumerate(ysides)])
    for e, yy in enumerate(ysides):
        flow.arrival(("ky", e), KY.at[yy], r_ky.at[yy])
    sx = (1 - yl) * X + x
    kx_row = lambda dx, ep: (yl + ep) % YL * X + (x + dx) % X

    def ky_work():
        for zz in range(Z):
            for yy in range(YH):
                KW[s, :, pl.ds((zz * YH + yy) * 128, 128)] = KY[yy, zz]

    def kx_send(dx, ep, way):
        ex = 1 if way == "x+" else -1
        row = kx_row(dx, ep)
        slot = s_kx.at[used[1]]
        used[1] += 1
        return (way, 64, ("kx", (dx - ex) % X, ep), lambda: w.send(
            KW.at[row], KW.at[row], slot, r_kx.at[row], yl * X + (x + ex) % X, f))
    used.append(0)
    flow.task("ky", needs=[("ky", e) for e in range(YH - 1)], work=ky_work, cost=0.2,
              sends=[("y+", 64, ("kl",), lambda: w.send(KW.at[s], KW.at[s], s_kl, r_kl, sx, f)),
                     kx_send(0, 0, "x+"), kx_send(0, 0, "x-")])
    flow.arrival(("kl",), KW.at[sx], r_kl)
    flow.task("kl", needs=[("kl",)], sends=[kx_send(0, 1, "x+"), kx_send(0, 1, "x-")])
    for ep in range(YL):
        for dx in range(1, X):
            flow.arrival(("kx", dx, ep), KW.at[kx_row(dx, ep)], r_kx.at[kx_row(dx, ep)])
            sends = []
            if dx == 3 and ep == 0:
                sends = [kx_send(dx, ep, "x+")]
            if dx == 1 and ep == 1:
                sends = [kx_send(dx, ep, "x-")]
            flow.task(("kx", dx, ep), needs=[("kx", dx, ep)], sends=sends)

    def kwf_work():
        for i in range(X * YL):
            KWF[pl.ds(i * 8, 8), :] = KW[i]
    flow.task("kwf", after=["ky", "kl"] + [("kx", dx, ep) for dx in range(1, X) for ep in range(YL)],
              work=kwf_work, cost=0.2, rank=1)

    def wq_work():
        mine_w, other_w = W2.at[pl.ds(c * 128, 128)], W2.at[pl.ds(o * 128, 128)]
        pltpu.make_async_copy(mine_w, mine_w, l_w).wait()
        recv(other_w, r_w)
        w.make(other_w, other_w, s_w, r_w, s, mate).wait_send()
        hown.wait()
        QP[...] = jnp.zeros_like(QP)
        KP[...] = jnp.zeros_like(KP)
    flow.task("wq0", sends=[("n", 8, ("wq",), lambda: None)], rank=-3)
    flow.task("wq", after=["wq0", ("Y", 0, 2, "A")], work=wq_work, cost=0.3, rank=1)
    for dz in range(Z):
        chunk_of = [(kind, dz, dy, h) for kind in KINDS for dy in range(YH) for h in "AB"]
        flow.task(("gkv", dz), after=chunk_of + ["wq", "kwf"], cost=0.15, rank=1,
                  work=functools.partial(lambda i: gain_kv((z + i) % Z), dz))
        flow.task(("gq", dz), after=chunk_of + ["wq"], cost=0.32, rank=2,
                  work=functools.partial(lambda i: gain((z + i) % Z), dz))
    flow.task("kvx", after=[("gkv", dz) for dz in range(Z)], rank=1,
              sends=[("m", 32, ("kr",), lambda: w.send(KP.at[o], KR, s_p, r_p, s, mate))])
    flow.task("qx", after=[("gq", dz) for dz in range(Z)], rank=1,
              sends=[("m", 128, ("qr",), lambda: w.send(QP.at[o], QR, s_q, r_q, s, mate))])

    def kblock(e, dx):
        yy, ll = yrel[e]
        return KVT.at[yy // 2, :, yy % 2, (c + e + dx) % 2, :, lanes(ll * X + (x + dx) % X, ROWS)]

    def kr_work():
        total = KP[c] + KR[...]
        kvb = total.astype(BF16)
        kf = kvb.astype(F32)
        b16 = pl.ds(pl.multiple_of((yh % 2) * 32 + c * 16, 16), 16)
        ck, sk = COS[b16, :], SIN[b16, :]
        iskey = yh < 2
        KB[0] = jnp.where(iskey, kf[0] * ck - kf[1] * sk, kf[0]).astype(BF16)
        KB[1] = jnp.where(iskey, kf[1] * ck + kf[0] * sk, kf[1]).astype(BF16)
        KVT[yh // 2, :, yh % 2, c, :, lanes(s, ROWS)] = KB[...]

    yrel = [(yh, yl)] + ypeers
    LATE = (4,)
    used.append(0)

    def x_send(dx, e, way):
        ex = {"x+": 1, "x-": -1, "x2": 2}[way]
        yy, ll = yrel[e]
        block = kblock(e, dx)
        src = KB if (dx, e) == (0, 0) else block
        slot = s_x.at[used[2]]
        used[2] += 1
        return (way, 16, ("x", (dx - ex) % X, e), lambda: w.send(
            src, block, slot, r_x.at[(x + dx) % X, yy, ll], yl * X + (x + ex) % X,
            f if ex == 2 else mate))

    def b_send(e):
        yy, ll = ypeers[e]
        return ("y+" if e < 4 else "y-", 16 * min(e + 1, 7 - e) / 4, ("b", 7 - e), lambda: w.send(
            KB, kblock(0, 0), s_b.at[e], r_b.at[yh, yl], ll * X + x, d.fid(z, yy, (c + e + 1) % 2)))

    flow.arrival(("kr",), KR, r_p)
    flow.task("kr", needs=[("kr",)], work=kr_work, cost=0.2,
              sends=[b_send(e) for e in (0, 6, 1, 5, 2, 4, 3)] + [x_send(0, 0, "x+"), x_send(0, 0, "x-")])
    for e in range(1, YH * YL):
        yy, ll = yrel[e]
        flow.arrival(("b", e), kblock(e, 0), r_b.at[yy, ll])
        flow.task(("b", e), needs=[("b", e)], sends=([x_send(0, e, "x2")] if e in LATE else []) + [
            x_send(0, e, "x+"), x_send(0, e, "x-")])
    for e in range(YH * YL):
        yy, ll = yrel[e]
        for dx in range(1, X):
            xx = (x + dx) % X
            flow.arrival(("x", dx, e), kblock(e, dx), r_x.at[xx, yy, ll])
            sends = []
            if dx == 3 and e % 2 == 0 and e not in LATE:
                sends = [x_send(dx, e, "x+")]
            if dx == 1 and e % 2 == 1 and e not in LATE:
                sends = [x_send(dx, e, "x-")]
            flow.task(("x", dx, e), needs=[("x", dx, e)], sends=sends)

    def c_send(dx, ep):
        col = (yl + ep) % YL * X + (x + dx) % X
        part = KVT.at[:, :, :, (c + ep + dx) % 2, :, lanes(col, ROWS)]
        other = KVT.at[:, :, :, (o + ep + dx) % 2, :, lanes(col, ROWS)]
        flow.arrival(("c", dx, ep), other, r_c.at[col])
        return ("m", 64, ("c", dx, ep), lambda: w.send(part, part, s_c.at[dx, ep], r_c.at[col], s, mate))
    for dx in range(X):
        for ep in range(YL):
            if dx:
                after = [("x", dx, e) for e in range(ep, 8, 2)]
            else:
                after = [("b", e) if e else "kr" for e in range(ep, 8, 2)]
            flow.task(("cs", dx, ep), after=after, sends=[c_send(dx, ep)])
            flow.task(("c", dx, ep), needs=[("c", dx, ep)], after=[("cs", i, j) for i in range(X) for j in range(YL)])

    def q_work():
        q = QP[c] + QR[...]
        q1, q2 = q[:64], q[64:]
        co, si = COS[...], SIN[...]
        qt = jnp.concatenate([q1 * co - q2 * si, q2 * co + q1 * si], axis=0)
        QB[...] = jnp.transpose(qt).astype(BF16)
    flow.arrival(("qr",), QR, r_q)
    flow.task("q", needs=[("qr",)], work=q_work, cost=0.3, rank=1)
    flow.emit(recv)

    pick = T["pick"]
    kt = KVT[0].reshape(HD, SEQ)
    vt = KVT[1].reshape(HD, SEQ)
    CH = 64

    for i in range(ROWS // CH):
        rows = pl.ds(i * CH, CH)
        raw = nn(QB[rows, :], kt) * (SCALE * math.log2(math.e)) + BIAS[rows, :]
        e = jnp.exp2(raw - jnp.max(raw, axis=1, keepdims=True))
        probs = (e * (1.0 / jnp.sum(e, axis=1, keepdims=True))).astype(BF16)
        PB[rows, :] = probs
        att_out[rows, :] = nt(probs, vt).astype(BF16)

    att = att_out[...]
    da = dat[...]
    rowdot = jnp.sum(da.astype(F32) * att.astype(F32), axis=1, keepdims=True)
    gathered = nn(jnp.concatenate([PB[...], vt], axis=0), CM[...])
    colp, cv = gathered[:ROWS], gathered[ROWS:].astype(BF16)
    cds = (colp * (nn(da, cv) - rowdot)).astype(BF16)
    kg = tn(cds, QB[...]).reshape(YL, X, PL, HD)
    vg = tn(colp.astype(BF16), da).reshape(YL, X, PL, HD)
    GB[0] = kg.astype(BF16)
    GB[1] = vg.astype(BF16)
    GP[...] = jnp.where(c == 0, kg, vg)
    for e in (2, 1, 3, 0):
        xx = (x + e) % X
        for i, (pp, ff) in enumerate(((c, f), (o, mate))):
            if e or i:
                w.send(GB.at[pp, :, xx], GX.at[x, c], s_d2.at[e, i], r_d2.at[x, c], yl * X + xx, ff)
    row_up = nn(pick, da)
    row_dot = jnp.sum(row_up * nn(pick, att), axis=1, keepdims=True)
    row_dp = nn(row_up.astype(BF16), vt)
    row_ds = (nn(pick, PB[...]) * (row_dp - row_dot)).astype(BF16)
    QG[c] = back(nt(row_ds, kt) * SCALE).astype(BF16)
    w.send(QG.at[c], QG.at[c], s_g, r_g, s, mate)

    recv(QG.at[o], r_g)
    both = jnp.concatenate([QG[0], QG[1]], axis=1)

    for e in (4, 3, 5, 2, 6, 1, 7, 0):
        zz = (z + e) % Z
        part = nn(both, W2[:, pl.ds(pl.multiple_of(zz * 512, 512), 512)])
        for yy in range(YH):
            piece = part[:, yy * 128:(yy + 1) * 128]
            if e:
                QF[zz, yy] = piece.astype(BF16)
            else:
                QS[yy] = piece
        if e:
            w.send(QF.at[zz], QY.at[z], s_e2.at[e - 1], r_e2.at[z], s, d.far(zz, yh))

    recv(GX.at[x, o], r_d2.at[x, o])
    acc = GP[:, x] + GX[x, o].astype(F32)
    for xx in xpeers:
        for cc in range(C):
            recv(GX.at[xx, cc], r_d2.at[xx, cc])
            acc = acc + GX[xx, cc].astype(F32)
    G2[...] = acc
    for e in (3, 2, 4, 1, 5, 0, 6):
        yy, ll = ypeers[e]
        w.send(G2.at[ll], GY.at[yh, yl], s_d3.at[e], r_d3.at[yh, yl], ll * X + x, d.fid(z, yy, c))
    acc = G2[yl]
    for yy, ll in ypeers:
        recv(GY.at[yy, ll], r_d3.at[yy, ll])
        acc = acc + GY[yy, ll]
    dkv = jnp.where(c == 0, back(acc * SCALE), acc).astype(BF16)
    DK[...] = dkv
    DKV[z, c] = dkv
    for e in (3, 2, 4, 1, 5, 0, 6):
        zz = zpeers[e]
        for i, cc in enumerate((c, o)):
            w.send(DK, DKV.at[z, c], s_d4.at[e, i], r_d4.at[z, c], s, d.fid(zz, yh, cc))
    w.send(DK, DKV.at[z, c], s_d4.at[Z - 1, 0], r_d4.at[z, c], s, mate)
    for zz in zpeers:
        recv(QY.at[zz], r_e2.at[zz])
        QS[...] = QS[...] + QY[zz].astype(F32)
    for e, yy in enumerate(ysides):
        w.send(QS.at[yy], QZ.at[yh], s_e3.at[e], r_e3.at[yh], s, d.far(z, yy))
    T["kvload"].wait()
    recv(DKV.at[z, o], r_d4.at[z, o])
    for zz in zpeers:
        recv(DKV.at[zz, 0], r_d4.at[zz, 0])
        recv(DKV.at[zz, 1], r_d4.at[zz, 1])
    wide = jnp.concatenate([DKV[g, p] for g in range(Z) for p in range(2)], axis=1)
    out = QS[yh] + nn(wide, KVL[...])
    for yy in ysides:
        recv(QZ.at[yy], r_e3.at[yy])
        out = out + QZ[yy]
    pg_out[...] = out
    w.finish()


def per_device(hidden, q_weight, kv_weight, d_attended, doc_lengths, prompt_pos):
    vm = pl.BlockSpec(memory_space=pltpu.VMEM)
    hbm = pl.BlockSpec(memory_space=pltpu.HBM)
    return pl.pallas_call(
        whole,
        out_shape=(jax.ShapeDtypeStruct((ROWS, HD), BF16),
                   jax.ShapeDtypeStruct((PL, HD), F32)),
        in_specs=[hbm] * 7,
        out_specs=(vm, vm),
        scratch_shapes=[
            VMEM((ROWS, 4096), BF16),
            VMEM((256, 4096), BF16),
            VMEM((Z, 2, 2, 8, FB), BF16),
            VMEM((YH, Z, 8, FB), BF16),
            VMEM((X * YL, 8, 4096), BF16),
            VMEM((64, 4096), BF16),
            VMEM((2, 2, 16, ROWS), F32),
            VMEM((2, 16, ROWS), F32),
            VMEM((2, 16, ROWS), BF16),
            VMEM((2, HD, ROWS), F32),
            VMEM((HD, ROWS), F32),
            VMEM((2, 2, 2, 2, 16, SEQ), BF16),
            VMEM((HD // 2, ROWS), F32),
            VMEM((HD // 2, ROWS), F32),
            VMEM((ROWS, HD), BF16),
            VMEM((ROWS, SEQ), BF16),
            VMEM((SEQ, NP), BF16),
            VMEM((SEQ, FB), BF16),
            VMEM((2, PL, HD), BF16),
            VMEM((YL, X, PL, HD), F32),
            VMEM((2, YL, X, PL, HD), BF16),
            VMEM((X, C, YL, PL, HD), BF16),
            VMEM((YL, PL, HD), F32),
            VMEM((YH, YL, PL, HD), F32),
            VMEM((PL, HD), BF16),
            VMEM((Z, 2, PL, HD), BF16),
            VMEM((Z, YH, PL, HD), BF16),
            VMEM((Z, YH, PL, HD), BF16),
            VMEM((YH, PL, HD), F32),
            VMEM((YH, PL, HD), F32),
            VMEM((ROWS, FB), BF16),
            pltpu.SMEM((4,), jnp.int32),
            VMEM((1, NP), jnp.int32),
            VMEM((ROWS, SEQ), F32),
            DMA((124,)), DMA((2, 2, Z * YH)),
            DMA(()), DMA(()), DMA(()),
            DMA((Z - 1,)), DMA((Z,)), DMA((YH - 1,)), DMA((YH,)),
            DMA(()), DMA(()), DMA((6,)), DMA((X * YL,)),
            DMA(()), DMA(()),
            DMA((YH * YL - 1,)), DMA((YH, YL)),
            DMA((24,)), DMA((X, YH, YL)),
            DMA((X, YL)), DMA((X * YL,)),
            DMA(()), DMA(()), DMA(()), DMA((5,)),
            DMA(()), DMA(()),
            DMA((X, C)), DMA((X, C)),
            DMA((YH * YL - 1,)), DMA((YH, YL)),
            DMA((Z, 2)), DMA((Z, 2)),
            DMA((Z - 1,)), DMA((Z,)),
            DMA((YH - 1,)), DMA((YH,)),
        ],
        compiler_params=pltpu.CompilerParams(
            collective_id=0, has_side_effects=True, vmem_limit_bytes=48 << 20),
        name="whole",
    )(*(pltpu.with_memory_space_constraint(a, pltpu.HBM) for a in (
        hidden, q_weight, kv_weight.reshape(Z, 2, 2, 2, 32, FB), kv_weight, d_attended,
        doc_lengths, prompt_pos.reshape(1, NP))))


def solution(mesh):
    placed = (P("seq", "fsdp"), P("fsdp", None), P(None, "fsdp"), P("seq", "fsdp"), P(), P())
    return jax.shard_map(
        per_device,
        mesh=mesh,
        in_specs=placed,
        out_specs=(P("seq", "fsdp"), P("seq", "fsdp")),
        check_vma=False,
    )
```

```python
import functools
import math

import jax
import jax.numpy as jnp
from jax import lax
from jax.experimental import pallas as pl
from jax.experimental.pallas import tpu as pltpu
from jax.sharding import PartitionSpec as P

ROPE_THETA = 1000000.0
MESH = pl.DeviceIdType.MESH
F32 = jnp.float32
BF16 = jnp.bfloat16
VMEM = pltpu.VMEM
DMA = pltpu.SemaphoreType.DMA

X, YL, YH, Z, C = 4, 2, 4, 8, 2
ZROWS = 32
KINDS = "YZ" if ZROWS else "Y"
ROWS, HD, FB = 256, 128, 128


def nt(a, b):
    return lax.dot_general(a, b, (((1,), (1,)), ((), ())), preferred_element_type=F32)


class Place:
    def __init__(self):
        self.s = lax.axis_index("seq")
        self.f = lax.axis_index("fsdp")
        self.x = self.s % X
        self.yl = self.s // X
        self.z = self.f // (YH * C)
        self.yh = (self.f // C) % YH
        self.c = self.f % C
        self.o = 1 - self.c

    def hop(self, z, yh):
        return (self.c + z + self.z + yh + self.yh) % 2

    def far(self, z, yh):
        return self.fid(z, yh, self.hop(z, yh))

    def fid(self, z, yh, c):
        return (z * YH + yh) * C + c


class Wires:
    def __init__(self):
        self.open = []

    def make(self, src, dst, ss, rs, seq, fs):
        return pltpu.make_async_remote_copy(
            src_ref=src, dst_ref=dst, send_sem=ss, recv_sem=rs,
            device_id={"seq": seq, "fsdp": fs}, device_id_type=MESH)

    def send(self, *args):
        copy = self.make(*args)
        copy.start()
        self.open.append(copy)

    def finish(self):
        for copy in self.open:
            copy.wait_send()


def nn(a, b):
    return lax.dot_general(a, b, (((1,), (0,)), ((), ())), preferred_element_type=F32)


def tn(a, b):
    return lax.dot_general(a, b, (((0,), (0,)), ((), ())), preferred_element_type=F32)


LAZY = 1.5


class Flow:
    RATE = {"z+": 45.0, "z-": 45.0, "y+": 22.0, "y-": 22.0, "x+": 45.0, "x-": 45.0, "x2": 22.0, "m": 300.0, "n": 1e9}
    LAG = {"z+": 2.1, "z-": 2.1, "y+": 2.9, "y-": 2.9, "x+": 2.1, "x-": 2.1, "x2": 2.8, "m": 1.0, "n": 4.0}

    def __init__(self):
        self.tasks = {}
        self.recvs = {}

    def arrival(self, key, ref, sem):
        self.recvs[key] = (ref, sem)

    def task(self, name, needs=(), after=(), sends=(), work=None, cost=0.05, rank=0):
        self.tasks[name] = (set(needs), set(after), list(sends), work, cost, rank)

    def order(self):
        at, done, free, now, out = {}, {}, {}, 0.0, []
        todo = list(self.tasks)
        while todo:
            best = None
            for i, name in enumerate(todo):
                needs, after, sends, work, _, rank = self.tasks[name]
                if all(n in at for n in needs) and all(a in done for a in after):
                    ready = max([at[n] for n in needs] + [done[a] for a in after] + [0.0])
                    if needs and not sends and work is None:
                        ready += LAZY
                    cand = (max(ready, now), rank, i)
                    if best is None or cand < best:
                        best = cand
            assert best is not None, todo
            name = todo.pop(best[2])
            _, _, sends, _, cost, _ = self.tasks[name]
            now = best[0] + cost
            done[name] = now
            for link, size, key, _ in sends:
                start = max(free.get(link, 0.0), now)
                free[link] = start + size / self.RATE[link]
                if key is not None:
                    lag = self.LAG[link] if key[0] != "b" else 1.5 + 0.8 * min(key[1], 8 - key[1])
                    at[key] = max(at.get(key, 0.0), free[link] + lag)
            out.append(name)
        self.model = done
        return out

    def emit(self, recv):
        for name in self.order():
            needs, _, sends, work, _, _ = self.tasks[name]
            for key in sorted(needs, key=repr):
                recv(*self.recvs[key])
            if work is not None:
                work()
            for _, _, _, go in sends:
                go()


def lanes(k, n=128):
    return pl.ds(pl.multiple_of(k * n, n), n)


STEP = -2.0 * math.log(ROPE_THETA) / HD
SCALE = 1.0 / math.sqrt(HD)
SEQ, NP, PL = 2048, 128, 16


def openings(tokens, doc):
    end = jnp.int32(0)
    start = jnp.zeros_like(tokens)
    for i in range(4):
        end = end + doc[i]
        start = start + jnp.where(tokens >= end, doc[i], 0)
    return start


def whole(hid, qw, kvw, kvflat, dhbm, dochbm, phbm, att_out, pg_out,
          H, W2, KZ, KY, KW, KWF, KP, KR, KB, QP, QR, KVT, COS, SIN, QB, PB, CM, KVL,
          QG, GP, GB, GX, G2, GY, DK, DKV, QF, QY, QS, QZ, dat, doc, prow, BIAS,
          s_h, r_h, s_w, r_w, l_w, s_kz, r_kz, s_ky, r_ky, s_kl, r_kl, s_kx, r_kx,
          s_p, r_p, s_b, r_b, s_x, r_x, s_c, r_c, s_q, r_q, l_v, l_in,
          s_g, r_g, s_d2, r_d2, s_d3, r_d3, s_d4, r_d4, s_e2, r_e2, s_e3, r_e3):
    d = Place()
    s, f, x, yl, z, yh, c, o = d.s, d.f, d.x, d.yl, d.z, d.yh, d.c, d.o
    mate = d.fid(z, yh, o)
    zup, zdn = (z + 1) % Z, (z + Z - 1) % Z
    w = Wires()

    loads = [pltpu.make_async_copy(a, b, l_in.at[i]) for i, (a, b) in enumerate(
        ((dochbm, doc), (phbm, prow), (dhbm, dat)))]
    for load in loads:
        load.start()
    bar = pltpu.get_barrier_semaphore()
    peers = []
    ypeers = []
    for e in range(1, YH * YL):
        y = (yh * YL + yl + e) % (YH * YL)
        ypeers.append((y // YL, y % YL))
    xpeers = [(x + e) % X for e in range(1, X)]
    zpeers = [(z + e) % Z for e in range(1, Z)]
    for e in (4, 3, 5, 2, 6, 1, 7):
        for cc in (c, o):
            peers.append((s, d.fid((z + e) % Z, yh, cc)))
    for e in (4, 3, 5, 2, 6, 1, 7):
        y = (yh * YL + yl + e) % (YH * YL)
        peers.append(((y % YL) * X + x, d.fid(z, y // YL, c)))
        if e % 2:
            peers.append(((y % YL) * X + x, d.fid(z, y // YL, o)))
    for e in (2, 1, 3):
        for ff in (f, mate):
            peers.append((yl * X + (x + e) % X, ff))
    for e in (1, 3):
        peers.append((s, d.fid(z, (yh + e) % YH, o)))
    peers.append((s, mate))
    for ps, pf in peers:
        pl.semaphore_signal(bar, inc=1, device_id={"seq": ps, "fsdp": pf}, device_id_type=MESH)
    pl.semaphore_wait(bar, len(peers))

    def hblock(zz, yy):
        return H.at[:, lanes(zz * YH + yy)]

    def recv(ref, sem):
        w.make(ref, ref, s_q, sem, s, mate).wait_recv()

    def eighth(g):
        return kvw.at[g, :, s // 4, :, pl.ds(pl.multiple_of((s % 4) * 8, 8), 8), :]
    for e, zz in enumerate(zpeers):
        w.send(eighth(zz), KZ.at[z], s_kz.at[e], r_kz.at[z], s, d.far(zz, yh))
    kzown = pltpu.make_async_copy(eighth(z), KZ.at[z], l_in.at[3])
    kzown.start()
    hown = pltpu.make_async_copy(hid, hblock(z, yh), l_in.at[4])
    hown.start()
    flow = Flow()
    used = [0]
    ny = ROWS - ZROWS
    ROW = {"Y": {"A": (0, ny // 2), "B": (ny // 2, ny // 2)}, "Z": {"A": (ny, ZROWS // 2), "B": (ny + ZROWS // 2, ZROWS // 2)}}
    REACH = {"A": {"z+": 4, "z-": 3, "y+": 2, "y-": 1}, "B": {"z+": 3, "z-": 4, "y+": 1, "y-": 2}}
    STEPS = {"z+": (1, 0), "z-": (-1, 0), "y+": (0, 1), "y-": (0, -1)}

    def hpiece(kind, dz, dy, h):
        r0, n = ROW[kind][h]
        return H.at[pl.ds(r0, n), lanes((z + dz) % Z * YH + (yh + dy) % YH)]

    def hsem(kind, dz, dy, h):
        return r_h.at["YZ".index(kind), "AB".index(h), (z + dz) % Z * YH + (yh + dy) % YH]

    def hsend(kind, dz, dy, h, way):
        ez, ey = STEPS[way]
        r0, n = ROW[kind][h]
        slot = s_h.at[used[0]]
        used[0] += 1
        src = hid.at[pl.ds(r0, n), :] if (dz, dy) == (0, 0) else hpiece(kind, dz, dy, h)

        def go():
            w.send(src, hpiece(kind, dz, dy, h), slot, hsem(kind, dz, dy, h),
                   s, d.fid((z + ez) % Z, (yh + ey) % YH, o))
        return (way, n / 4, (kind, (dz - ez) % Z, (dy - ey) % YH, h), go)

    def onward(dist, size, h, up, down, first):
        if dist == 0:
            return [up, down] if first == up else [down, up]
        out = []
        back = size - dist
        if back < REACH[h][up] and dist > size // 2:
            out.append(up)
        if dist < REACH[h][down] and dist < size // 2:
            out.append(down)
        return out

    def hidden_tasks():
        for kind in KINDS:
            start = []
            for dz in range(Z):
                for dy in range(YH):
                    for h in "AB":
                        name = (kind, dz, dy, h)
                        needs = [name] if dz or dy else []
                        if needs:
                            flow.arrival(name, hpiece(*name), hsem(*name))
                        alongz = onward(dz, Z, h, "z+", "z-", "z+" if h == "A" else "z-")
                        alongy = onward(dy, YH, h, "y+", "y-", "y+" if h == "A" else "y-")
                        if kind == "Y":
                            ways = (alongy if dz == 0 else []) + alongz
                            if dz == 0 and dy == 0:
                                ways = [alongy[0], alongz[0], alongz[1], alongy[1]]
                        else:
                            ways = alongz if dy == 0 else alongy
                        if kind == "Z" and dy == 0:
                            after = [name] + ([("Y", 0, 1, "B"), ("Y", 0, 3, "A")] if dz else [])
                            flow.task(("Zy", dz, h), after=after, rank=1,
                                      sends=[hsend(kind, dz, dy, h, way) for way in alongy])
                        if dz or dy:
                            flow.task(name, needs=needs, sends=[hsend(kind, dz, dy, h, way) for way in ways])
                        else:
                            start += [(i, hsend(kind, dz, dy, h, way)) for i, way in enumerate(ways)]
            start.sort(key=lambda pair: (pair[0] + 1) // 2)
            flow.task((kind, 0, 0, "A"), sends=[send for _, send in start], rank=-1 if kind == "Z" else -2)
            flow.task((kind, 0, 0, "B"), after=[(kind, 0, 0, "A")], rank=-2)
    hidden_tasks()

    T = {}

    def setup():
        def wload(k, _):
            keep = d.hop(k // YH, k % YH)
            pltpu.make_async_copy(qw.at[:, lanes(k * 2 + keep)], W2.at[pl.ds(c * 128, 128), lanes(k)], l_w).start()
            w.make(qw.at[:, lanes(k * 2 + 1 - keep)], W2.at[pl.ds(c * 128, 128), lanes(k)], s_w, r_w, s, mate).start()
            return 0
        lax.fori_loop(0, Z * YH, wload, 0)
        kvload = pltpu.make_async_copy(kvflat, KVL, l_v)
        kvload.start()
        for load in loads:
            load.wait()

        tok = s * ROWS + lax.broadcasted_iota(jnp.int32, (1, ROWS), 1)
        place = (tok - openings(tok, doc)).astype(F32)
        freq = jnp.exp(lax.broadcasted_iota(jnp.int32, (HD // 2, 1), 0).astype(F32) * STEP)
        angle = freq * place
        COS[...] = jnp.cos(angle)
        SIN[...] = jnp.sin(angle)
        prompts = prow[...]
        for i in range(8):
            at = i * 256 + lax.broadcasted_iota(jnp.int32, (256, NP), 0)
            CM[pl.ds(i * 256, 256), :] = jnp.where(at == prompts, 1.0, 0.0).astype(BF16)
        def mask(i, _):
            t = s * ROWS + i * 32 + lax.broadcasted_iota(jnp.int32, (32, 1), 0)
            j = lax.broadcasted_iota(jnp.int32, (32, SEQ), 1)
            BIAS[pl.ds(pl.multiple_of(i * 32, 32), 32), :] = jnp.where(
                (j >= openings(t, doc)) & (j <= t), 0.0, -jnp.inf)
            return 0
        lax.fori_loop(0, ROWS // 32, mask, 0)
        near = lax.broadcasted_iota(jnp.int32, (PL, NP), 1) == (
            s * PL + lax.broadcasted_iota(jnp.int32, (PL, NP), 0))
        own_p = jnp.sum(jnp.where(near, prompts.astype(F32), 0.0), axis=1, keepdims=True).astype(jnp.int32)
        pick = jnp.where(lax.broadcasted_iota(jnp.int32, (PL, ROWS), 1) == own_p - s * ROWS,
                         1.0, 0.0).astype(BF16)
        lane = lax.broadcasted_iota(jnp.int32, (1, HD), 1)
        freq_l = jnp.exp(jnp.where(lane < 64, lane, lane - 64).astype(F32) * STEP)
        angle_p = (own_p - openings(own_p, doc)).astype(F32) * freq_l
        cos_p = jnp.cos(angle_p)
        sin_p = jnp.where(lane < 64, 1.0, -1.0) * jnp.sin(angle_p)
        T.update(kvload=kvload, pick=pick, cos_p=cos_p, sin_p=sin_p)

    def back(u):
        return u * T["cos_p"] + pltpu.roll(u, 64, 1) * T["sin_p"]

    flow.task("setup", after=[("Y", 0, 0, "A"), ("Y", 0, 0, "B")], work=setup, cost=1.0, rank=-1)

    def gain(zz):
        cols = pl.ds(pl.multiple_of(zz * 512, 512), 512)
        part = nt(W2[:, cols], H[:, cols])
        QP[0] = QP[0] + part[:128]
        QP[1] = QP[1] + part[128:]

    def gain_kv(zz):
        cols = pl.ds(pl.multiple_of(zz * 512, 512), 512)
        part = nt(KWF[:, cols], H[:, cols]).reshape(2, 2, 16, ROWS)
        KP[0] = KP[0] + part[:, 0]
        KP[1] = KP[1] + part[:, 1]

    kz_keys = [("kz", i) for i in range(Z - 1)]
    for key, zz in zip(kz_keys, zpeers):
        flow.arrival(key, KZ.at[zz], r_kz.at[zz])
    ysides = [(yh + e) % YH for e in range(1, YH)]

    def ky_go(e, yy):
        return lambda: w.send(KZ.at[:, yy // 2, yy % 2], KY.at[yh], s_ky.at[e], r_ky.at[yh], s, d.far(z, yy))

    def kz_work():
        kzown.wait()
        KY[yh] = KZ[:, yh // 2, yh % 2]
    flow.task("kz0", sends=[("n", 8, key, lambda: None) for key in kz_keys], rank=-3)
    flow.task("kz", needs=kz_keys, work=kz_work,
              sends=[(("y+", "y-", "y+")[e], 16, ("ky", e), ky_go(e, yy)) for e, yy in enumerate(ysides)])
    for e, yy in enumerate(ysides):
        flow.arrival(("ky", e), KY.at[yy], r_ky.at[yy])
    sx = (1 - yl) * X + x
    kx_row = lambda dx, ep: (yl + ep) % YL * X + (x + dx) % X

    def ky_work():
        for zz in range(Z):
            for yy in range(YH):
                KW[s, :, pl.ds((zz * YH + yy) * 128, 128)] = KY[yy, zz]

    def kx_send(dx, ep, way):
        ex = 1 if way == "x+" else -1
        row = kx_row(dx, ep)
        slot = s_kx.at[used[1]]
        used[1] += 1
        return (way, 64, ("kx", (dx - ex) % X, ep), lambda: w.send(
            KW.at[row], KW.at[row], slot, r_kx.at[row], yl * X + (x + ex) % X, f))
    used.append(0)
    flow.task("ky", needs=[("ky", e) for e in range(YH - 1)], work=ky_work, cost=0.2,
              sends=[("y+", 64, ("kl",), lambda: w.send(KW.at[s], KW.at[s], s_kl, r_kl, sx, f)),
                     kx_send(0, 0, "x+"), kx_send(0, 0, "x-")])
    flow.arrival(("kl",), KW.at[sx], r_kl)
    flow.task("kl", needs=[("kl",)], sends=[kx_send(0, 1, "x+"), kx_send(0, 1, "x-")])
    for ep in range(YL):
        for dx in range(1, X):
            flow.arrival(("kx", dx, ep), KW.at[kx_row(dx, ep)], r_kx.at[kx_row(dx, ep)])
            sends = []
            if dx == 3 and ep == 0:
                sends = [kx_send(dx, ep, "x+")]
            if dx == 1 and ep == 1:
                sends = [kx_send(dx, ep, "x-")]
            flow.task(("kx", dx, ep), needs=[("kx", dx, ep)], sends=sends)

    def kwf_work():
        for i in range(X * YL):
            KWF[pl.ds(i * 8, 8), :] = KW[i]
    flow.task("kwf", after=["ky", "kl"] + [("kx", dx, ep) for dx in range(1, X) for ep in range(YL)],
              work=kwf_work, cost=0.2, rank=1)

    def wq_work():
        mine_w, other_w = W2.at[pl.ds(c * 128, 128)], W2.at[pl.ds(o * 128, 128)]
        pltpu.make_async_copy(mine_w, mine_w, l_w).wait()
        recv(other_w, r_w)
        w.make(other_w, other_w, s_w, r_w, s, mate).wait_send()
        hown.wait()
        QP[...] = jnp.zeros_like(QP)
        KP[...] = jnp.zeros_like(KP)
    flow.task("wq0", sends=[("n", 8, ("wq",), lambda: None)], rank=-3)
    flow.task("wq", after=["wq0", ("Y", 0, 2, "A")], work=wq_work, cost=0.3, rank=1)
    for dz in range(Z):
        chunk_of = [(kind, dz, dy, h) for kind in KINDS for dy in range(YH) for h in "AB"]
        flow.task(("gkv", dz), after=chunk_of + ["wq", "kwf"], cost=0.15, rank=1,
                  work=functools.partial(lambda i: gain_kv((z + i) % Z), dz))
        flow.task(("gq", dz), after=chunk_of + ["wq"], cost=0.32, rank=2,
                  work=functools.partial(lambda i: gain((z + i) % Z), dz))
    flow.task("kvx", after=[("gkv", dz) for dz in range(Z)], rank=1,
              sends=[("m", 32, ("kr",), lambda: w.send(KP.at[o], KR, s_p, r_p, s, mate))])
    flow.task("qx", after=[("gq", dz) for dz in range(Z)], rank=1,
              sends=[("m", 128, ("qr",), lambda: w.send(QP.at[o], QR, s_q, r_q, s, mate))])

    def kblock(e, dx):
        yy, ll = yrel[e]
        return KVT.at[yy // 2, :, yy % 2, (c + e + dx) % 2, :, lanes(ll * X + (x + dx) % X, ROWS)]

    def kr_work():
        total = KP[c] + KR[...]
        kvb = total.astype(BF16)
        kf = kvb.astype(F32)
        b16 = pl.ds(pl.multiple_of((yh % 2) * 32 + c * 16, 16), 16)
        ck, sk = COS[b16, :], SIN[b16, :]
        iskey = yh < 2
        KB[0] = jnp.where(iskey, kf[0] * ck - kf[1] * sk, kf[0]).astype(BF16)
        KB[1] = jnp.where(iskey, kf[1] * ck + kf[0] * sk, kf[1]).astype(BF16)
        KVT[yh // 2, :, yh % 2, c, :, lanes(s, ROWS)] = KB[...]

    yrel = [(yh, yl)] + ypeers
    LATE = (4,)
    used.append(0)

    def x_send(dx, e, way):
        ex = {"x+": 1, "x-": -1, "x2": 2}[way]
        yy, ll = yrel[e]
        block = kblock(e, dx)
        src = KB if (dx, e) == (0, 0) else block
        slot = s_x.at[used[2]]
        used[2] += 1
        return (way, 16, ("x", (dx - ex) % X, e), lambda: w.send(
            src, block, slot, r_x.at[(x + dx) % X, yy, ll], yl * X + (x + ex) % X,
            f if ex == 2 else mate))

    def b_send(e):
        yy, ll = ypeers[e]
        return ("y+" if e < 4 else "y-", 16 * min(e + 1, 7 - e) / 4, ("b", 7 - e), lambda: w.send(
            KB, kblock(0, 0), s_b.at[e], r_b.at[yh, yl], ll * X + x, d.fid(z, yy, (c + e + 1) % 2)))

    flow.arrival(("kr",), KR, r_p)
    flow.task("kr", needs=[("kr",)], work=kr_work, cost=0.2,
              sends=[b_send(e) for e in (0, 6, 1, 5, 2, 4, 3)] + [x_send(0, 0, "x+"), x_send(0, 0, "x-")])
    for e in range(1, YH * YL):
        yy, ll = yrel[e]
        flow.arrival(("b", e), kblock(e, 0), r_b.at[yy, ll])
        flow.task(("b", e), needs=[("b", e)], sends=([x_send(0, e, "x2")] if e in LATE else []) + [
            x_send(0, e, "x+"), x_send(0, e, "x-")])
    for e in range(YH * YL):
        yy, ll = yrel[e]
        for dx in range(1, X):
            xx = (x + dx) % X
            flow.arrival(("x", dx, e), kblock(e, dx), r_x.at[xx, yy, ll])
            sends = []
            if dx == 3 and e % 2 == 0 and e not in LATE:
                sends = [x_send(dx, e, "x+")]
            if dx == 1 and e % 2 == 1 and e not in LATE:
                sends = [x_send(dx, e, "x-")]
            flow.task(("x", dx, e), needs=[("x", dx, e)], sends=sends)

    def c_send(dx, ep):
        col = (yl + ep) % YL * X + (x + dx) % X
        part = KVT.at[:, :, :, (c + ep + dx) % 2, :, lanes(col, ROWS)]
        other = KVT.at[:, :, :, (o + ep + dx) % 2, :, lanes(col, ROWS)]
        flow.arrival(("c", dx, ep), other, r_c.at[col])
        return ("m", 64, ("c", dx, ep), lambda: w.send(part, part, s_c.at[dx, ep], r_c.at[col], s, mate))
    for dx in range(X):
        for ep in range(YL):
            if dx:
                after = [("x", dx, e) for e in range(ep, 8, 2)]
            else:
                after = [("b", e) if e else "kr" for e in range(ep, 8, 2)]
            flow.task(("cs", dx, ep), after=after, sends=[c_send(dx, ep)])
            flow.task(("c", dx, ep), needs=[("c", dx, ep)], after=[("cs", i, j) for i in range(X) for j in range(YL)])

    def q_work():
        q = QP[c] + QR[...]
        q1, q2 = q[:64], q[64:]
        co, si = COS[...], SIN[...]
        qt = jnp.concatenate([q1 * co - q2 * si, q2 * co + q1 * si], axis=0)
        QB[...] = jnp.transpose(qt).astype(BF16)
    flow.arrival(("qr",), QR, r_q)
    flow.task("q", needs=[("qr",)], work=q_work, cost=0.3, rank=1)
    flow.emit(recv)

    pick = T["pick"]
    kt = KVT[0].reshape(HD, SEQ)
    vt = KVT[1].reshape(HD, SEQ)
    CH = 64

    for i in range(ROWS // CH):
        rows = pl.ds(i * CH, CH)
        raw = nn(QB[rows, :], kt) * (SCALE * math.log2(math.e)) + BIAS[rows, :]
        e = jnp.exp2(raw - jnp.max(raw, axis=1, keepdims=True))
        probs = (e * (1.0 / jnp.sum(e, axis=1, keepdims=True))).astype(BF16)
        PB[rows, :] = probs
        att_out[rows, :] = nt(probs, vt).astype(BF16)

    att = att_out[...]
    da = dat[...]
    rowdot = jnp.sum(da.astype(F32) * att.astype(F32), axis=1, keepdims=True)
    colp = nn(PB[...], CM[...])
    cv = nn(vt, CM[...]).astype(BF16)
    cds = (colp * (nn(da, cv) - rowdot)).astype(BF16)
    kg = tn(cds, QB[...]).reshape(YL, X, PL, HD)
    vg = tn(colp.astype(BF16), da).reshape(YL, X, PL, HD)
    GB[0] = kg.astype(BF16)
    GB[1] = vg.astype(BF16)
    GP[...] = jnp.where(c == 0, kg, vg)
    for e in (2, 1, 3, 0):
        xx = (x + e) % X
        for i, (pp, ff) in enumerate(((c, f), (o, mate))):
            if e or i:
                w.send(GB.at[pp, :, xx], GX.at[x, c], s_d2.at[e, i], r_d2.at[x, c], yl * X + xx, ff)
    row_up = nn(pick, da)
    row_dot = jnp.sum(row_up * nn(pick, att), axis=1, keepdims=True)
    row_dp = nn(row_up.astype(BF16), vt)
    row_ds = (nn(pick, PB[...]) * (row_dp - row_dot)).astype(BF16)
    QG[c] = back(nt(row_ds, kt) * SCALE).astype(BF16)
    w.send(QG.at[c], QG.at[c], s_g, r_g, s, mate)

    recv(QG.at[o], r_g)
    both = jnp.concatenate([QG[0], QG[1]], axis=1)

    for e in (4, 3, 5, 2, 6, 1, 7, 0):
        zz = (z + e) % Z
        part = nn(both, W2[:, pl.ds(pl.multiple_of(zz * 512, 512), 512)])
        for yy in range(YH):
            piece = part[:, yy * 128:(yy + 1) * 128]
            if e:
                QF[zz, yy] = piece.astype(BF16)
            else:
                QS[yy] = piece
        if e:
            w.send(QF.at[zz], QY.at[z], s_e2.at[e - 1], r_e2.at[z], s, d.far(zz, yh))

    recv(GX.at[x, o], r_d2.at[x, o])
    acc = GP[:, x] + GX[x, o].astype(F32)
    for xx in xpeers:
        for cc in range(C):
            recv(GX.at[xx, cc], r_d2.at[xx, cc])
            acc = acc + GX[xx, cc].astype(F32)
    G2[...] = acc
    for e in (3, 2, 4, 1, 5, 0, 6):
        yy, ll = ypeers[e]
        w.send(G2.at[ll], GY.at[yh, yl], s_d3.at[e], r_d3.at[yh, yl], ll * X + x, d.fid(z, yy, c))
    acc = G2[yl]
    for yy, ll in ypeers:
        recv(GY.at[yy, ll], r_d3.at[yy, ll])
        acc = acc + GY[yy, ll]
    dkv = jnp.where(c == 0, back(acc * SCALE), acc).astype(BF16)
    DK[...] = dkv
    DKV[z, c] = dkv
    for e in (3, 2, 4, 1, 5, 0, 6):
        zz = zpeers[e]
        for i, cc in enumerate((c, o)):
            w.send(DK, DKV.at[z, c], s_d4.at[e, i], r_d4.at[z, c], s, d.fid(zz, yh, cc))
    w.send(DK, DKV.at[z, c], s_d4.at[Z - 1, 0], r_d4.at[z, c], s, mate)
    for zz in zpeers:
        recv(QY.at[zz], r_e2.at[zz])
        QS[...] = QS[...] + QY[zz].astype(F32)
    for e, yy in enumerate(ysides):
        w.send(QS.at[yy], QZ.at[yh], s_e3.at[e], r_e3.at[yh], s, d.far(z, yy))
    T["kvload"].wait()
    recv(DKV.at[z, o], r_d4.at[z, o])
    for zz in zpeers:
        recv(DKV.at[zz, 0], r_d4.at[zz, 0])
        recv(DKV.at[zz, 1], r_d4.at[zz, 1])
    wide = jnp.concatenate([DKV[g, p] for g in range(Z) for p in range(2)], axis=1)
    out = QS[yh] + nn(wide, KVL[...])
    for yy in ysides:
        recv(QZ.at[yy], r_e3.at[yy])
        out = out + QZ[yy]
    pg_out[...] = out
    w.finish()


def per_device(hidden, q_weight, kv_weight, d_attended, doc_lengths, prompt_pos):
    vm = pl.BlockSpec(memory_space=pltpu.VMEM)
    hbm = pl.BlockSpec(memory_space=pltpu.HBM)
    return pl.pallas_call(
        whole,
        out_shape=(jax.ShapeDtypeStruct((ROWS, HD), BF16),
                   jax.ShapeDtypeStruct((PL, HD), F32)),
        in_specs=[hbm] * 7,
        out_specs=(vm, vm),
        scratch_shapes=[
            VMEM((ROWS, 4096), BF16),
            VMEM((256, 4096), BF16),
            VMEM((Z, 2, 2, 8, FB), BF16),
            VMEM((YH, Z, 8, FB), BF16),
            VMEM((X * YL, 8, 4096), BF16),
            VMEM((64, 4096), BF16),
            VMEM((2, 2, 16, ROWS), F32),
            VMEM((2, 16, ROWS), F32),
            VMEM((2, 16, ROWS), BF16),
            VMEM((2, HD, ROWS), F32),
            VMEM((HD, ROWS), F32),
            VMEM((2, 2, 2, 2, 16, SEQ), BF16),
            VMEM((HD // 2, ROWS), F32),
            VMEM((HD // 2, ROWS), F32),
            VMEM((ROWS, HD), BF16),
            VMEM((ROWS, SEQ), BF16),
            VMEM((SEQ, NP), BF16),
            VMEM((SEQ, FB), BF16),
            VMEM((2, PL, HD), BF16),
            VMEM((YL, X, PL, HD), F32),
            VMEM((2, YL, X, PL, HD), BF16),
            VMEM((X, C, YL, PL, HD), BF16),
            VMEM((YL, PL, HD), F32),
            VMEM((YH, YL, PL, HD), F32),
            VMEM((PL, HD), BF16),
            VMEM((Z, 2, PL, HD), BF16),
            VMEM((Z, YH, PL, HD), BF16),
            VMEM((Z, YH, PL, HD), BF16),
            VMEM((YH, PL, HD), F32),
            VMEM((YH, PL, HD), F32),
            VMEM((ROWS, FB), BF16),
            pltpu.SMEM((4,), jnp.int32),
            VMEM((1, NP), jnp.int32),
            VMEM((ROWS, SEQ), F32),
            DMA((124,)), DMA((2, 2, Z * YH)),
            DMA(()), DMA(()), DMA(()),
            DMA((Z - 1,)), DMA((Z,)), DMA((YH - 1,)), DMA((YH,)),
            DMA(()), DMA(()), DMA((6,)), DMA((X * YL,)),
            DMA(()), DMA(()),
            DMA((YH * YL - 1,)), DMA((YH, YL)),
            DMA((24,)), DMA((X, YH, YL)),
            DMA((X, YL)), DMA((X * YL,)),
            DMA(()), DMA(()), DMA(()), DMA((5,)),
            DMA(()), DMA(()),
            DMA((X, C)), DMA((X, C)),
            DMA((YH * YL - 1,)), DMA((YH, YL)),
            DMA((Z, 2)), DMA((Z, 2)),
            DMA((Z - 1,)), DMA((Z,)),
            DMA((YH - 1,)), DMA((YH,)),
        ],
        compiler_params=pltpu.CompilerParams(
            collective_id=0, has_side_effects=True, vmem_limit_bytes=48 << 20),
        name="whole",
    )(*(pltpu.with_memory_space_constraint(a, pltpu.HBM) for a in (
        hidden, q_weight, kv_weight.reshape(Z, 2, 2, 2, 32, FB), kv_weight, d_attended,
        doc_lengths, prompt_pos.reshape(1, NP))))


def solution(mesh):
    placed = (P("seq", "fsdp"), P("fsdp", None), P(None, "fsdp"), P("seq", "fsdp"), P(), P())
    return jax.shard_map(
        per_device,
        mesh=mesh,
        in_specs=placed,
        out_specs=(P("seq", "fsdp"), P("seq", "fsdp")),
        check_vma=False,
    )
```
